32 devices in a mesh: fsdp: 16 (over z, y, core), rep: 2 (over x).
Axes of the slice: x: 2, y: 2, z: 4, core: 2. Of those that a mesh axis runs over, the one named last changes fastest.
Arguments:
- tokens: bfloat16 [32768, 768], P(('fsdp', 'rep')), may hold values from -6 to 6
- segment: int32 [32, 4], P(('fsdp', 'rep')), may hold values from 0 to 3, as said below
- live: int32 [32, 4], P(('fsdp', 'rep')), may hold values from 0 to 1, as said below
- cotangent: bfloat16 [32768, 768], P(('fsdp', 'rep')), may hold values from -6 to 6
- ln1_gain: bfloat16 [2, 768], P(None, 'fsdp'), may hold values from 0.5 to 1.5
- ln1_bias: bfloat16 [2, 768], P(None, 'fsdp'), may hold values from -1.25 to 1.25
- q_weight: bfloat16 [2, 768, 768], P(None, 'fsdp'), may hold values from -0.21875 to 0.21875
- q_bias: bfloat16 [2, 768], P(None, 'fsdp'), may hold values from -1.25 to 1.25
- k_weight: bfloat16 [2, 768, 768], P(None, 'fsdp'), may hold values from -0.21875 to 0.21875
- v_weight: bfloat16 [2, 768, 768], P(None, 'fsdp'), may hold values from -0.21875 to 0.21875
- v_bias: bfloat16 [2, 768], P(None, 'fsdp'), may hold values from -1.25 to 1.25
- o_weight: bfloat16 [2, 768, 768], P(None, 'fsdp'), may hold values from -1.75 to 1.75
- o_bias: bfloat16 [2, 768], P(None, 'fsdp'), may hold values from -1.25 to 1.25
- ln2_gain: bfloat16 [2, 768], P(None, 'fsdp'), may hold values from 0.5 to 1.5
- ln2_bias: bfloat16 [2, 768], P(None, 'fsdp'), may hold values from -1.25 to 1.25
- up_weight: bfloat16 [2, 768, 3072], P(None, 'fsdp'), may hold values from -0.21875 to 0.21875
- up_bias: bfloat16 [2, 3072], P(None, 'fsdp'), may hold values from -1.25 to 1.25
- down_weight: bfloat16 [2, 3072, 768], P(None, 'fsdp'), may hold values from -0.109375 to 0.109375
- down_bias: bfloat16 [2, 768], P(None, 'fsdp'), may hold values from -1.25 to 1.25
Outputs:
- block_out: bfloat16 [32768, 768], P(('fsdp', 'rep'))
- input_grad: float32 [32768, 768], P(('fsdp', 'rep'))
- grad_ln1_gain: float32 [2, 768], P(None, 'fsdp')
- grad_ln1_bias: float32 [2, 768], P(None, 'fsdp')
- grad_q_weight: float32 [2, 768, 768], P(None, 'fsdp')
- grad_q_bias: float32 [2, 768], P(None, 'fsdp')
- grad_k_weight: float32 [2, 768, 768], P(None, 'fsdp')
- grad_v_weight: float32 [2, 768, 768], P(None, 'fsdp')
- grad_v_bias: float32 [2, 768], P(None, 'fsdp')
- grad_o_weight: float32 [2, 768, 768], P(None, 'fsdp')
- grad_o_bias: float32 [2, 768], P(None, 'fsdp')
- grad_ln2_gain: float32 [2, 768], P(None, 'fsdp')
- grad_ln2_bias: float32 [2, 768], P(None, 'fsdp')
- grad_up_weight: float32 [2, 768, 3072], P(None, 'fsdp')
- grad_up_bias: float32 [2, 3072], P(None, 'fsdp')
- grad_down_weight: float32 [2, 3072, 768], P(None, 'fsdp')
- grad_down_bias: float32 [2, 768], P(None, 'fsdp')
The draws below stay inside these ranges and needn't reach their ends.
Inputs may be any that keep to these rules, and one draw needn't show every extreme that they name: `segment`: in each buffer either every slot has 0 (one image of 1024 tokens) or each slot has its own index (one image of 256 tokens a slot); exactly 12 buffers hold one image of 1024 tokens. Every slot of a buffer of one image is live, and the first slot of every buffer is live.
All inputs are finite; a program needn't handle non-finite values.
Results may differ from the reference program's by a relative error of at most 0.015.
Values may be sent and summed in bfloat16 or wider, within the bound.
A program may use at most 448 MiB of HBM per device.

```python
import jax
import jax.numpy as jnp
from jax import lax

D = 768
FF = 3072
HEADS = 16
LAYERS = 2
SLOT_LEN = 256
SLOTS = 4
SEQ = 1024
BUFFERS = 32
TOKENS = 32768


def buffer_layout(key):
    ranking = jax.random.permutation(jax.random.fold_in(key, 11), BUFFERS)
    long_cut = 2 * BUFFERS // 5
    is_long = ranking < long_cut
    slot_index = jnp.arange(SLOTS, dtype=jnp.int32)
    segment_ids = jnp.where(is_long[:, None], 0, slot_index[None, :]).astype(jnp.int32)
    coin_flip = jax.random.randint(jax.random.fold_in(key, 23), (BUFFERS, SLOTS), 0, 4)
    short_live = (coin_flip != 0) | (slot_index[None, :] == 0)
    first_short = ranking == long_cut
    forced_empty = first_short[:, None] & (slot_index[None, :] == SLOTS - 1)
    live_slots = jnp.where(is_long[:, None], 1, jnp.where(short_live & ~forced_empty, 1, 0))
    return (segment_ids, live_slots.astype(jnp.int32))


def draw_segment(key, part):
    return buffer_layout(key)[0]


def draw_live(key, part):
    return buffer_layout(key)[1]


def raised(entries, own_key, source, target, parts, factor):
    owner, partner = [(jnp.arange(entries.shape[dim]) // (entries.shape[dim] // parts)).reshape([-1 if axis == dim else 1 for axis in range(entries.ndim)]) for dim in (source, target)]
    chosen = jax.random.permutation(own_key, parts)[partner]
    strong = (owner == chosen) | (owner == (partner + parts // 2) % parts)
    return jnp.where(strong, factor * entries, entries)


def steps_of(rng, dims, split, least, top_value):
    loudness = 1.0
    for axis_at, blocks in split:
        heights = jax.random.uniform(jax.random.fold_in(jax.random.fold_in(rng, 6), axis_at), (blocks,), jnp.float32, least / len(split), top_value / len(split))
        loudness = loudness * jnp.repeat(jnp.exp(heights), dims[axis_at] // blocks).reshape((-1,) + (1,) * (len(dims) - 1 - axis_at))
    return loudness


def centred(stream_key, shape, scale, reach, split=(), kind=jnp.bfloat16):
    loudness = steps_of(stream_key, shape, split, -0.22, 0.18) if split else 1.0
    entries = jax.random.normal(stream_key, shape, jnp.float32) * scale * loudness
    return jnp.minimum(jnp.maximum(entries, -reach), reach).astype(kind)


def noise_with(stream_key, shape, scale, limit, split, heavy, kind=jnp.bfloat16):
    result = scale * jax.random.normal(stream_key, shape, jnp.float32)
    if split:
        result = result * steps_of(stream_key, shape, split, -0.22, 0.18)
    return jnp.clip(raised(result, jax.random.fold_in(stream_key, 3), *heavy), -limit, limit).astype(kind)


def setup_inputs(seed: int = 0) -> dict:
    key_list = jax.random.split(jax.random.key(seed), 20)
    return {
        "tokens": centred(key_list[0], (TOKENS, D), 1.0, 6.0, ((0, 32),)),
        "segment": draw_segment(jax.random.fold_in(key_list[19], 71), 0),
        "live": draw_live(jax.random.fold_in(key_list[19], 71), 0),
        "cotangent": noise_with(key_list[3], (TOKENS, D), 1.0, 6.0, ((0, 32),), (0, 1, 32, 2.75)),
        "ln1_gain": jnp.clip(1.0 + 0.1 * jax.random.normal(key_list[4], (LAYERS, D), jnp.float32), 0.5, 1.5).astype(jnp.bfloat16),
        "ln1_bias": centred(key_list[5], (LAYERS, D), 0.2, 1.25, ((1, 16),)),
        "q_weight": centred(key_list[6], (LAYERS, D, D), D ** -0.5, 0.21875, ((1, 16),)),
        "q_bias": centred(key_list[7], (LAYERS, D), 0.2, 1.25, ((1, 16),)),
        "k_weight": centred(key_list[8], (LAYERS, D, D), D ** -0.5, 0.21875, ((1, 16),)),
        "v_weight": centred(key_list[9], (LAYERS, D, D), D ** -0.5, 0.21875, ((1, 16),)),
        "v_bias": centred(key_list[10], (LAYERS, D), 0.2, 1.25, ((1, 16),)),
        "o_weight": centred(key_list[11], (LAYERS, D, D), (D // 64) ** -0.5, 1.75, ((1, 16),)),
        "o_bias": centred(key_list[12], (LAYERS, D), 0.2, 1.25, ((1, 16),)),
        "ln2_gain": jnp.clip(1.0 + 0.1 * jax.random.normal(key_list[13], (LAYERS, D), jnp.float32), 0.5, 1.5).astype(jnp.bfloat16),
        "ln2_bias": centred(key_list[14], (LAYERS, D), 0.2, 1.25, ((1, 16),)),
        "up_weight": centred(key_list[15], (LAYERS, D, FF), D ** -0.5, 0.21875, ((1, 16),)),
        "up_bias": centred(key_list[16], (LAYERS, FF), 0.2, 1.25, ((1, 16),)),
        "down_weight": centred(key_list[17], (LAYERS, FF, D), FF ** -0.5, 0.109375, ((1, 16),)),
        "down_bias": centred(key_list[18], (LAYERS, D), 0.2, 1.25, ((1, 16),)),
    }


EPSILON = 1e-06
HIGHEST = lax.Precision.HIGHEST

@jax.custom_vjp
def low(v):
    return lax.optimization_barrier(v.astype(jnp.bfloat16)).astype(jnp.float32)

@jax.custom_vjp
def low_back(v):
    return v

def low_keep(v):
    return (low(v), None)

def low_pass(kept, grad):
    return (grad,)

def back_keep(v):
    return (v, None)

def back_low(kept, grad):
    return (low(grad),)
low.defvjp(low_keep, low_pass)
low_back.defvjp(back_keep, back_low)

def norm_apply(source, gain_vec, offset):
    mean_val = lax.optimization_barrier(jnp.mean(source, axis=-1, keepdims=True))
    centered = source - mean_val
    variance = lax.optimization_barrier(jnp.mean(centered * centered, axis=-1, keepdims=True))
    return centered * lax.rsqrt(variance + EPSILON) * gain_vec + offset

def project(source, matrix):
    return jnp.dot(source, matrix, precision=HIGHEST)

def block_apply(hidden, weights, same_image):
    ln1_gain, ln1_bias, q_weight, q_bias, k_weight, v_weight, v_bias, o_weight, o_bias, ln2_gain, ln2_bias, up_weight, up_bias, down_weight, down_bias = weights
    length = hidden.shape[0]
    head_dim = D // HEADS
    normed = low(norm_apply(hidden, ln1_gain, ln1_bias))
    queries = low_back(low(project(normed, q_weight) + q_bias))
    key_rows = low_back(low(project(normed, k_weight)))
    value_rows = low_back(low(project(normed, v_weight) + v_bias))
    query_heads = queries.reshape(length, HEADS, head_dim)
    key_heads = key_rows.reshape(length, HEADS, head_dim)
    value_heads = value_rows.reshape(length, HEADS, head_dim)
    scores = jnp.einsum('qhd,khd->hqk', query_heads, key_heads, precision=HIGHEST) * head_dim ** (-0.5)
    scores = low_back(jnp.where(same_image[None], scores, -1e+30))
    attn_probs = low(jax.nn.softmax(scores, axis=-1))
    mixture = jnp.einsum('hqk,khd->qhd', attn_probs, value_heads, precision=HIGHEST).reshape(length, D)
    mixture = low_back(low(mixture))
    midway = hidden + low_back(project(mixture, o_weight) + o_bias)
    normed_mid = low(norm_apply(midway, ln2_gain, ln2_bias))
    upper_pre = low_back(project(normed_mid, up_weight) + up_bias)
    active = low(jax.nn.gelu(upper_pre, approximate=True))
    return midway + low_back(project(active, down_weight) + down_bias)

def reference(tokens, segment, live, cotangent, ln1_gain, ln1_bias, q_weight, q_bias, k_weight, v_weight, v_bias, o_weight, o_bias, ln2_gain, ln2_bias, up_weight, up_bias, down_weight, down_bias):
    parameters = tuple((item.astype(jnp.float32) for item in (ln1_gain, ln1_bias, q_weight, q_bias, k_weight, v_weight, v_bias, o_weight, o_bias, ln2_gain, ln2_bias, up_weight, up_bias, down_weight, down_bias)))
    seg_tok = jnp.repeat(segment, SLOT_LEN, axis=1).astype(jnp.int32)
    live_tok = jnp.repeat(live, SLOT_LEN, axis=1).astype(jnp.float32)
    inputs = tokens.astype(jnp.float32).reshape(BUFFERS, SEQ, D)

    def forward(source_all, weight_all):

        def one_buffer(pair):
            source, segment_row = pair
            same_image = segment_row[:, None] == segment_row[None, :]
            hidden = source
            for layer_index in range(LAYERS):
                hidden = block_apply(hidden, tuple((item[layer_index] for item in weight_all)), same_image)
            return hidden
        return lax.map(jax.checkpoint(one_buffer), (source_all, seg_tok))
    outputs, backward = jax.vjp(forward, inputs, parameters)
    masked = cotangent.astype(jnp.float32).reshape(BUFFERS, SEQ, D) * live_tok[:, :, None]
    grad_inputs, grad_params = backward(masked)
    return (outputs.reshape(TOKENS, D).astype(jnp.bfloat16), grad_inputs.reshape(TOKENS, D)) + tuple(grad_params)
```

```python
import functools
import math

import jax
import jax.numpy as jnp
from jax import lax
from jax.experimental import pallas as pl
from jax.experimental.pallas import tpu as pltpu
from jax.sharding import PartitionSpec as P

HEADS = 16
PIECES = 16
EXTRA = 16
EPSILON = 1e-06
BIG = 1e30
bf16 = jnp.bfloat16
f32 = jnp.float32
FORWARD_PARTS = 1
BACKWARD_PARTS = 4
UNROLL = 2
ATTN_PLAN = {0: [(0, 0)], 1: [(1, 0)], 2: [(0, 1)], 5: [(1, 1), (0, 2)], 7: [(1, 2), (0, 3)]}
ATTN_MIDDLE = []
ATTN_TILES = {0: [(1, 3), (0, 4)], 3: [(1, 4), (0, 5)]}
ATTN_END = [(1, 5)]
VMEM_BYTES = 60 * 1024 * 1024


def mm(a, b):
    return jnp.dot(a, b, preferred_element_type=f32)


def mm_tn(a, b):
    return lax.dot_general(a, b, (((0,), (0,)), ((), ())), preferred_element_type=f32)


def mm_nt(a, b):
    return lax.dot_general(a, b, (((1,), (1,)), ((), ())), preferred_element_type=f32)


def normalised(x):
    mean = jnp.mean(x, axis=-1, keepdims=True)
    centred = x - mean
    var = jnp.mean(centred * centred, axis=-1, keepdims=True)
    r = lax.rsqrt(var + EPSILON)
    return centred * r, r


def norm_back(d, xh, r, gain):
    e = d * gain
    m1 = jnp.mean(e, axis=-1, keepdims=True)
    m2 = jnp.mean(e * xh, axis=-1, keepdims=True)
    return r * (e - m1 - xh * m2)


def split3(x):
    hi = x.astype(bf16)
    rest = x - hi.astype(f32)
    mid = rest.astype(bf16)
    low = (rest - mid.astype(f32)).astype(bf16)
    return hi, mid, low


def joined(ref):
    x = ref[...]
    return x.reshape(x.shape[0] * x.shape[1], x.shape[2])


def weight(ref, index, rows):
    x = ref[:, index * rows : (index + 1) * rows, :]
    return x.reshape(x.shape[0] * rows, x.shape[2])


def window(w_any, w_ref, sem, base):
    return pltpu.make_async_copy(w_any.at[:, base : base + w_ref.shape[1], :], w_ref, sem)


def down(ref, j, rows, blocks):
    quarter = PIECES // blocks
    x = ref[quarter * j : quarter * (j + 1), rows * blocks : 2 * rows * blocks, :]
    return x.reshape(quarter * rows * blocks, x.shape[2])


def gelu_parts(u):
    c0 = math.sqrt(2.0 / math.pi)
    c1 = c0 * 0.044715
    u2 = u * u
    t = jnp.tanh(u * (c0 + c1 * u2))
    half = 0.5 * (1.0 + t)
    z = u * half
    slope = half + u * (half * (1.0 - t)) * (c0 + (3.0 * c1) * u2)
    return z, slope


def mask_rows(seg_ref, length, slots):
    width = length // slots
    qs, ks = [], []
    for s in range(slots):
        row = lax.broadcasted_iota(jnp.int32, (EXTRA, width), 0)
        seg = seg_ref[0, s]
        same = row == seg
        first = row < slots
        qs.append(jnp.where(same | ~first, 0.0, 1.0))
        ks.append(jnp.where(same, -BIG, jnp.where((row >= 4) & (row < 7), 1.0, 0.0)))
    return jnp.concatenate(qs, axis=1), jnp.concatenate(ks, axis=1)


class Links:
    def __init__(self):
        me = lax.axis_index("fsdp")
        x = lax.axis_index("rep")
        c = lax.rem(me, 2)
        y = lax.rem(lax.div(me, 2), 2)
        low = lax.rem(lax.div(me, 4), 2)
        high = lax.div(me, 8)
        self.at = {"c": c, "y": y, "l": low, "h": high, "x": x}
        self.peer = {
            "c": {"fsdp": me + 1 - 2 * c, "rep": x},
            "y": {"fsdp": me + 2 - 4 * y, "rep": x},
            "l": {"fsdp": me + 4 - 8 * low, "rep": x},
            "h": {"fsdp": me + 8 - 16 * high, "rep": x},
            "x": {"fsdp": me, "rep": 1 - x},
        }

    def meet(self):
        barrier = pltpu.get_barrier_semaphore()
        for who in self.peer.values():
            pl.semaphore_signal(barrier, inc=1, device_id=who, device_id_type=pl.DeviceIdType.MESH)
        pl.semaphore_wait(barrier, len(self.peer))


class Reduction(Links):
    ORDERS = ("yxlh", "xylh", "lhyx")
    STEPS = 6

    @classmethod
    def paths(cls, rows, subs):
        found, start = [], 0
        for sub in range(subs):
            units = rows // 32 * (sub + 1) // subs - rows // 32 * sub // subs
            third = (units + 2) // 4
            first = (units - third + 1) // 2
            for order, count in zip(cls.ORDERS, (first, units - third - first, third)):
                found.append((order, start, 32 * count))
                start += 32 * count
        return found

    @classmethod
    def scratch(cls, rows, subs, width):
        shapes = [pltpu.VMEM((2, 2, 2, rows, width), bf16)] * 2
        for order, _, count in cls.paths(rows, subs):
            free = 3
            for axis in order:
                if axis == "x":
                    count //= 2
                else:
                    free -= 1
                shapes.append(pltpu.VMEM((2,) * free + (count, width), bf16))
        return shapes + [pltpu.SemaphoreType.DMA((18 * subs,)), pltpu.SemaphoreType.DMA((21 * subs,))]

    def __init__(self, subs, v_any, fin_ref, refs):
        self.subs, self.v, self.fin = subs, v_any, fin_ref
        self.own, self.got = refs[0], refs[1]
        self.bufs = [refs[2 + 4 * k : 6 + 4 * k] for k in range(3 * subs)]
        self.send_sem, self.recv_sem = refs[-2], refs[-1]
        self.parts = self.paths(self.own.shape[3], subs)
        super().__init__()

    def remote(self, src, dst, sem, who):
        return pltpu.make_async_remote_copy(
            src_ref=src,
            dst_ref=dst,
            send_sem=self.send_sem.at[sem],
            recv_sem=self.recv_sem.at[sem],
            device_id=self.peer[who],
            device_id_type=pl.DeviceIdType.MESH,
        )

    def local(self, path):
        _, start, count = self.parts[path]
        rows = pl.ds(start, count)
        return pltpu.make_async_copy(
            self.v.at[:, :, :, self.at["c"], rows, :], self.own.at[:, :, :, rows, :], self.recv_sem.at[18 * self.subs + path]
        )

    def cores(self, path):
        _, start, count = self.parts[path]
        rows = pl.ds(start, count)
        src = self.v.at[:, :, :, 1 - self.at["c"], rows, :]
        return self.remote(src, self.got.at[:, :, :, rows, :], 6 * path, "c")

    def places(self, path, step):
        order, start, count = self.parts[path]
        fixed = {}
        rows = pl.ds(start, count)
        send = None
        for axis in order[: step + 1]:
            send = (dict(fixed), rows)
            if axis == "x":
                half = count // 2
                send = (dict(fixed), pl.ds(pl.multiple_of(start + (1 - self.at["x"]) * half, 16), half))
                rows = pl.ds(pl.multiple_of(start + self.at["x"] * half, 16), half)
            else:
                send[0][axis] = 1 - self.at[axis]
                fixed[axis] = self.at[axis]
        return send, (fixed, rows)

    @staticmethod
    def index(place, free=()):
        fixed, rows = place
        found, free = [], list(free)
        for axis in "hly":
            found.append(fixed[axis] if axis in fixed else (free.pop(0) if free else slice(None)))
        return (*found, rows, slice(None))

    def exchange(self, path, step):
        sem = 6 * path + 1 + step
        if step == 4:
            keep = self.places(path, 3)[1]
            return self.remote(self.own.at[self.index(keep)], self.fin.at[keep[1], :], sem, "x")
        send, _ = self.places(path, step)
        return self.remote(self.own.at[self.index(send)], self.bufs[path][step], sem, self.parts[path][0][step])

    def start(self):
        self.meet()
        for path in range(3 * self.subs):
            self.cores(path).start()
            self.local(path).start()

    def add(self, place, other):
        free = 3 - len(place[0])

        def one(i, carry):
            bits = [lax.rem(lax.div(i, 2 ** (free - 1 - b)), 2) for b in range(free)]
            where = self.index(place, bits)
            self.own[where] = self.own[where] + other(bits)
            return carry

        if free:
            lax.fori_loop(0, 2**free, one, 0)
        else:
            one(0, 0)

    def advance(self, path, step):
        if step == 0:
            self.cores(path).wait()
            self.local(path).wait()
            _, start, count = self.parts[path]
            place = ({}, pl.ds(start, count))
            self.add(place, lambda bits: self.got[self.index(place, bits)])
            self.exchange(path, 0).start()
            return
        k = step - 1
        self.exchange(path, k).wait()
        if k == 4:
            return
        place = self.places(path, k)[1]
        buf = self.bufs[path][k]
        self.add(place, lambda bits: buf[(*bits, slice(None), slice(None))])
        self.exchange(path, k + 1).start()
        if k == 3:
            self.fin[place[1], :] = self.own[self.index(place)]

    def run(self, moves):
        for sub, step in moves:
            for path in range(3 * sub, 3 * sub + 3):
                self.advance(path, step)


def reduction_kernel(subs, v_any, fin_ref, *refs):
    red = Reduction(subs, v_any, fin_ref, refs)
    red.start()
    for step in range(Reduction.STEPS):
        red.run([(sub, step) for sub in range(subs)])


def six(x):
    return x.reshape((2, 2, 2, 2) + x.shape[1:])


def reduced(x, subs, ident):
    rows, width = x.shape[1:]
    return pl.pallas_call(
        functools.partial(reduction_kernel, subs),
        name="reduction",
        in_specs=[pl.BlockSpec(memory_space=pl.ANY)],
        out_specs=pl.BlockSpec(memory_space=pltpu.VMEM),
        out_shape=sds((rows, width), bf16),
        scratch_shapes=Reduction.scratch(rows, subs, width),
        compiler_params=pltpu.CompilerParams(
            vmem_limit_bytes=VMEM_BYTES, collective_id=ident, has_side_effects=True
        ),
    )(six(x))


def gather_kernel(ident, x_any, out_any, send_sem, recv_sem, own_sem):
    red = Links()
    at = red.at
    rows = x_any.shape[0]
    mine = (at["h"], at["l"], at["y"], at["c"])
    own = pltpu.make_async_copy(x_any, out_any.at[(*mine, slice(None), slice(None))], own_sem)
    own.start()
    own.wait()
    red.meet()

    def copy(path, step):
        order, start, count = path
        order = order[::-1] + "c"
        free = order[:step]
        half = count // 2
        if "x" in free:
            span = pl.ds(start, count)
        else:
            span = pl.ds(pl.multiple_of(start + at["x"] * half, 16), half)
        where = tuple(slice(None) if a in free else at[a] for a in "hlyc") + (span, slice(None))
        sem = 5 * paths.index(path) + step
        return pltpu.make_async_remote_copy(
            src_ref=out_any.at[where],
            dst_ref=out_any.at[where],
            send_sem=send_sem.at[sem],
            recv_sem=recv_sem.at[sem],
            device_id=red.peer[order[step]],
            device_id_type=pl.DeviceIdType.MESH,
        )

    paths = Reduction.paths(rows, 1)
    for path in paths:
        copy(path, 0).start()
    for step in range(5):
        for path in paths:
            copy(path, step).wait()
            if step < 4:
                copy(path, step + 1).start()


def gathered(x, ident):
    rows, width = x.shape
    out = pl.pallas_call(
        functools.partial(gather_kernel, ident),
        name="gather",
        in_specs=[pl.BlockSpec(memory_space=pl.ANY)],
        out_specs=pl.BlockSpec(memory_space=pl.ANY),
        out_shape=sds((2, 2, 2, 2, rows, width), bf16),
        scratch_shapes=[pltpu.SemaphoreType.DMA((15,)), pltpu.SemaphoreType.DMA((15,)), pltpu.SemaphoreType.DMA],
        compiler_params=pltpu.CompilerParams(
            vmem_limit_bytes=8 * 1024 * 1024, collective_id=ident, has_side_effects=True
        ),
        cost_estimate=pl.CostEstimate(flops=0, bytes_accessed=100 << 20, transcendentals=0),
    )(x)
    return out.reshape(PIECES, rows, width)


def attn_forward_kernel(
    base, red, h_ref, w_any, vec_ref, seg_ref,
    g_ref, at_ref, qe_ref, ke_ref, ve_ref, ot_ref, ol_ref, w_ref, w_sem,
):
    length, width = h_ref.shape
    hd = width // HEADS
    rows = width // PIECES
    scale = math.log2(math.e) / math.sqrt(hd)
    fetch = window(w_any, w_ref, w_sem, base)
    fetch.start()
    x = h_ref[...].astype(f32)
    xh, _ = normalised(x)
    a = (xh * vec_ref[0:1, :] + vec_ref[1:2, :]).astype(bf16)
    at_ref[...] = a.T
    fetch.wait()
    q = (mm(a, weight(w_ref, 0, rows)) + vec_ref[2:3, :]).astype(bf16)
    qe_ref[:, 0:hd, :] = q.T.reshape(HEADS, hd, length)
    k = mm(a, weight(w_ref, 1, rows)).astype(bf16)
    ke_ref[:, 0:hd, :] = k.T.reshape(HEADS, hd, length)
    v = (mm(a, weight(w_ref, 2, rows)) + vec_ref[3:4, :]).astype(bf16)
    ve_ref[:, 0:hd, :] = v.T.reshape(HEADS, hd, length)
    mask_q, mask_k = mask_rows(seg_ref, length, seg_ref.shape[1])
    qe_ref[:, hd:, :] = jnp.broadcast_to(mask_q.astype(bf16)[None], (HEADS, EXTRA, length))
    ke_ref[:, hd:, :] = jnp.broadcast_to(mask_k.astype(bf16)[None], (HEADS, EXTRA, length))
    ve_ref[:, hd:, :] = jnp.ones((HEADS, EXTRA, length), bf16)
    row = lax.broadcasted_iota(jnp.int32, (EXTRA, length // FORWARD_PARTS), 0)

    part = length // FORWARD_PARTS

    def head(i):
        for t in range(FORWARD_PARTS):
            cols = slice(t * part, (t + 1) * part)
            st = mm_tn(ke_ref[i], qe_ref[i, :, cols])
            peak = jnp.max(st, axis=0, keepdims=True)
            e = jnp.exp2((st - peak) * scale).astype(bf16)
            mix = mm(ve_ref[i], e)
            total = mix[hd : hd + 1, :]
            o = mix[0:hd, :] * (1.0 / total)
            high = o.astype(bf16)
            ot_ref[i, :, cols] = high
            ol_ref[i, :, cols] = (o - high.astype(f32)).astype(bf16)
            lse = -(peak + jnp.log2(total) * (1.0 / scale))
            hi, mid, low = split3(lse)
            ext = jnp.where(row == 6, low.astype(f32), mask_q[:, cols])
            ext = jnp.where(row == 4, hi.astype(f32), jnp.where(row == 5, mid.astype(f32), ext))
            qe_ref[i, hd:, cols] = ext.astype(bf16)

    def pair(j, carry):
        for k in range(UNROLL):
            head(UNROLL * j + k)
        return carry

    lax.fori_loop(0, HEADS // UNROLL, pair, 0)
    g_ref[...] = x + (mm_tn(joined(ot_ref), weight(w_ref, 3, rows)) + vec_ref[4:5, :])


def full(shape):
    return pl.BlockSpec(shape, lambda: (0,) * len(shape))


ANY = pl.BlockSpec(memory_space=pl.ANY)


def call(kernel, name, args, specs, outs, flops, nbytes, scratch, carry=None, ident=None):
    n_in, n_out, n_scratch = len(args), len(outs), len(scratch)
    args, outs, scratch = list(args), list(outs), list(scratch)
    specs = list(specs)
    out_specs = [full(s.shape) for s in outs]
    if carry is None:
        body = functools.partial(kernel, None)
    else:
        grads, subs = carry
        rows, width = grads.shape[1:]
        args.append(six(grads))
        specs.append(ANY)
        outs.append(sds((rows, width), bf16))
        out_specs.append(full((rows, width)))
        scratch += Reduction.scratch(rows, subs, width)

        def body(*refs):
            ins, v = refs[:n_in], refs[n_in]
            results = refs[n_in + 1 : n_in + 1 + n_out]
            fin = refs[n_in + 1 + n_out]
            rest = refs[n_in + 2 + n_out :]
            kernel(Reduction(subs, v, fin, rest[n_scratch:]), *ins, *results, *rest[:n_scratch])

    return pl.pallas_call(
        body,
        name=name,
        in_specs=specs,
        out_specs=out_specs,
        out_shape=outs,
        scratch_shapes=scratch,
        compiler_params=pltpu.CompilerParams(
            vmem_limit_bytes=VMEM_BYTES, collective_id=ident, has_side_effects=ident is not None
        ),
        cost_estimate=pl.CostEstimate(flops=flops, bytes_accessed=nbytes, transcendentals=0),
    )(*args)


def advance_at(red, index, plan):
    if red is None:
        return
    for at, moves in plan.items():

        @pl.when(index == at)
        def _(moves=moves):
            red.run(moves)


def sds(shape, dtype):
    return jax.ShapeDtypeStruct(shape, dtype)


SMEM = pltpu.SMEM


def attn_forward(h, square, vec, seg):
    square, base = square
    n, d = h.shape
    hd = d // HEADS
    rows = d // PIECES
    ext = hd + EXTRA
    outs = (
        sds((n, d), f32),
        sds((d, n), bf16),
        sds((HEADS, ext, n), bf16),
        sds((HEADS, ext, n), bf16),
        sds((HEADS, ext, n), bf16),
        sds((HEADS, hd, n), bf16),
        sds((HEADS, hd, n), bf16),
    )
    specs = [full(h.shape), pl.BlockSpec(memory_space=pl.ANY)]
    specs += [full(vec.shape), pl.BlockSpec(memory_space=SMEM)]
    flops = 8 * n * d * d + 2 * HEADS * 2 * n * n * 256
    scratch = [pltpu.VMEM((PIECES, 4 * rows, d), bf16), pltpu.SemaphoreType.DMA]
    return call(
        functools.partial(attn_forward_kernel, base), "attn_forward", (h, square, vec, seg),
        specs, outs, flops, 30 << 20, scratch,
    )


def ff_forward_kernel(base, g_ref, w_any, vec_ref, h_ref, b_ref, z_ref, s_ref, w_ref, w_sem):
    width = g_ref.shape[1]
    rows = width // PIECES
    blocks = z_ref.shape[1] // width

    @pl.when(pl.program_id(0) == 0)
    def _():
        fetch = window(w_any, w_ref, w_sem, base)
        fetch.start()
        fetch.wait()

    gg = g_ref[...]
    xh, _ = normalised(gg)
    b = (xh * vec_ref[5:6, :] + vec_ref[6:7, :]).astype(bf16)
    b_ref[...] = b
    acc = gg + vec_ref[7:8, :]
    for j in range(blocks):
        w = weight(w_ref, j, rows)
        u = mm(b, w) + vec_ref[8 + j : 9 + j, :]
        z, slope = gelu_parts(u)
        zb = z.astype(bf16)
        z_ref[:, j * width : (j + 1) * width] = zb
        s_ref[:, j * width : (j + 1) * width] = slope.astype(bf16)
        wd = down(w_ref, j, rows, blocks)
        acc = acc + mm(zb, wd)
    h_ref[...] = acc


def ff_forward(g, wide, vec, ff):
    wide, base = wide
    n, d = g.shape
    tile = 256
    outs = (sds((n, d), f32), sds((n, d), bf16), sds((n, ff), bf16), sds((n, ff), bf16))
    row = lambda w: pl.BlockSpec((tile, w), lambda i: (i, 0))
    return pl.pallas_call(
        functools.partial(ff_forward_kernel, base),
        name="ff_forward",
        grid=(n // tile,),
        in_specs=[
            row(d),
            pl.BlockSpec(memory_space=pl.ANY),
            pl.BlockSpec(vec.shape, lambda i: (0, 0)),
        ],
        out_specs=[row(d), row(d), row(ff), row(ff)],
        out_shape=outs,
        scratch_shapes=[pltpu.VMEM((PIECES, 2 * ff // PIECES, d), bf16), pltpu.SemaphoreType.DMA],
        compiler_params=pltpu.CompilerParams(vmem_limit_bytes=VMEM_BYTES),
        cost_estimate=pl.CostEstimate(flops=4 * n * d * ff, bytes_accessed=30 << 20, transcendentals=0),
    )(g, wide, vec)


def put_vectors(grad_ref, base, cols_ref, per):
    pad = grad_ref.shape[1] - base
    lanes = grad_ref.shape[2] // 128
    count = per // lanes
    for m in range(lanes):
        part = cols_ref[pl.ds(m, PIECES * count, stride=lanes), :]
        part = part.reshape(PIECES, count, 128)
        part = jnp.concatenate([part, jnp.zeros((PIECES, pad - count, 128), f32)], axis=1)
        grad_ref[:, base : base + pad, m * 128 : (m + 1) * 128] = part.astype(bf16)


def ff_tail(z_ref, du_ref, b_ref, cm_ref, grad_ref, cols_ref, vecs, width, blocks, red=None):
    rows = width // PIECES
    quarter = PIECES // blocks
    n = b_ref.shape[0]

    def block(j, carry):
        advance_at(red, j, {1: [(0, 2)], 2: [(0, 3)], 3: [(0, 4)]})
        cols = pl.ds(pl.multiple_of(j * width, 128), width)
        dwd = mm_tn(z_ref[:, cols], cm_ref[...])
        grad_ref[pl.ds(quarter * j, quarter), rows * blocks : 2 * rows * blocks, :] = (
            dwd.reshape(quarter, rows * blocks, width).astype(bf16)
        )
        dwu = mm_tn(b_ref[...], du_ref[:, cols])
        grad_ref[:, pl.ds(pl.multiple_of(rows * j, 16), rows), :] = (
            dwu.reshape(PIECES, rows, width).astype(bf16)
        )
        return carry

    lax.fori_loop(0, blocks, block, 0)
    ones = jnp.ones((n, 128), bf16)
    vt = jnp.concatenate([*vecs, jnp.zeros((128 - len(vecs), width), f32)], axis=0).T
    vt = vt.reshape(PIECES, rows, 128)
    lane = lax.broadcasted_iota(jnp.int32, (quarter, rows, 128), 2)
    for j in range(blocks):
        part = mm_tn(du_ref[:, j * width : (j + 1) * width], ones)
        part = part.reshape(quarter, blocks, rows, 128)
        piece = vt[quarter * j : quarter * (j + 1)]
        for c in range(blocks):
            piece = jnp.where(lane == len(vecs) + c, part[:, c], piece)
        cols_ref[quarter * rows * j : quarter * rows * (j + 1), :] = piece.reshape(quarter * rows, 128)
    put_vectors(grad_ref, 2 * rows * blocks, cols_ref, rows)
    if red is not None:
        red.run([(0, 5)])


def ff_last_kernel(
    base, red, g_ref, w_any, vec_ref, cot_ref, live_ref, out_ref, dg_ref, grad_ref,
    z_ref, du_ref, b_ref, cm_ref, cols_ref, w_ref, w_sem,
):
    n, width = g_ref.shape
    rows = width // PIECES
    blocks = z_ref.shape[1] // width
    tile = n // 4
    gain = vec_ref[5:6, :]
    fetch = window(w_any, w_ref, w_sem, base)
    fetch.start()
    fetch.wait()

    def step(t, sums):
        sum_gain, sum_bias, sum_down = sums
        span = pl.ds(pl.multiple_of(t * tile, 16), tile)
        gg = g_ref[span, :]
        xh, r = normalised(gg)
        b = (xh * gain + vec_ref[6:7, :]).astype(bf16)
        b_ref[span, :] = b
        grad = cot_ref[span, :].astype(f32) * live_ref[0, t].astype(f32)
        cm = grad.astype(bf16)
        cm_ref[span, :] = cm
        acc = gg + vec_ref[7:8, :]
        db = jnp.zeros((tile, width), f32)
        for j in range(blocks):
            cols = slice(j * width, (j + 1) * width)
            w = weight(w_ref, j, rows)
            wd = down(w_ref, j, rows, blocks)
            u = mm(b, w) + vec_ref[8 + j : 9 + j, :]
            dz = mm_nt(cm, wd)
            z, slope = gelu_parts(u)
            zb = z.astype(bf16)
            z_ref[span, cols] = zb
            acc = acc + mm(zb, wd)
            du = (slope * dz).astype(bf16)
            du_ref[span, cols] = du
            db = db + mm_nt(du, w)
        out_ref[span, :] = acc.astype(bf16)
        dg_ref[span, :] = grad + norm_back(db, xh, r, gain)
        sum_gain = sum_gain + jnp.sum(db * xh, axis=0, keepdims=True)
        sum_bias = sum_bias + jnp.sum(db, axis=0, keepdims=True)
        sum_down = sum_down + jnp.sum(cm.astype(f32), axis=0, keepdims=True)
        return sum_gain, sum_bias, sum_down

    zero = jnp.zeros((1, width), f32)
    sums = lax.fori_loop(0, 4, step, (zero, zero, zero))
    ff_tail(z_ref, du_ref, b_ref, cm_ref, grad_ref, cols_ref, sums, width, blocks)


def ff_last(g, wide, vec, cot, live, ff):
    wide, base = wide
    n, d = g.shape
    rows = d // PIECES
    outs = (sds((n, d), bf16), sds((n, d), f32), sds((PIECES, 2 * rows * (ff // d) + 2 * EXTRA, d), bf16))
    specs = [full(g.shape), pl.BlockSpec(memory_space=pl.ANY), full(vec.shape), full(cot.shape), pl.BlockSpec(memory_space=SMEM)]
    scratch = [
        pltpu.VMEM((n, ff), bf16), pltpu.VMEM((n, ff), bf16), pltpu.VMEM((n, d), bf16),
        pltpu.VMEM((n, d), bf16), pltpu.VMEM((d, 128), f32),
        pltpu.VMEM((PIECES, 2 * ff // PIECES, d), bf16), pltpu.SemaphoreType.DMA,
    ]
    return call(
        functools.partial(ff_last_kernel, base), "ff_last", (g, wide, vec, cot, live),
        specs, outs, 12 * n * d * ff, 30 << 20, scratch,
    )


def ff_backward_kernel(
    base, red, g_ref, w_any, vec_ref, c_ref, b_ref, z_ref, s_ref, dg_ref, grad_ref, du_ref, cm_ref, cols_ref,
    w_ref, w_sem,
):
    n, width = g_ref.shape
    rows = width // PIECES
    blocks = z_ref.shape[1] // width
    tile = n // 4
    gain = vec_ref[5:6, :]
    fetch = window(w_any, w_ref, w_sem, base)
    fetch.start()
    if red is not None:
        red.start()
    fetch.wait()

    def step(t, sums):
        advance_at(red, t, {0: [(0, 0)], 3: [(0, 1)]})
        sum_gain, sum_bias, sum_down = sums
        span = pl.ds(pl.multiple_of(t * tile, 16), tile)
        xh, r = normalised(g_ref[span, :])
        grad = c_ref[span, :]
        cm = grad.astype(bf16)
        cm_ref[span, :] = cm
        db = jnp.zeros((tile, width), f32)
        for j in range(blocks):
            cols = slice(j * width, (j + 1) * width)
            w = weight(w_ref, j, rows)
            wd = down(w_ref, j, rows, blocks)
            du = (s_ref[span, cols].astype(f32) * mm_nt(cm, wd)).astype(bf16)
            du_ref[span, cols] = du
            db = db + mm_nt(du, w)
        dg_ref[span, :] = grad + norm_back(db, xh, r, gain)
        sum_gain = sum_gain + jnp.sum(db * xh, axis=0, keepdims=True)
        sum_bias = sum_bias + jnp.sum(db, axis=0, keepdims=True)
        sum_down = sum_down + jnp.sum(cm.astype(f32), axis=0, keepdims=True)
        return sum_gain, sum_bias, sum_down

    zero = jnp.zeros((1, width), f32)
    sums = lax.fori_loop(0, 4, step, (zero, zero, zero))
    ff_tail(z_ref, du_ref, b_ref, cm_ref, grad_ref, cols_ref, sums, width, blocks, red)


def ff_backward(g, wide, vec, c, b, z, s, carry=None, ident=None):
    wide, base = wide
    n, d = g.shape
    ff = z.shape[1]
    rows = d // PIECES
    outs = (sds((n, d), f32), sds((PIECES, 2 * rows * (ff // d) + 2 * EXTRA, d), bf16))
    specs = [full(g.shape), pl.BlockSpec(memory_space=pl.ANY)] + [full(x.shape) for x in (vec, c, b, z, s)]
    scratch = [pltpu.VMEM((n, ff), bf16), pltpu.VMEM((n, d), bf16), pltpu.VMEM((d, 128), f32)]
    scratch += [pltpu.VMEM((PIECES, 2 * ff // PIECES, d), bf16), pltpu.SemaphoreType.DMA]
    return call(
        functools.partial(ff_backward_kernel, base), "ff_backward", (g, wide, vec, c, b, z, s),
        specs, outs, 8 * n * d * ff, 40 << 20, scratch, carry, ident,
    )


def attn_backward_kernel(
    base, red, h_ref, dg_ref, w_any, vec_ref, at_ref, qe_ref, ke_ref, ve_ref, ot_ref, ol_ref,
    c_ref, grad_ref, doe_ref, dq_ref, dk_ref, dv_ref, cols_ref, w_ref, w_sem,
):
    n, width = h_ref.shape
    hd = width // HEADS
    rows = width // PIECES
    scale = math.log2(math.e) / math.sqrt(hd)
    factor = 1.0 / math.sqrt(hd)
    fetch = window(w_any, w_ref, w_sem, base)
    fetch.start()
    if red is not None:
        red.start()
    co = dg_ref[...].astype(bf16)
    grad_ref[:, 3 * rows : 4 * rows, :] = mm(joined(ot_ref), co).reshape(PIECES, rows, width).astype(bf16)
    fetch.wait()
    dot = mm_nt(weight(w_ref, 3, rows), co).astype(bf16)
    doe_ref[:, 0:hd, :] = dot.reshape(HEADS, hd, n)
    row = lax.broadcasted_iota(jnp.int32, (EXTRA, n), 0)
    part = n // BACKWARD_PARTS

    def head(i):
        doh = doe_ref[i, 0:hd, :]
        delta = jnp.sum(doh.astype(f32) * (ot_ref[i].astype(f32) + ol_ref[i].astype(f32)), axis=0, keepdims=True)
        hi, mid, low = split3(-delta)
        ext = jnp.where(row == 0, hi.astype(f32), jnp.where(row == 1, mid.astype(f32), jnp.where(row == 2, low.astype(f32), 0.0)))
        doe_ref[i, hd:, :] = ext.astype(bf16)
        dk = dv = None
        for t in range(BACKWARD_PARTS):
            cols = slice(t * part, (t + 1) * part)
            s = mm_tn(qe_ref[i, :, cols], ke_ref[i])
            p = jnp.exp2(s * scale)
            dp = mm_tn(doe_ref[i, :, cols], ve_ref[i])
            ds = (p * dp).astype(bf16)
            dv_t = mm(doe_ref[i, 0:hd, cols], p.astype(bf16))
            dk_t = mm(qe_ref[i, 0:hd, cols], ds)
            dv = dv_t if t == 0 else dv + dv_t
            dk = dk_t if t == 0 else dk + dk_t
            dq_ref[i, :, cols] = (mm_nt(ke_ref[i, 0:hd, :], ds) * factor).astype(bf16)
        dv_ref[i] = dv.astype(bf16)
        dk_ref[i] = (dk * factor).astype(bf16)

    def pair(j, carry):
        advance_at(red, j, ATTN_PLAN)
        for k in range(UNROLL):
            head(UNROLL * j + k)
        return carry

    lax.fori_loop(0, HEADS // UNROLL, pair, 0)
    if red is not None:
        red.run(ATTN_MIDDLE)
    at = at_ref[...]
    dq = joined(dq_ref)
    dk = joined(dk_ref)
    dv = joined(dv_ref)
    grad_ref[:, 0:rows, :] = mm_nt(at, dq).reshape(PIECES, rows, width).astype(bf16)
    grad_ref[:, rows : 2 * rows, :] = mm_nt(at, dk).reshape(PIECES, rows, width).astype(bf16)
    grad_ref[:, 2 * rows : 3 * rows, :] = mm_nt(at, dv).reshape(PIECES, rows, width).astype(bf16)
    tile = n // 4

    def norm_tile(t, sums):
        advance_at(red, t, ATTN_TILES)
        sum_gain, sum_bias, sum_out = sums
        span = pl.ds(pl.multiple_of(t * tile, 128), tile)
        dat = mm(weight(w_ref, 0, rows), dq_ref[:, :, span].reshape(width, tile))
        dat = dat + mm(weight(w_ref, 1, rows), dk_ref[:, :, span].reshape(width, tile))
        dat = dat + mm(weight(w_ref, 2, rows), dv_ref[:, :, span].reshape(width, tile))
        da = dat.T
        xh, r = normalised(h_ref[span, :].astype(f32))
        dg = dg_ref[span, :]
        c_ref[span, :] = dg + norm_back(da, xh, r, vec_ref[0:1, :])
        sum_gain = sum_gain + jnp.sum(da * xh, axis=0, keepdims=True)
        sum_bias = sum_bias + jnp.sum(da, axis=0, keepdims=True)
        sum_out = sum_out + jnp.sum(dg.astype(bf16).astype(f32), axis=0, keepdims=True)
        return sum_gain, sum_bias, sum_out

    zero = jnp.zeros((1, width), f32)
    vecs = lax.fori_loop(0, 4, norm_tile, (zero, zero, zero))
    vt = jnp.concatenate([*vecs, jnp.zeros((128 - len(vecs), width), f32)], axis=0).T
    lane = lax.broadcasted_iota(jnp.int32, (width, 128), 1)
    vt = jnp.where(lane == 3, jnp.sum(dq.astype(f32), axis=1, keepdims=True), vt)
    vt = jnp.where(lane == 4, jnp.sum(dv.astype(f32), axis=1, keepdims=True), vt)
    cols_ref[...] = vt
    put_vectors(grad_ref, 4 * rows, cols_ref, rows)
    if red is not None:
        red.run(ATTN_END)


def attn_backward(h, dg, square, vec, kept, carry=None, ident=None):
    square, base = square
    n, d = h.shape
    hd = d // HEADS
    rows = d // PIECES
    at, qe, ke, ve, ot, ol = kept
    outs = (sds((n, d), f32), sds((PIECES, 4 * rows + 2 * EXTRA, d), bf16))
    specs = [full(h.shape), full(dg.shape), pl.BlockSpec(memory_space=pl.ANY)]
    specs += [full(x.shape) for x in (vec, at, qe, ke, ve, ot, ol)]
    scratch = [pltpu.VMEM((HEADS, hd + EXTRA, n), bf16)] + [pltpu.VMEM((HEADS, hd, n), bf16)] * 3
    scratch += [pltpu.VMEM((d, 128), f32), pltpu.VMEM((PIECES, 4 * rows, d), bf16), pltpu.SemaphoreType.DMA]
    flops = 16 * n * d * d + 5 * HEADS * 2 * n * n * 256
    return call(
        functools.partial(attn_backward_kernel, base), "attn_backward", (h, dg, square, vec, at, qe, ke, ve, ot, ol),
        specs, outs, flops, 40 << 20, scratch, carry, ident,
    )


NAMES = (
    "ln1_gain", "ln1_bias", "q_weight", "q_bias", "k_weight", "v_weight", "v_bias", "o_weight", "o_bias",
    "ln2_gain", "ln2_bias", "up_weight", "up_bias", "down_weight", "down_bias",
)
ROW_VECTORS = ("ln1_gain", "ln1_bias", "q_bias", "v_bias", "o_bias", "ln2_gain", "ln2_bias", "down_bias")


def gather(x, axis="fsdp"):
    return lax.all_gather(x, axis, axis=0, tiled=True)


def column_blocks(up, d):
    return [up[:, j * d : (j + 1) * d] for j in range(up.shape[1] // d)]


def fetch_even(w, layers, shards):
    d = w["q_weight"].shape[2]
    per = w["q_weight"].shape[1]
    ff = w["up_weight"].shape[2]
    packed = []
    for l in range(layers):
        row = jnp.concatenate([w[x][l] for x in ROW_VECTORS] + [w["up_bias"][l]])
        packed.append(jnp.pad(row, (0, d - row.shape[0]))[None])
    rows = jnp.concatenate(packed + [jnp.zeros((2 * EXTRA - layers, d), bf16)], axis=0)
    square = lambda l: [w[x][l] for x in ("q_weight", "k_weight", "v_weight", "o_weight")]
    wide = lambda l: column_blocks(w["up_weight"][l], d) + [w["down_weight"][l]]
    first = jnp.concatenate(square(0) + [rows], axis=0)
    first = gathered(first, 20)
    rest = wide(0)
    for l in range(1, layers):
        rest = rest + square(l) + wide(l)
    rest = gather(jnp.concatenate(rest, axis=0)).reshape(shards, -1, d)
    flat = first[:, 4 * per : 4 * per + layers, :]
    count = len(ROW_VECTORS)
    vecs = flat[:, :, : count * per].reshape(shards, layers, count, per).transpose(1, 2, 0, 3)
    vecs = vecs.reshape(layers, count, d)
    ups = flat[:, :, count * per : count * per + ff // shards].transpose(1, 0, 2).reshape(layers, ff // d, d)
    vec = jnp.concatenate([vecs, ups], axis=1).astype(f32)
    wides = [(rest, 0)]
    squares = [(first, 0)]
    base = 2 * per * (ff // d)
    for l in range(1, layers):
        squares.append((rest, base))
        wides.append((rest, base + 4 * per))
        base += 4 * per + 2 * per * (ff // d)
    return squares, wides, [vec[l] for l in range(layers)]


def fetch_any(w, layers):
    d = w["q_weight"].shape[2]
    squares, wides, vecs = [], [], []
    for l in range(layers):
        whole = {x: gather(w[x][l]) for x in NAMES}
        cut = lambda x: x.reshape(PIECES, x.shape[0] // PIECES, d)
        squares.append((jnp.concatenate([cut(whole[x]) for x in ("q_weight", "k_weight", "v_weight", "o_weight")], axis=1), 0))
        blocks = [cut(x) for x in column_blocks(whole["up_weight"], d)] + [cut(whole["down_weight"])]
        wides.append((jnp.concatenate(blocks, axis=1), 0))
        rows = [whole[x][None] for x in ROW_VECTORS] + [whole["up_bias"].reshape(-1, d)]
        vecs.append(jnp.concatenate(rows, axis=0).astype(f32))
    return squares, wides, vecs


def over_rep(x):
    size = lax.axis_size("rep")
    if size == 1:
        return x.astype(f32)
    other = lax.ppermute(x, "rep", [(i, (i + 1) % size) for i in range(size)])
    return x.astype(f32) + other.astype(f32)


def restack(grads_square, grads_wide, d, ff):
    per = d // PIECES
    blocks = ff // d
    gs, gw = grads_square, grads_wide
    out = {x: gs[:, j * per : (j + 1) * per].reshape(d, d) for j, x in enumerate(("q_weight", "k_weight", "v_weight", "o_weight"))}
    out["up_weight"] = jnp.concatenate([gw[:, j * per : (j + 1) * per].reshape(d, d) for j in range(blocks)], axis=1)
    out["down_weight"] = gw[:, blocks * per : 2 * blocks * per].reshape(ff, d)
    count = per // (d // 128)
    vs = gs[:, 4 * per : 4 * per + count].reshape(d, 128)
    vw = gw[:, 2 * blocks * per : 2 * blocks * per + count].reshape(PIECES, per, 128)
    for j, x in enumerate(("ln1_gain", "ln1_bias", "o_bias", "q_bias", "v_bias")):
        out[x] = vs[:, j]
    for j, x in enumerate(("ln2_gain", "ln2_bias", "down_bias")):
        out[x] = vw[:, :, j].reshape(d)
    out["up_bias"] = vw[:, :, 3 : 3 + blocks].transpose(0, 2, 1).reshape(ff)
    sums = {}
    for x, g in out.items():
        sums[x] = over_rep(lax.psum_scatter(g, "fsdp", scatter_dimension=0, tiled=True))
    return sums


def finish_kernel(layers, blocks, *refs):
    ins, outs, cols_ref = refs[: 2 * layers], dict(zip(NAMES, refs[2 * layers : -1])), refs[-1]
    per = outs["q_weight"].shape[1]
    width = outs["q_weight"].shape[2]
    lanes = width // 128
    for l in range(layers):
        square, wide = ins[2 * l], ins[2 * l + 1]
        for j, x in enumerate(("q_weight", "k_weight", "v_weight", "o_weight")):
            outs[x][l] = square[j * per : (j + 1) * per, :].astype(f32)
        for j in range(blocks):
            outs["up_weight"][l, :, j * width : (j + 1) * width] = wide[j * per : (j + 1) * per, :].astype(f32)
        outs["down_weight"][l] = wide[blocks * per : 2 * blocks * per, :].astype(f32)
        for ref, base, names in (
            (square, 4 * per, ("ln1_gain", "ln1_bias", "o_bias", "q_bias", "v_bias")),
            (wide, 2 * blocks * per, ("ln2_gain", "ln2_bias", "down_bias")),
        ):
            for m in range(lanes):
                part = ref[base : base + per // lanes, m * 128 : (m + 1) * 128].astype(f32)
                cols_ref[pl.ds(m, per // lanes, stride=lanes), :] = part
            turned = cols_ref[...].T
            for j, x in enumerate(names):
                outs[x][l : l + 1, :] = turned[j : j + 1, :]
            if ref is wide:
                for c in range(blocks):
                    row = turned[len(names) + c : len(names) + c + 1, :]
                    outs["up_bias"][l : l + 1, c * per : (c + 1) * per] = row


def finish(pairs, d, ff):
    layers, per = len(pairs), d // PIECES
    shapes = {x: (layers, per) for x in NAMES}
    for x in ("q_weight", "k_weight", "v_weight", "o_weight"):
        shapes[x] = (layers, per, d)
    shapes["up_weight"], shapes["down_weight"], shapes["up_bias"] = (layers, per, ff), (layers, ff // PIECES, d), (layers, ff // PIECES)
    args = [x for pair in pairs for x in pair]
    return pl.pallas_call(
        functools.partial(finish_kernel, layers, ff // d),
        name="finish",
        in_specs=[full(x.shape) for x in args],
        out_specs=[full(shapes[x]) for x in NAMES],
        out_shape=[sds(shapes[x], f32) for x in NAMES],
        scratch_shapes=[pltpu.VMEM((per, 128), f32)],
        compiler_params=pltpu.CompilerParams(vmem_limit_bytes=VMEM_BYTES),
    )(*args)


def on_device(tokens, segment, live, cotangent, *weights):
    w = dict(zip(NAMES, weights))
    layers, per, d = w["q_weight"].shape
    ff = w["up_weight"].shape[2]
    shards = lax.axis_size("fsdp")
    even = shards == PIECES and lax.axis_size("rep") == 2
    squares, wides, vecs = fetch_even(w, layers, shards) if even else fetch_any(w, layers)
    hidden = tokens
    kept = []
    for l in range(layers - 1):
        g, *saved = attn_forward(hidden, squares[l], vecs[l], segment)
        after, *more = ff_forward(g, wides[l], vecs[l], ff)
        kept.append((hidden, g, saved, more))
        hidden = after
    l = layers - 1
    g, *saved = attn_forward(hidden, squares[l], vecs[l], segment)
    block_out, grad, gw = ff_last(g, wides[l], vecs[l], cotangent, live, ff)
    if not even:
        grad, gs = attn_backward(hidden, grad, squares[l], vecs[l], saved)
        results = [restack(gs, gw, d, ff)]
        for l in reversed(range(layers - 1)):
            hidden, g, saved, more = kept[l]
            grad, gw = ff_backward(g, wides[l], vecs[l], grad, *more)
            grad, gs = attn_backward(hidden, grad, squares[l], vecs[l], saved)
            results.insert(0, restack(gs, gw, d, ff))
    else:
        grad, gs, rw = attn_backward(hidden, grad, squares[l], vecs[l], saved, (gw, 2), 2 + 2 * l)
        pairs = []
        for l in reversed(range(layers - 1)):
            hidden, g, saved, more = kept[l]
            grad, gw, rs = ff_backward(g, wides[l], vecs[l], grad, *more, carry=(gs, 1), ident=3 + 2 * l)
            pairs.insert(0, (rs, rw))
            grad, gs, rw = attn_backward(hidden, grad, squares[l], vecs[l], saved, (gw, 2), 2 + 2 * l)
        pairs.insert(0, (reduced(gs, 1, 1), rw))
        return (block_out, grad) + tuple(finish(pairs, d, ff))
    return (block_out, grad) + tuple(jnp.stack([r[x] for r in results]) for x in NAMES)


def solution(mesh):
    tok = P(("fsdp", "rep"), None)
    specs = tuple(P(None, "fsdp", None) if x.endswith("weight") else P(None, "fsdp") for x in NAMES)
    return jax.shard_map(
        on_device,
        mesh=mesh,
        in_specs=(tok, tok, tok, tok) + specs,
        out_specs=(tok, tok) + specs,
        check_vma=False,
    )
```

```python
import functools
import math

import jax
import jax.numpy as jnp
from jax import lax
from jax.experimental import pallas as pl
from jax.experimental.pallas import tpu as pltpu
from jax.sharding import PartitionSpec as P

HEADS = 16
PIECES = 16
EXTRA = 16
EPSILON = 1e-06
BIG = 1e30
bf16 = jnp.bfloat16
f32 = jnp.float32
FORWARD_PARTS = 1
BACKWARD_PARTS = 4
UNROLL = 2
ATTN_PLAN = {2: [(0, 1)], 4: [(1, 1)], 5: [(0, 2)], 6: [(1, 2)], 7: [(0, 3)]}
ATTN_MIDDLE = [(1, 3), (0, 4)]
ATTN_TILES = {0: [(0, 5)], 1: [(1, 4)]}
ATTN_END = [(1, 5)]
FF_TILES = {3: [(0, 1)]}
FF_BLOCKS = {1: [(0, 2)], 2: [(0, 3)], 3: [(0, 4)]}
FF_END = [(0, 5)]
VMEM_BYTES = 60 * 1024 * 1024


def mm(a, b):
    return jnp.dot(a, b, preferred_element_type=f32)


def mm_tn(a, b):
    return lax.dot_general(a, b, (((0,), (0,)), ((), ())), preferred_element_type=f32)


def mm_nt(a, b):
    return lax.dot_general(a, b, (((1,), (1,)), ((), ())), preferred_element_type=f32)


def normalised(x):
    mean = jnp.mean(x, axis=-1, keepdims=True)
    centred = x - mean
    var = jnp.mean(centred * centred, axis=-1, keepdims=True)
    r = lax.rsqrt(var + EPSILON)
    return centred * r, r


def norm_back(d, xh, r, gain):
    e = d * gain
    m1 = jnp.mean(e, axis=-1, keepdims=True)
    m2 = jnp.mean(e * xh, axis=-1, keepdims=True)
    return r * (e - m1 - xh * m2)


def split3(x):
    hi = x.astype(bf16)
    rest = x - hi.astype(f32)
    mid = rest.astype(bf16)
    low = (rest - mid.astype(f32)).astype(bf16)
    return hi, mid, low


def joined(ref):
    x = ref[...]
    return x.reshape(x.shape[0] * x.shape[1], x.shape[2])


def weight(ref, index, rows):
    x = ref[:, index * rows : (index + 1) * rows, :]
    return x.reshape(x.shape[0] * rows, x.shape[2])


def window(w_any, w_ref, sem, base):
    return pltpu.make_async_copy(w_any.at[:, base : base + w_ref.shape[1], :], w_ref, sem)


def down(ref, j, rows, blocks):
    quarter = PIECES // blocks
    x = ref[quarter * j : quarter * (j + 1), rows * blocks : 2 * rows * blocks, :]
    return x.reshape(quarter * rows * blocks, x.shape[2])


def gelu_parts(u):
    c0 = math.sqrt(2.0 / math.pi)
    c1 = c0 * 0.044715
    u2 = u * u
    t = jnp.tanh(u * (c0 + c1 * u2))
    half = 0.5 * (1.0 + t)
    z = u * half
    slope = half + u * (half * (1.0 - t)) * (c0 + (3.0 * c1) * u2)
    return z, slope


def mask_rows(seg_ref, length, slots):
    width = length // slots
    qs, ks = [], []
    for s in range(slots):
        row = lax.broadcasted_iota(jnp.int32, (EXTRA, width), 0)
        seg = seg_ref[0, s]
        same = row == seg
        first = row < slots
        qs.append(jnp.where(same | ~first, 0.0, 1.0))
        ks.append(jnp.where(same, -BIG, jnp.where((row >= 4) & (row < 7), 1.0, 0.0)))
    return jnp.concatenate(qs, axis=1), jnp.concatenate(ks, axis=1)


class Links:
    def __init__(self):
        me = lax.axis_index("fsdp")
        x = lax.axis_index("rep")
        c = lax.rem(me, 2)
        y = lax.rem(lax.div(me, 2), 2)
        low = lax.rem(lax.div(me, 4), 2)
        high = lax.div(me, 8)
        self.at = {"c": c, "y": y, "l": low, "h": high, "x": x}
        self.peer = {
            "c": {"fsdp": me + 1 - 2 * c, "rep": x},
            "y": {"fsdp": me + 2 - 4 * y, "rep": x},
            "l": {"fsdp": me + 4 - 8 * low, "rep": x},
            "h": {"fsdp": me + 8 - 16 * high, "rep": x},
            "x": {"fsdp": me, "rep": 1 - x},
        }

    def meet(self, names="cylhx"):
        barrier = pltpu.get_barrier_semaphore()
        for name in names:
            pl.semaphore_signal(barrier, inc=1, device_id=self.peer[name], device_id_type=pl.DeviceIdType.MESH)
        pl.semaphore_wait(barrier, len(names))

    def remote(self, src, dst, sems, who):
        return pltpu.make_async_remote_copy(
            src_ref=src,
            dst_ref=dst,
            send_sem=sems[0],
            recv_sem=sems[1],
            device_id=self.peer[who],
            device_id_type=pl.DeviceIdType.MESH,
        )


class Reduction:
    ORDERS = ("yxlh", "xylh", "lhyx")
    STEPS = 6

    @classmethod
    def paths(cls, rows, subs):
        found, start = [], 0
        for sub in range(subs):
            units = rows // 32 * (sub + 1) // subs - rows // 32 * sub // subs
            third = (units + 2) // 4
            first = (units - third + 1) // 2
            for order, count in zip(cls.ORDERS, (first, units - third - first, third)):
                found.append((order, start, 32 * count))
                start += 32 * count
        return found

    @classmethod
    def scratch(cls, rows, subs, width):
        shapes = []
        for order, _, count in cls.paths(rows, subs):
            free = 3
            for axis in order:
                if axis == "x":
                    count //= 2
                else:
                    free -= 1
                shapes.append(pltpu.VMEM((2,) * free + (count, width), bf16))
        return shapes + [pltpu.SemaphoreType.DMA((15 * subs,)), pltpu.SemaphoreType.DMA((15 * subs,))]

    @staticmethod
    def scratch_count(subs):
        return 12 * subs + 2

    def __init__(self, links, subs, own, core, fin_ref, refs):
        self.links, self.subs, self.own, self.core, self.fin = links, subs, own, core, fin_ref
        self.at = links.at
        self.bufs = [refs[4 * k : 4 + 4 * k] for k in range(3 * subs)]
        self.send_sem, self.recv_sem = refs[-2], refs[-1]
        self.parts = self.paths(own.shape[-2], subs)

    def places(self, path, step):
        order, start, count = self.parts[path]
        fixed = {}
        rows = pl.ds(start, count)
        send = None
        for axis in order[: step + 1]:
            send = (dict(fixed), rows)
            if axis == "x":
                half = count // 2
                send = (dict(fixed), pl.ds(pl.multiple_of(start + (1 - self.at["x"]) * half, 16), half))
                rows = pl.ds(pl.multiple_of(start + self.at["x"] * half, 16), half)
            else:
                send[0][axis] = 1 - self.at[axis]
                fixed[axis] = self.at[axis]
        return send, (fixed, rows)

    def index(self, place, free=()):
        fixed, rows = place
        found, free = [], list(free)
        for axis in "hly":
            found.append(fixed[axis] if axis in fixed else (free.pop(0) if free else slice(None)))
        if self.core is not None:
            found.append(self.core)
        return (*found, rows, slice(None))

    def exchange(self, path, step):
        sems = (self.send_sem.at[5 * path + step], self.recv_sem.at[5 * path + step])
        if step == 4:
            keep = self.places(path, 3)[1]
            return self.links.remote(self.own.at[self.index(keep)], self.fin.at[keep[1], :], sems, "x")
        send, _ = self.places(path, step)
        axis = self.parts[path][0][step]
        return self.links.remote(self.own.at[self.index(send)], self.bufs[path][step], sems, axis)

    def begin(self, path):
        self.exchange(path, 0).start()

    def add(self, place, other):
        free = 3 - len(place[0])

        def one(i, carry):
            bits = [lax.rem(lax.div(i, 2 ** (free - 1 - b)), 2) for b in range(free)]
            where = self.index(place, bits)
            self.own[where] = self.own[where] + other(bits)
            return carry

        if free:
            lax.fori_loop(0, 2**free, one, 0)
        else:
            one(0, 0)

    def advance(self, path, step):
        k = step - 1
        self.exchange(path, k).wait()
        if k == 4:
            return
        place = self.places(path, k)[1]
        buf = self.bufs[path][k]
        self.add(place, lambda bits: buf[(*bits, slice(None), slice(None))])
        self.exchange(path, k + 1).start()
        if k == 3:
            self.fin[place[1], :] = self.own[self.index(place)]

    def run(self, moves):
        for sub, step in moves:
            for path in range(3 * sub, 3 * sub + 3):
                self.advance(path, step)


class Halving:
    def __init__(self, links, grad, refs, half_any):
        self.links, self.grad, self.half = links, grad, half_any
        self.got, self.send_sem, self.recv_sem, self.out_sem = refs
        self.core = links.at["c"]

    @staticmethod
    def scratch(rows, width, regions):
        dma = pltpu.SemaphoreType.DMA
        return [pltpu.VMEM((2, 2, 2, rows, width), bf16), dma((regions,)), dma((regions,)), dma]

    def copy(self, k, where):
        h, l, y, rows = where
        src = self.grad.at[h, l, y, 1 - self.core, rows, :]
        sems = (self.send_sem.at[k], self.recv_sem.at[k])
        return self.links.remote(src, self.got.at[h, l, y, rows, :], sems, "c")

    def send(self, k, where):
        self.copy(k, where).start()

    def settle(self, k, where):
        self.copy(k, where).wait()
        h, l, y, rows = where
        whole = [isinstance(i, slice) for i in (h, l, y)]
        free = sum(whole)

        def one(i, carry):
            bits = [lax.rem(lax.div(i, 2 ** (free - 1 - b)), 2) for b in range(free)]
            at = [bits.pop(0) if w else i for w, i in zip(whole, (h, l, y))]
            mine = (*at, self.core, rows, slice(None))
            self.grad[mine] = self.grad[mine] + self.got[(*at, rows, slice(None))]
            return carry

        lax.fori_loop(0, 2**free, one, 0)
        if self.half is not None:
            pltpu.make_async_copy(
                self.grad.at[h, l, y, self.core, rows, :], self.half.at[h, l, y, rows, :], self.out_sem
            ).start()

    def drain(self):
        if self.half is not None:
            every = slice(None)
            pltpu.make_async_copy(
                self.grad.at[every, every, every, self.core, every, every], self.half, self.out_sem
            ).wait()


def gather_kernel(ident, x_any, out_any, send_sem, recv_sem, own_sem):
    red = Links()
    at = red.at
    rows = x_any.shape[0]
    mine = (at["h"], at["l"], at["y"], at["c"])
    own = pltpu.make_async_copy(x_any, out_any.at[(*mine, slice(None), slice(None))], own_sem)
    own.start()
    own.wait()
    red.meet()

    def copy(path, step):
        order, start, count = path
        order = order[::-1] + "c"
        free = order[:step]
        half = count // 2
        if "x" in free:
            span = pl.ds(start, count)
        else:
            span = pl.ds(pl.multiple_of(start + at["x"] * half, 16), half)
        where = tuple(slice(None) if a in free else at[a] for a in "hlyc") + (span, slice(None))
        sem = 5 * paths.index(path) + step
        return pltpu.make_async_remote_copy(
            src_ref=out_any.at[where],
            dst_ref=out_any.at[where],
            send_sem=send_sem.at[sem],
            recv_sem=recv_sem.at[sem],
            device_id=red.peer[order[step]],
            device_id_type=pl.DeviceIdType.MESH,
        )

    paths = [("xylh", start, count) for _, start, count in Reduction.paths(rows, 1)]
    for path in paths:
        copy(path, 0).start()
    for step in range(5):
        for path in paths:
            copy(path, step).wait()
            if step < 4:
                copy(path, step + 1).start()


def gathered(x, ident):
    rows, width = x.shape
    out = pl.pallas_call(
        functools.partial(gather_kernel, ident),
        name="gather",
        in_specs=[pl.BlockSpec(memory_space=pl.ANY)],
        out_specs=pl.BlockSpec(memory_space=pl.ANY),
        out_shape=sds((2, 2, 2, 2, rows, width), bf16),
        scratch_shapes=[pltpu.SemaphoreType.DMA((15,)), pltpu.SemaphoreType.DMA((15,)), pltpu.SemaphoreType.DMA],
        compiler_params=pltpu.CompilerParams(
            vmem_limit_bytes=8 * 1024 * 1024, collective_id=ident, has_side_effects=True
        ),
        cost_estimate=pl.CostEstimate(flops=0, bytes_accessed=100 << 20, transcendentals=0),
    )(x)
    return out.reshape(PIECES, rows, width)


def attn_forward_kernel(
    tools, h_ref, w_ref, vec_ref, seg_ref,
    g_ref, at_ref, qe_ref, ke_ref, ve_ref, ot_ref, ol_ref,
):
    length, width = h_ref.shape
    hd = width // HEADS
    rows = width // PIECES
    scale = math.log2(math.e) / math.sqrt(hd)
    tools.wait(0)
    x = h_ref[...].astype(f32)
    xh, _ = normalised(x)
    a = (xh * vec_ref[0:1, :] + vec_ref[1:2, :]).astype(bf16)
    at_ref[...] = a.T
    tools.flush(1, ...)
    tools.wait(1)
    q = (mm(a, weight(w_ref, 0, rows)) + vec_ref[2:3, :]).astype(bf16)
    qe_ref[:, 0:hd, :] = q.T.reshape(HEADS, hd, length)
    k = mm(a, weight(w_ref, 1, rows)).astype(bf16)
    ke_ref[:, 0:hd, :] = k.T.reshape(HEADS, hd, length)
    v = (mm(a, weight(w_ref, 2, rows)) + vec_ref[3:4, :]).astype(bf16)
    ve_ref[:, 0:hd, :] = v.T.reshape(HEADS, hd, length)
    mask_q, mask_k = mask_rows(seg_ref, length, seg_ref.shape[1])
    qe_ref[:, hd:, :] = jnp.broadcast_to(mask_q.astype(bf16)[None], (HEADS, EXTRA, length))
    ke_ref[:, hd:, :] = jnp.broadcast_to(mask_k.astype(bf16)[None], (HEADS, EXTRA, length))
    ve_ref[:, hd:, :] = jnp.ones((HEADS, EXTRA, length), bf16)
    tools.flush(3, ...)
    tools.flush(4, ...)
    row = lax.broadcasted_iota(jnp.int32, (EXTRA, length // FORWARD_PARTS), 0)

    part = length // FORWARD_PARTS

    def head(i):
        for t in range(FORWARD_PARTS):
            cols = slice(t * part, (t + 1) * part)
            st = mm_tn(ke_ref[i], qe_ref[i, :, cols])
            peak = jnp.max(st, axis=0, keepdims=True)
            e = jnp.exp2((st - peak) * scale).astype(bf16)
            mix = mm(ve_ref[i], e)
            total = mix[hd : hd + 1, :]
            o = mix[0:hd, :] * (1.0 / total)
            high = o.astype(bf16)
            ot_ref[i, :, cols] = high
            ol_ref[i, :, cols] = (o - high.astype(f32)).astype(bf16)
            lse = -(peak + jnp.log2(total) * (1.0 / scale))
            hi, mid, low = split3(lse)
            ext = jnp.where(row == 6, low.astype(f32), mask_q[:, cols])
            ext = jnp.where(row == 4, hi.astype(f32), jnp.where(row == 5, mid.astype(f32), ext))
            qe_ref[i, hd:, cols] = ext.astype(bf16)
        for k in (2, 5, 6):
            tools.flush(k, i)

    def some_heads(j, carry):
        for k in range(UNROLL):
            head(UNROLL * j + k)
        return carry

    lax.fori_loop(0, HEADS // UNROLL, some_heads, 0)
    g_ref[...] = x + (mm_tn(joined(ot_ref), weight(w_ref, 3, rows)) + vec_ref[4:5, :])
    tools.flush(0, ...)


def full(shape):
    return pl.BlockSpec(shape, lambda: (0,) * len(shape))


ANY = pl.BlockSpec(memory_space=pl.ANY)


class Late:
    def __init__(self, turn, base=0, rows=None):
        self.turn, self.base, self.rows = turn, base, rows


class Tools:
    red = pair = tail = None

    def wait(self, *numbers):
        for i in numbers:
            self.fetch[i].wait()

    def flush(self, k, index):
        pltpu.make_async_copy(self.made[k].at[index], self.out[k].at[index], self.out_sem.at[k]).start()

    def finish(self):
        for k in self.made:
            pltpu.make_async_copy(self.made[k], self.out[k], self.out_sem.at[k]).wait()
        if self.pair is not None:
            self.pair.drain()


def call(kernel, name, args, specs, outs, flops, nbytes, scratch, grads=None, ident=None, carry=None, tail=False):
    args, specs = list(args), list(specs)
    n_args = len(args)
    late = sorted((i for i in range(n_args) if isinstance(specs[i], Late)), key=lambda i: specs[i].turn)
    shapes = {}
    for i in late:
        a = args[i]
        rows = specs[i].rows
        shapes[i] = (a.shape[0], rows) + a.shape[2:] if rows else a.shape
    use = [pltpu.VMEM(shapes[i], args[i].dtype) for i in late] + [pltpu.SemaphoreType.DMA((max(1, len(late)),))]
    use += [pltpu.VMEM(o.shape, o.dtype) for o in outs] + [pltpu.SemaphoreType.DMA((max(1, len(outs)),))]
    results = list(outs)
    out_specs = [ANY] * len(outs)
    if grads is not None:
        rows, width, regions = grads
        six_shape = (2, 2, 2, 2, rows, width)
        use.append(pltpu.VMEM(six_shape, bf16))
        if ident is None:
            use.append(pltpu.SemaphoreType.DMA)
            results.append(sds(six_shape, bf16))
            out_specs.append(ANY)
        else:
            use += Halving.scratch(rows, width, regions)
            if tail:
                use += Reduction.scratch(rows, 1, width)
                results.append(sds((rows, width), bf16))
                out_specs.append(full((rows, width)))
            else:
                results.append(sds((2, 2, 2, rows, width), bf16))
                out_specs.append(ANY)
    if carry is not None:
        held, subs = carry
        crows, cwidth = held.shape[3:]
        args.append(held)
        specs.append(None)
        use += [pltpu.VMEM(held.shape, bf16), pltpu.SemaphoreType.DMA] + Reduction.scratch(crows, subs, cwidth)
        results.append(sds((crows, cwidth), bf16))
        out_specs.append(full((crows, cwidth)))
    n_use = len(use)
    base_specs = [ANY if s is None or isinstance(s, Late) else s for s in specs]

    def body(*refs):
        refs = list(refs)
        ins, refs = refs[: len(args)], refs[len(args) :]
        res, refs = refs[: len(results)], refs[len(results) :]
        used, own_scratch = refs[:n_use], refs[n_use:]
        take = lambda n: [used.pop(0) for _ in range(n)]
        t = Tools()
        buffers, (in_sem,) = take(len(late)), take(1)
        made, (t.out_sem,) = take(len(outs)), take(1)
        t.fetch = {}
        for k, i in enumerate(late):
            src = ins[i]
            if specs[i].rows:
                src = src.at[:, specs[i].base : specs[i].base + specs[i].rows]
            t.fetch[i] = pltpu.make_async_copy(src, buffers[k], in_sem.at[k])
            ins[i] = buffers[k]
        t.made, t.out = dict(enumerate(made)), dict(enumerate(res))
        links = Links() if ident is not None else None
        grad = ()
        after = len(outs)
        if grads is not None:
            (grad_ref,) = take(1)
            grad = (grad_ref,)
            if ident is None:
                t.made[after], t.out[after] = grad_ref, res[after]
                (t.grad_sem,) = take(1)
            else:
                t.pair = Halving(links, grad_ref, take(4), None if tail else res[after])
                if tail:
                    t.tail = Reduction(links, 1, grad_ref, links.at["c"], res[after], take(Reduction.scratch_count(1)))
            after += 1
        if carry is not None:
            own, own_sem = take(2)
            t.red = Reduction(links, subs, own, None, res[after], take(Reduction.scratch_count(subs)))
            load = pltpu.make_async_copy(ins[n_args], own, own_sem)
            load.start()
        for i in late:
            t.fetch[i].start()
        if ident is not None:
            links.meet("cylhx" if carry is not None or tail else "c")
        if carry is not None:
            load.wait()
            for path in range(3 * subs):
                t.red.begin(path)
        kernel(t, *ins[:n_args], *made, *grad, *own_scratch)
        if grads is not None and ident is None:
            k = len(outs)
            pltpu.make_async_copy(t.made[k], t.out[k], t.grad_sem).start()
            pltpu.make_async_copy(t.made[k], t.out[k], t.grad_sem).wait()
            del t.made[k]
        t.finish()

    return pl.pallas_call(
        body,
        name=name,
        in_specs=base_specs,
        out_specs=out_specs,
        out_shape=results,
        scratch_shapes=use + list(scratch),
        compiler_params=pltpu.CompilerParams(
            vmem_limit_bytes=VMEM_BYTES, collective_id=ident, has_side_effects=ident is not None
        ),
        cost_estimate=pl.CostEstimate(flops=flops, bytes_accessed=nbytes, transcendentals=0),
    )(*args)


def advance_at(red, index, plan):
    if red is None:
        return
    for at, moves in plan.items():

        @pl.when(index == at)
        def _(moves=moves):
            red.run(moves)


def sds(shape, dtype):
    return jax.ShapeDtypeStruct(shape, dtype)


SMEM = pltpu.SMEM


def attn_forward(h, square, vec, seg):
    square, base = square
    n, d = h.shape
    hd = d // HEADS
    rows = d // PIECES
    ext = hd + EXTRA
    outs = (
        sds((n, d), f32),
        sds((d, n), bf16),
        sds((HEADS, ext, n), bf16),
        sds((HEADS, ext, n), bf16),
        sds((HEADS, ext, n), bf16),
        sds((HEADS, hd, n), bf16),
        sds((HEADS, hd, n), bf16),
    )
    specs = [Late(0), Late(1, base, 4 * rows), full(vec.shape), pl.BlockSpec(memory_space=SMEM)]
    flops = 8 * n * d * d + 2 * HEADS * 2 * n * n * 256
    return call(attn_forward_kernel, "attn_forward", (h, square, vec, seg), specs, outs, flops, 30 << 20, ())


def ff_forward_kernel(base, g_ref, w_any, vec_ref, h_ref, b_ref, z_ref, s_ref, w_ref, w_sem):
    width = g_ref.shape[1]
    rows = width // PIECES
    blocks = z_ref.shape[1] // width

    @pl.when(pl.program_id(0) == 0)
    def _():
        fetch = window(w_any, w_ref, w_sem, base)
        fetch.start()
        fetch.wait()

    gg = g_ref[...]
    xh, _ = normalised(gg)
    b = (xh * vec_ref[5:6, :] + vec_ref[6:7, :]).astype(bf16)
    b_ref[...] = b
    acc = gg + vec_ref[7:8, :]
    for j in range(blocks):
        w = weight(w_ref, j, rows)
        u = mm(b, w) + vec_ref[8 + j : 9 + j, :]
        z, slope = gelu_parts(u)
        zb = z.astype(bf16)
        z_ref[:, j * width : (j + 1) * width] = zb
        s_ref[:, j * width : (j + 1) * width] = slope.astype(bf16)
        wd = down(w_ref, j, rows, blocks)
        acc = acc + mm(zb, wd)
    h_ref[...] = acc


def ff_forward(g, wide, vec, ff):
    wide, base = wide
    n, d = g.shape
    tile = 256
    outs = (sds((n, d), f32), sds((n, d), bf16), sds((n, ff), bf16), sds((n, ff), bf16))
    row = lambda w: pl.BlockSpec((tile, w), lambda i: (i, 0))
    return pl.pallas_call(
        functools.partial(ff_forward_kernel, base),
        name="ff_forward",
        grid=(n // tile,),
        in_specs=[
            row(d),
            pl.BlockSpec(memory_space=pl.ANY),
            pl.BlockSpec(vec.shape, lambda i: (0, 0)),
        ],
        out_specs=[row(d), row(d), row(ff), row(ff)],
        out_shape=outs,
        scratch_shapes=[pltpu.VMEM((PIECES, 2 * ff // PIECES, d), bf16), pltpu.SemaphoreType.DMA],
        compiler_params=pltpu.CompilerParams(vmem_limit_bytes=VMEM_BYTES),
        cost_estimate=pl.CostEstimate(flops=4 * n * d * ff, bytes_accessed=30 << 20, transcendentals=0),
    )(g, wide, vec)


def put_vectors(grad_ref, base, cols_ref, per):
    pad = grad_ref.shape[4] - base
    lanes = grad_ref.shape[5] // 128
    count = per // lanes
    for m in range(lanes):
        part = cols_ref[pl.ds(m, PIECES * count, stride=lanes), :]
        part = part.reshape(PIECES, count, 128)
        part = jnp.concatenate([part, jnp.zeros((PIECES, pad - count, 128), f32)], axis=1)
        part = part.reshape(2, 2, 2, 2, pad, 128)
        grad_ref[:, :, :, :, base : base + pad, m * 128 : (m + 1) * 128] = part.astype(bf16)


EVERY = slice(None)


def ff_tail(tools, z_ref, du_ref, b_ref, cm_ref, grad_ref, cols_ref, vecs, width, blocks):
    rows = width // PIECES
    quarter = PIECES // blocks
    n = b_ref.shape[0]
    pair = tools.pair
    lower = pl.ds(rows * blocks, rows * blocks)

    def regions(j):
        up = (EVERY, EVERY, EVERY, pl.ds(pl.multiple_of(rows * j, 16), rows))
        return (j, (lax.div(j, 2), lax.rem(j, 2), EVERY, lower)), (blocks + j, up)

    def settle(j):
        if pair is not None:
            for k, where in regions(j):
                pair.settle(k, where)

    def block(j, carry):
        advance_at(tools.red, j, FF_BLOCKS)
        cols = pl.ds(pl.multiple_of(j * width, 128), width)
        (kd, where_d), (ku, where_u) = regions(j)
        dwd = mm_tn(z_ref[:, cols], cm_ref[...]).reshape(2, 2, rows * blocks, width)
        grad_ref[lax.div(j, 2), lax.rem(j, 2), :, :, lower, :] = dwd.astype(bf16)
        if pair is not None:
            pair.send(kd, where_d)
        dwu = mm_tn(b_ref[...], du_ref[:, cols])
        grad_ref[:, :, :, :, where_u[3], :] = dwu.reshape(2, 2, 2, 2, rows, width).astype(bf16)
        if pair is not None:
            pair.send(ku, where_u)

            @pl.when(j > 0)
            def _():
                settle(j - 1)

        return carry

    lax.fori_loop(0, blocks, block, 0)
    ones = jnp.ones((n, 128), bf16)
    vt = jnp.concatenate([*vecs, jnp.zeros((128 - len(vecs), width), f32)], axis=0).T
    vt = vt.reshape(PIECES, rows, 128)
    lane = lax.broadcasted_iota(jnp.int32, (quarter, rows, 128), 2)
    for j in range(blocks):
        part = mm_tn(du_ref[:, j * width : (j + 1) * width], ones)
        part = part.reshape(quarter, blocks, rows, 128)
        piece = vt[quarter * j : quarter * (j + 1)]
        for c in range(blocks):
            piece = jnp.where(lane == len(vecs) + c, part[:, c], piece)
        cols_ref[quarter * rows * j : quarter * rows * (j + 1), :] = piece.reshape(quarter * rows, 128)
    put_vectors(grad_ref, 2 * rows * blocks, cols_ref, rows)
    if pair is not None:
        last = (EVERY, EVERY, EVERY, pl.ds(2 * rows * blocks, 2 * EXTRA))
        pair.send(2 * blocks, last)
        settle(blocks - 1)
        pair.settle(2 * blocks, last)


def ff_last_kernel(
    tools, g_ref, w_ref, vec_ref, cot_ref, live_ref, out_ref, dg_ref, grad_ref, z_ref, du_ref, b_ref, cm_ref, cols_ref,
):
    n, width = g_ref.shape
    rows = width // PIECES
    blocks = z_ref.shape[1] // width
    tile = n // 4
    gain = vec_ref[5:6, :]
    tools.wait(0, 3, 1)

    def step(t, sums):
        sum_gain, sum_bias, sum_down = sums
        span = pl.ds(pl.multiple_of(t * tile, 16), tile)
        gg = g_ref[span, :]
        xh, r = normalised(gg)
        b = (xh * gain + vec_ref[6:7, :]).astype(bf16)
        b_ref[span, :] = b
        grad = cot_ref[span, :].astype(f32) * live_ref[0, t].astype(f32)
        cm = grad.astype(bf16)
        cm_ref[span, :] = cm
        acc = gg + vec_ref[7:8, :]
        db = jnp.zeros((tile, width), f32)
        for j in range(blocks):
            cols = slice(j * width, (j + 1) * width)
            w = weight(w_ref, j, rows)
            wd = down(w_ref, j, rows, blocks)
            u = mm(b, w) + vec_ref[8 + j : 9 + j, :]
            dz = mm_nt(cm, wd)
            z, slope = gelu_parts(u)
            zb = z.astype(bf16)
            z_ref[span, cols] = zb
            acc = acc + mm(zb, wd)
            du = (slope * dz).astype(bf16)
            du_ref[span, cols] = du
            db = db + mm_nt(du, w)
        out_ref[span, :] = acc.astype(bf16)
        dg_ref[span, :] = grad + norm_back(db, xh, r, gain)
        tools.flush(0, (span, EVERY))
        tools.flush(1, (span, EVERY))
        sum_gain = sum_gain + jnp.sum(db * xh, axis=0, keepdims=True)
        sum_bias = sum_bias + jnp.sum(db, axis=0, keepdims=True)
        sum_down = sum_down + jnp.sum(cm.astype(f32), axis=0, keepdims=True)
        return sum_gain, sum_bias, sum_down

    zero = jnp.zeros((1, width), f32)
    sums = lax.fori_loop(0, 4, step, (zero, zero, zero))
    ff_tail(tools, z_ref, du_ref, b_ref, cm_ref, grad_ref, cols_ref, sums, width, blocks)


def ff_last(g, wide, vec, cot, live, ff, ident=None):
    wide, base = wide
    n, d = g.shape
    rows = d // PIECES
    blocks = ff // d
    outs = (sds((n, d), bf16), sds((n, d), f32))
    specs = [Late(0), Late(1, base, 2 * rows * blocks), full(vec.shape), Late(2), pl.BlockSpec(memory_space=SMEM)]
    scratch = [
        pltpu.VMEM((n, ff), bf16), pltpu.VMEM((n, ff), bf16), pltpu.VMEM((n, d), bf16),
        pltpu.VMEM((n, d), bf16), pltpu.VMEM((d, 128), f32),
    ]
    grads = (2 * rows * blocks + 2 * EXTRA, d, 2 * blocks + 1)
    return call(
        ff_last_kernel, "ff_last", (g, wide, vec, cot, live), specs, outs, 12 * n * d * ff, 30 << 20, scratch,
        grads, ident,
    )


def ff_backward_kernel(
    tools, g_ref, w_ref, vec_ref, c_ref, b_ref, z_ref, s_ref, dg_ref, grad_ref, cm_ref, cols_ref,
):
    n, width = g_ref.shape
    rows = width // PIECES
    blocks = z_ref.shape[1] // width
    tile = n // 4
    gain = vec_ref[5:6, :]
    tools.wait(3, 1, 6, 0)

    def step(t, sums):
        advance_at(tools.red, t, FF_TILES)
        sum_gain, sum_bias, sum_down = sums
        span = pl.ds(pl.multiple_of(t * tile, 16), tile)
        xh, r = normalised(g_ref[span, :])
        grad = c_ref[span, :]
        cm = grad.astype(bf16)
        cm_ref[span, :] = cm
        db = jnp.zeros((tile, width), f32)
        for j in range(blocks):
            cols = slice(j * width, (j + 1) * width)
            w = weight(w_ref, j, rows)
            wd = down(w_ref, j, rows, blocks)
            du = (s_ref[span, cols].astype(f32) * mm_nt(cm, wd)).astype(bf16)
            s_ref[span, cols] = du
            db = db + mm_nt(du, w)
        dg_ref[span, :] = grad + norm_back(db, xh, r, gain)
        tools.flush(0, (span, EVERY))
        sum_gain = sum_gain + jnp.sum(db * xh, axis=0, keepdims=True)
        sum_bias = sum_bias + jnp.sum(db, axis=0, keepdims=True)
        sum_down = sum_down + jnp.sum(cm.astype(f32), axis=0, keepdims=True)
        return sum_gain, sum_bias, sum_down

    zero = jnp.zeros((1, width), f32)
    sums = lax.fori_loop(0, 4, step, (zero, zero, zero))
    tools.wait(5, 4)
    ff_tail(tools, z_ref, s_ref, b_ref, cm_ref, grad_ref, cols_ref, sums, width, blocks)
    if tools.red is not None:
        tools.red.run(FF_END)


def ff_backward(g, wide, vec, c, b, z, s, ident=None, carry=None):
    wide, base = wide
    n, d = g.shape
    ff = z.shape[1]
    rows = d // PIECES
    blocks = ff // d
    outs = (sds((n, d), f32),)
    specs = [Late(3), Late(1, base, 2 * rows * blocks), full(vec.shape), Late(0), Late(5), Late(4), Late(2)]
    scratch = [pltpu.VMEM((n, d), bf16), pltpu.VMEM((d, 128), f32)]
    grads = (2 * rows * blocks + 2 * EXTRA, d, 2 * blocks + 1)
    return call(
        ff_backward_kernel, "ff_backward", (g, wide, vec, c, b, z, s), specs, outs, 8 * n * d * ff, 40 << 20, scratch,
        grads, ident, carry,
    )


def attn_backward_kernel(
    tools, h_ref, dg_ref, w_ref, vec_ref, at_ref, qe_ref, ke_ref, ve_ref, ot_ref, ol_ref,
    c_ref, grad_ref, doe_ref, dq_ref, dk_ref, dv_ref, cols_ref,
):
    n, width = h_ref.shape
    hd = width // HEADS
    rows = width // PIECES
    scale = math.log2(math.e) / math.sqrt(hd)
    factor = 1.0 / math.sqrt(hd)
    red, pair, tail = tools.red, tools.pair, tools.tail

    def region(j):
        return (EVERY, EVERY, EVERY, pl.ds(j * rows, rows if j < 4 else 2 * EXTRA))

    def put(j, value):
        grad_ref[:, :, :, :, j * rows : (j + 1) * rows, :] = value.reshape(2, 2, 2, 2, rows, width).astype(bf16)
        if pair is not None:
            pair.send(j, region(j))

    tools.wait(1, 8)
    co = dg_ref[...].astype(bf16)
    put(3, mm(joined(ot_ref), co))
    tools.wait(2)
    dot = mm_nt(weight(w_ref, 3, rows), co).astype(bf16)
    doe_ref[:, 0:hd, :] = dot.reshape(HEADS, hd, n)
    row = lax.broadcasted_iota(jnp.int32, (EXTRA, n), 0)
    tools.wait(5, 6, 7, 9)
    part = n // BACKWARD_PARTS

    def head(i):
        doh = doe_ref[i, 0:hd, :]
        delta = jnp.sum(doh.astype(f32) * (ot_ref[i].astype(f32) + ol_ref[i].astype(f32)), axis=0, keepdims=True)
        hi, mid, low = split3(-delta)
        ext = jnp.where(row == 0, hi.astype(f32), jnp.where(row == 1, mid.astype(f32), jnp.where(row == 2, low.astype(f32), 0.0)))
        doe_ref[i, hd:, :] = ext.astype(bf16)
        dk = dv = None
        for t in range(BACKWARD_PARTS):
            cols = slice(t * part, (t + 1) * part)
            s = mm_tn(qe_ref[i, :, cols], ke_ref[i])
            p = jnp.exp2(s * scale)
            dp = mm_tn(doe_ref[i, :, cols], ve_ref[i])
            ds = (p * dp).astype(bf16)
            dv_t = mm(doe_ref[i, 0:hd, cols], p.astype(bf16))
            dk_t = mm(qe_ref[i, 0:hd, cols], ds)
            dv = dv_t if t == 0 else dv + dv_t
            dk = dk_t if t == 0 else dk + dk_t
            dq_ref[i, :, cols] = (mm_nt(ke_ref[i, 0:hd, :], ds) * factor).astype(bf16)
        dv_ref[i] = dv.astype(bf16)
        dk_ref[i] = (dk * factor).astype(bf16)

    def some_heads(j, carry):
        advance_at(red, j, ATTN_PLAN)
        for k in range(UNROLL):
            head(UNROLL * j + k)
        return carry

    lax.fori_loop(0, HEADS // UNROLL, some_heads, 0)
    tools.wait(4, 0)
    if red is not None:
        red.run(ATTN_MIDDLE)
    if pair is not None:
        pair.settle(3, region(3))
    at = at_ref[...]
    put(0, mm_nt(at, joined(dq_ref)))
    put(1, mm_nt(at, joined(dk_ref)))
    put(2, mm_nt(at, joined(dv_ref)))
    if pair is not None:
        for j in range(3):
            pair.settle(j, region(j))
    if tail is not None:
        tail.begin(0)
        tail.begin(1)
    tile = n // 4

    def norm_tile(t, sums):
        advance_at(red, t, ATTN_TILES)
        sum_gain, sum_bias, sum_out = sums
        span = pl.ds(pl.multiple_of(t * tile, 128), tile)
        dat = mm(weight(w_ref, 0, rows), dq_ref[:, :, span].reshape(width, tile))
        dat = dat + mm(weight(w_ref, 1, rows), dk_ref[:, :, span].reshape(width, tile))
        dat = dat + mm(weight(w_ref, 2, rows), dv_ref[:, :, span].reshape(width, tile))
        da = dat.T
        xh, r = normalised(h_ref[span, :].astype(f32))
        dg = dg_ref[span, :]
        c_ref[span, :] = dg + norm_back(da, xh, r, vec_ref[0:1, :])
        tools.flush(0, (span, EVERY))
        sum_gain = sum_gain + jnp.sum(da * xh, axis=0, keepdims=True)
        sum_bias = sum_bias + jnp.sum(da, axis=0, keepdims=True)
        sum_out = sum_out + jnp.sum(dg.astype(bf16).astype(f32), axis=0, keepdims=True)
        return sum_gain, sum_bias, sum_out

    zero = jnp.zeros((1, width), f32)
    vecs = lax.fori_loop(0, 4, norm_tile, (zero, zero, zero))
    vt = jnp.concatenate([*vecs, jnp.zeros((128 - len(vecs), width), f32)], axis=0).T
    lane = lax.broadcasted_iota(jnp.int32, (width, 128), 1)
    vt = jnp.where(lane == 3, jnp.sum(joined(dq_ref).astype(f32), axis=1, keepdims=True), vt)
    vt = jnp.where(lane == 4, jnp.sum(joined(dv_ref).astype(f32), axis=1, keepdims=True), vt)
    cols_ref[...] = vt
    put_vectors(grad_ref, 4 * rows, cols_ref, rows)
    if pair is not None:
        pair.send(4, region(4))
        pair.settle(4, region(4))
    if tail is not None:
        tail.begin(2)
    if red is not None:
        red.run(ATTN_END)
    if tail is not None:
        for step in range(1, Reduction.STEPS):
            tail.run([(0, step)])


def attn_backward(h, dg, square, vec, kept, ident=None, carry=None, tail=False):
    square, base = square
    n, d = h.shape
    hd = d // HEADS
    rows = d // PIECES
    at, qe, ke, ve, ot, ol = kept
    outs = (sds((n, d), f32),)
    specs = [Late(8), Late(0), Late(2, base, 4 * rows), full(vec.shape), Late(7), Late(3), Late(4), Late(5), Late(1), Late(6)]
    scratch = [pltpu.VMEM((HEADS, hd + EXTRA, n), bf16)] + [pltpu.VMEM((HEADS, hd, n), bf16)] * 3
    scratch += [pltpu.VMEM((d, 128), f32)]
    flops = 16 * n * d * d + 5 * HEADS * 2 * n * n * 256
    return call(
        attn_backward_kernel, "attn_backward", (h, dg, square, vec, at, qe, ke, ve, ot, ol), specs, outs, flops, 40 << 20,
        scratch, (4 * rows + 2 * EXTRA, d, 5), ident, carry, tail,
    )


NAMES = (
    "ln1_gain", "ln1_bias", "q_weight", "q_bias", "k_weight", "v_weight", "v_bias", "o_weight", "o_bias",
    "ln2_gain", "ln2_bias", "up_weight", "up_bias", "down_weight", "down_bias",
)
ROW_VECTORS = ("ln1_gain", "ln1_bias", "q_bias", "v_bias", "o_bias", "ln2_gain", "ln2_bias", "down_bias")


def gather(x, axis="fsdp"):
    return lax.all_gather(x, axis, axis=0, tiled=True)


def column_blocks(up, d):
    return [up[:, j * d : (j + 1) * d] for j in range(up.shape[1] // d)]


def fetch_even(w, layers, shards):
    d = w["q_weight"].shape[2]
    per = w["q_weight"].shape[1]
    ff = w["up_weight"].shape[2]
    packed = []
    for l in range(layers):
        row = jnp.concatenate([w[x][l] for x in ROW_VECTORS] + [w["up_bias"][l]])
        packed.append(jnp.pad(row, (0, d - row.shape[0]))[None])
    rows = jnp.concatenate(packed + [jnp.zeros((2 * EXTRA - layers, d), bf16)], axis=0)
    square = lambda l: [w[x][l] for x in ("q_weight", "k_weight", "v_weight", "o_weight")]
    wide = lambda l: column_blocks(w["up_weight"][l], d) + [w["down_weight"][l]]
    first = jnp.concatenate(square(0) + [rows], axis=0)
    first = gathered(first, 20)
    rest = wide(0)
    for l in range(1, layers):
        rest = rest + square(l) + wide(l)
    rest = gather(jnp.concatenate(rest, axis=0)).reshape(shards, -1, d)
    flat = first[:, 4 * per : 4 * per + layers, :]
    count = len(ROW_VECTORS)
    vecs = flat[:, :, : count * per].reshape(shards, layers, count, per).transpose(1, 2, 0, 3)
    vecs = vecs.reshape(layers, count, d)
    ups = flat[:, :, count * per : count * per + ff // shards].transpose(1, 0, 2).reshape(layers, ff // d, d)
    vec = jnp.concatenate([vecs, ups], axis=1).astype(f32)
    wides = [(rest, 0)]
    squares = [(first, 0)]
    base = 2 * per * (ff // d)
    for l in range(1, layers):
        squares.append((rest, base))
        wides.append((rest, base + 4 * per))
        base += 4 * per + 2 * per * (ff // d)
    return squares, wides, [vec[l] for l in range(layers)]


def fetch_any(w, layers):
    d = w["q_weight"].shape[2]
    squares, wides, vecs = [], [], []
    for l in range(layers):
        whole = {x: gather(w[x][l]) for x in NAMES}
        cut = lambda x: x.reshape(PIECES, x.shape[0] // PIECES, d)
        squares.append((jnp.concatenate([cut(whole[x]) for x in ("q_weight", "k_weight", "v_weight", "o_weight")], axis=1), 0))
        blocks = [cut(x) for x in column_blocks(whole["up_weight"], d)] + [cut(whole["down_weight"])]
        wides.append((jnp.concatenate(blocks, axis=1), 0))
        rows = [whole[x][None] for x in ROW_VECTORS] + [whole["up_bias"].reshape(-1, d)]
        vecs.append(jnp.concatenate(rows, axis=0).astype(f32))
    return squares, wides, vecs


def over_rep(x):
    size = lax.axis_size("rep")
    if size == 1:
        return x.astype(f32)
    other = lax.ppermute(x, "rep", [(i, (i + 1) % size) for i in range(size)])
    return x.astype(f32) + other.astype(f32)


def restack(grads_square, grads_wide, d, ff):
    per = d // PIECES
    blocks = ff // d
    gs, gw = grads_square, grads_wide
    out = {x: gs[:, j * per : (j + 1) * per].reshape(d, d) for j, x in enumerate(("q_weight", "k_weight", "v_weight", "o_weight"))}
    out["up_weight"] = jnp.concatenate([gw[:, j * per : (j + 1) * per].reshape(d, d) for j in range(blocks)], axis=1)
    out["down_weight"] = gw[:, blocks * per : 2 * blocks * per].reshape(ff, d)
    count = per // (d // 128)
    vs = gs[:, 4 * per : 4 * per + count].reshape(d, 128)
    vw = gw[:, 2 * blocks * per : 2 * blocks * per + count].reshape(PIECES, per, 128)
    for j, x in enumerate(("ln1_gain", "ln1_bias", "o_bias", "q_bias", "v_bias")):
        out[x] = vs[:, j]
    for j, x in enumerate(("ln2_gain", "ln2_bias", "down_bias")):
        out[x] = vw[:, :, j].reshape(d)
    out["up_bias"] = vw[:, :, 3 : 3 + blocks].transpose(0, 2, 1).reshape(ff)
    sums = {}
    for x, g in out.items():
        sums[x] = over_rep(lax.psum_scatter(g, "fsdp", scatter_dimension=0, tiled=True))
    return sums


def finish_kernel(layers, blocks, *refs):
    ins, outs, cols_ref = refs[: 2 * layers], dict(zip(NAMES, refs[2 * layers : -1])), refs[-1]
    per = outs["q_weight"].shape[1]
    width = outs["q_weight"].shape[2]
    lanes = width // 128
    for l in range(layers):
        square, wide = ins[2 * l], ins[2 * l + 1]
        for j, x in enumerate(("q_weight", "k_weight", "v_weight", "o_weight")):
            outs[x][l] = square[j * per : (j + 1) * per, :].astype(f32)
        for j in range(blocks):
            outs["up_weight"][l, :, j * width : (j + 1) * width] = wide[j * per : (j + 1) * per, :].astype(f32)
        outs["down_weight"][l] = wide[blocks * per : 2 * blocks * per, :].astype(f32)
        for ref, base, names in (
            (square, 4 * per, ("ln1_gain", "ln1_bias", "o_bias", "q_bias", "v_bias")),
            (wide, 2 * blocks * per, ("ln2_gain", "ln2_bias", "down_bias")),
        ):
            for m in range(lanes):
                part = ref[base : base + per // lanes, m * 128 : (m + 1) * 128].astype(f32)
                cols_ref[pl.ds(m, per // lanes, stride=lanes), :] = part
            turned = cols_ref[...].T
            for j, x in enumerate(names):
                outs[x][l : l + 1, :] = turned[j : j + 1, :]
            if ref is wide:
                for c in range(blocks):
                    row = turned[len(names) + c : len(names) + c + 1, :]
                    outs["up_bias"][l : l + 1, c * per : (c + 1) * per] = row


def finish(pairs, d, ff):
    layers, per = len(pairs), d // PIECES
    shapes = {x: (layers, per) for x in NAMES}
    for x in ("q_weight", "k_weight", "v_weight", "o_weight"):
        shapes[x] = (layers, per, d)
    shapes["up_weight"], shapes["down_weight"], shapes["up_bias"] = (layers, per, ff), (layers, ff // PIECES, d), (layers, ff // PIECES)
    args = [x for pair in pairs for x in pair]
    return pl.pallas_call(
        functools.partial(finish_kernel, layers, ff // d),
        name="finish",
        in_specs=[full(x.shape) for x in args],
        out_specs=[full(shapes[x]) for x in NAMES],
        out_shape=[sds(shapes[x], f32) for x in NAMES],
        scratch_shapes=[pltpu.VMEM((per, 128), f32)],
        compiler_params=pltpu.CompilerParams(vmem_limit_bytes=VMEM_BYTES),
    )(*args)


def on_device(tokens, segment, live, cotangent, *weights):
    w = dict(zip(NAMES, weights))
    layers, per, d = w["q_weight"].shape
    ff = w["up_weight"].shape[2]
    shards = lax.axis_size("fsdp")
    even = shards == PIECES and lax.axis_size("rep") == 2
    squares, wides, vecs = fetch_even(w, layers, shards) if even else fetch_any(w, layers)
    hidden = tokens
    kept = []
    for l in range(layers - 1):
        g, *saved = attn_forward(hidden, squares[l], vecs[l], segment)
        after, *more = ff_forward(g, wides[l], vecs[l], ff)
        kept.append((hidden, g, saved, more))
        hidden = after
    l = layers - 1
    g, *saved = attn_forward(hidden, squares[l], vecs[l], segment)
    if not even:
        whole = lambda x: x.reshape((PIECES,) + x.shape[4:])
        block_out, grad, gw = ff_last(g, wides[l], vecs[l], cotangent, live, ff)
        grad, gs = attn_backward(hidden, grad, squares[l], vecs[l], saved)
        results = [restack(whole(gs), whole(gw), d, ff)]
        for l in reversed(range(layers - 1)):
            hidden, g, saved, more = kept[l]
            grad, gw = ff_backward(g, wides[l], vecs[l], grad, *more)
            grad, gs = attn_backward(hidden, grad, squares[l], vecs[l], saved)
            results.insert(0, restack(whole(gs), whole(gw), d, ff))
    else:
        block_out, grad, gw = ff_last(g, wides[l], vecs[l], cotangent, live, ff, 1)
        grad, gs, rw = attn_backward(hidden, grad, squares[l], vecs[l], saved, 2 + 2 * l, (gw, 2), l == 0)
        pairs = []
        for l in reversed(range(layers - 1)):
            hidden, g, saved, more = kept[l]
            grad, gw, rs = ff_backward(g, wides[l], vecs[l], grad, *more, ident=3 + 2 * l, carry=(gs, 1))
            pairs.insert(0, (rs, rw))
            grad, gs, rw = attn_backward(hidden, grad, squares[l], vecs[l], saved, 2 + 2 * l, (gw, 2), l == 0)
        pairs.insert(0, (gs, rw))
        return (block_out, grad) + tuple(finish(pairs, d, ff))
    return (block_out, grad) + tuple(jnp.stack([r[x] for r in results]) for x in NAMES)


def solution(mesh):
    tok = P(("fsdp", "rep"), None)
    specs = tuple(P(None, "fsdp", None) if x.endswith("weight") else P(None, "fsdp") for x in NAMES)
    return jax.shard_map(
        on_device,
        mesh=mesh,
        in_specs=(tok, tok, tok, tok) + specs,
        out_specs=(tok, tok) + specs,
        check_vma=False,
    )
```

```python
import functools
import math

import jax
import jax.numpy as jnp
from jax import lax
from jax.experimental import pallas as pl
from jax.experimental.pallas import tpu as pltpu
from jax.sharding import PartitionSpec as P

HEADS = 16
PIECES = 16
EXTRA = 16
EPSILON = 1e-06
BIG = 1e30
bf16 = jnp.bfloat16
f32 = jnp.float32
FORWARD_PARTS = 1
BACKWARD_PARTS = 4
UNROLL = 2
ATTN_PLAN = {2: [(0, 1)], 4: [(1, 1)], 5: [(0, 2)], 6: [(1, 2)], 7: [(0, 3)]}
ATTN_MIDDLE = [(1, 3), (0, 4)]
ATTN_TILES = {0: [(0, 5)], 1: [(1, 4)]}
ATTN_END = [(1, 5)]
FF_TILES = {7: [(0, 1)], 13: [(1, 1), (0, 2)]}
FF_BLOCKS = {1: [(0, 3), (1, 2)], 4: [(0, 4), (1, 3)], 7: [(0, 5), (1, 4)]}
FF_END = [(1, 5)]
VMEM_BYTES = 60 * 1024 * 1024


def mm(a, b):
    return jnp.dot(a, b, preferred_element_type=f32)


def mm_tn(a, b):
    return lax.dot_general(a, b, (((0,), (0,)), ((), ())), preferred_element_type=f32)


def mm_nt(a, b):
    return lax.dot_general(a, b, (((1,), (1,)), ((), ())), preferred_element_type=f32)


def normalised(x):
    mean = jnp.mean(x, axis=-1, keepdims=True)
    centred = x - mean
    var = jnp.mean(centred * centred, axis=-1, keepdims=True)
    r = lax.rsqrt(var + EPSILON)
    return centred * r, r


def norm_back(d, xh, r, gain):
    e = d * gain
    m1 = jnp.mean(e, axis=-1, keepdims=True)
    m2 = jnp.mean(e * xh, axis=-1, keepdims=True)
    return r * (e - m1 - xh * m2)


def split3(x):
    hi = x.astype(bf16)
    rest = x - hi.astype(f32)
    mid = rest.astype(bf16)
    low = (rest - mid.astype(f32)).astype(bf16)
    return hi, mid, low


def joined(ref):
    x = ref[...]
    return x.reshape(x.shape[0] * x.shape[1], x.shape[2])


def weight(ref, index, rows):
    x = ref[:, index * rows : (index + 1) * rows, :]
    return x.reshape(x.shape[0] * rows, x.shape[2])


def window(w_any, w_ref, sem, base):
    return pltpu.make_async_copy(w_any.at[:, base : base + w_ref.shape[1], :], w_ref, sem)


def down(ref, j, rows, blocks):
    quarter = PIECES // blocks
    x = ref[quarter * j : quarter * (j + 1), rows * blocks : 2 * rows * blocks, :]
    return x.reshape(quarter * rows * blocks, x.shape[2])


def gelu_parts(u):
    c0 = math.sqrt(2.0 / math.pi)
    c1 = c0 * 0.044715
    u2 = u * u
    t = jnp.tanh(u * (c0 + c1 * u2))
    half = 0.5 * (1.0 + t)
    z = u * half
    slope = half + u * (half * (1.0 - t)) * (c0 + (3.0 * c1) * u2)
    return z, slope


def mask_rows(seg_ref, length, slots):
    width = length // slots
    qs, ks = [], []
    for s in range(slots):
        row = lax.broadcasted_iota(jnp.int32, (EXTRA, width), 0)
        seg = seg_ref[0, s]
        same = row == seg
        first = row < slots
        qs.append(jnp.where(same | ~first, 0.0, 1.0))
        ks.append(jnp.where(same, -BIG, jnp.where((row >= 4) & (row < 7), 1.0, 0.0)))
    return jnp.concatenate(qs, axis=1), jnp.concatenate(ks, axis=1)


class Links:
    def __init__(self):
        me = lax.axis_index("fsdp")
        x = lax.axis_index("rep")
        c = lax.rem(me, 2)
        y = lax.rem(lax.div(me, 2), 2)
        low = lax.rem(lax.div(me, 4), 2)
        high = lax.div(me, 8)
        self.at = {"c": c, "y": y, "l": low, "h": high, "x": x}
        self.peer = {
            "c": {"fsdp": me + 1 - 2 * c, "rep": x},
            "y": {"fsdp": me + 2 - 4 * y, "rep": x},
            "l": {"fsdp": me + 4 - 8 * low, "rep": x},
            "h": {"fsdp": me + 8 - 16 * high, "rep": x},
            "x": {"fsdp": me, "rep": 1 - x},
        }

    def meet(self, names="cylhx"):
        barrier = pltpu.get_barrier_semaphore()
        for name in names:
            pl.semaphore_signal(barrier, inc=1, device_id=self.peer[name], device_id_type=pl.DeviceIdType.MESH)
        pl.semaphore_wait(barrier, len(names))

    def remote(self, src, dst, sems, who):
        return pltpu.make_async_remote_copy(
            src_ref=src,
            dst_ref=dst,
            send_sem=sems[0],
            recv_sem=sems[1],
            device_id=self.peer[who],
            device_id_type=pl.DeviceIdType.MESH,
        )


class Reduction:
    ORDERS = ("yxlh", "xylh", "lhyx")
    STEPS = 6

    @classmethod
    def paths(cls, rows, subs):
        found, start = [], 0
        for sub in range(subs):
            units = rows // 32 * (sub + 1) // subs - rows // 32 * sub // subs
            third = (units + 2) // 4
            first = (units - third + 1) // 2
            for order, count in zip(cls.ORDERS, (first, units - third - first, third)):
                found.append((order, start, 32 * count))
                start += 32 * count
        return found

    @classmethod
    def scratch(cls, rows, subs, width):
        shapes = []
        for order, _, count in cls.paths(rows, subs):
            free = 3
            for axis in order:
                if axis == "x":
                    count //= 2
                else:
                    free -= 1
                shapes.append(pltpu.VMEM((2,) * free + (count, width), bf16))
        return shapes + [pltpu.SemaphoreType.DMA((15 * subs,)), pltpu.SemaphoreType.DMA((15 * subs,))]

    @staticmethod
    def scratch_count(subs):
        return 12 * subs + 2

    def __init__(self, links, subs, own, core, fin_ref, refs):
        self.links, self.subs, self.own, self.core, self.fin = links, subs, own, core, fin_ref
        self.at = links.at
        self.bufs = [refs[4 * k : 4 + 4 * k] for k in range(3 * subs)]
        self.send_sem, self.recv_sem = refs[-2], refs[-1]
        self.parts = self.paths(own.shape[-2], subs)

    def places(self, path, step):
        order, start, count = self.parts[path]
        fixed = {}
        rows = pl.ds(start, count)
        send = None
        for axis in order[: step + 1]:
            send = (dict(fixed), rows)
            if axis == "x":
                half = count // 2
                send = (dict(fixed), pl.ds(pl.multiple_of(start + (1 - self.at["x"]) * half, 16), half))
                rows = pl.ds(pl.multiple_of(start + self.at["x"] * half, 16), half)
            else:
                send[0][axis] = 1 - self.at[axis]
                fixed[axis] = self.at[axis]
        return send, (fixed, rows)

    def index(self, place, free=()):
        fixed, rows = place
        found, free = [], list(free)
        for axis in "hly":
            found.append(fixed[axis] if axis in fixed else (free.pop(0) if free else slice(None)))
        if self.core is not None:
            found.append(self.core)
        return (*found, rows, slice(None))

    def exchange(self, path, step):
        sems = (self.send_sem.at[5 * path + step], self.recv_sem.at[5 * path + step])
        if step == 4:
            keep = self.places(path, 3)[1]
            return self.links.remote(self.own.at[self.index(keep)], self.fin.at[keep[1], :], sems, "x")
        send, _ = self.places(path, step)
        axis = self.parts[path][0][step]
        return self.links.remote(self.own.at[self.index(send)], self.bufs[path][step], sems, axis)

    def begin(self, path):
        self.exchange(path, 0).start()

    def add(self, place, other):
        free = 3 - len(place[0])

        def one(i, carry):
            bits = [lax.rem(lax.div(i, 2 ** (free - 1 - b)), 2) for b in range(free)]
            where = self.index(place, bits)
            self.own[where] = self.own[where] + other(bits)
            return carry

        if free:
            lax.fori_loop(0, 2**free, one, 0)
        else:
            one(0, 0)

    def advance(self, path, step):
        k = step - 1
        self.exchange(path, k).wait()
        if k == 4:
            return
        place = self.places(path, k)[1]
        buf = self.bufs[path][k]
        self.add(place, lambda bits: buf[(*bits, slice(None), slice(None))])
        self.exchange(path, k + 1).start()
        if k == 3:
            self.fin[place[1], :] = self.own[self.index(place)]

    def run(self, moves):
        for sub, step in moves:
            for path in range(3 * sub, 3 * sub + 3):
                self.advance(path, step)


class Halving:
    def __init__(self, links, grad, refs, half_any):
        self.links, self.grad, self.half = links, grad, half_any
        self.got, self.send_sem, self.recv_sem, self.out_sem = refs
        self.core = links.at["c"]

    @staticmethod
    def scratch(rows, width, regions):
        dma = pltpu.SemaphoreType.DMA
        return [pltpu.VMEM((2, 2, 2, rows, width), bf16), dma((regions,)), dma((regions,)), dma]

    def copy(self, k, where):
        h, l, y, rows = where
        src = self.grad.at[h, l, y, 1 - self.core, rows, :]
        sems = (self.send_sem.at[k], self.recv_sem.at[k])
        return self.links.remote(src, self.got.at[h, l, y, rows, :], sems, "c")

    def send(self, k, where):
        self.copy(k, where).start()

    def settle(self, k, where):
        self.copy(k, where).wait()
        h, l, y, rows = where
        whole = [isinstance(i, slice) for i in (h, l, y)]
        free = sum(whole)

        def one(i, carry):
            bits = [lax.rem(lax.div(i, 2 ** (free - 1 - b)), 2) for b in range(free)]
            at = [bits.pop(0) if w else i for w, i in zip(whole, (h, l, y))]
            mine = (*at, self.core, rows, slice(None))
            self.grad[mine] = self.grad[mine] + self.got[(*at, rows, slice(None))]
            return carry

        lax.fori_loop(0, 2**free, one, 0)
        if self.half is not None:
            pltpu.make_async_copy(
                self.grad.at[h, l, y, self.core, rows, :], self.half.at[h, l, y, rows, :], self.out_sem
            ).start()

    def drain(self):
        if self.half is not None:
            every = slice(None)
            pltpu.make_async_copy(
                self.grad.at[every, every, every, self.core, every, every], self.half, self.out_sem
            ).wait()


def gather_kernel(x_ref, out_ref, send_sem, recv_sem):
    red = Links()
    at = red.at
    rows = x_ref.shape[0]
    mine = (at["h"], at["l"], at["y"], at["c"])
    out_ref[(*mine, slice(None), slice(None))] = x_ref[...]
    red.meet()

    def copy(path, step):
        order, start, count = path
        order = order[::-1] + "c"
        free = order[:step]
        half = count // 2
        if "x" in free:
            span = pl.ds(start, count)
        else:
            span = pl.ds(pl.multiple_of(start + at["x"] * half, 16), half)
        where = tuple(slice(None) if a in free else at[a] for a in "hlyc") + (span, slice(None))
        sem = 5 * paths.index(path) + step
        return pltpu.make_async_remote_copy(
            src_ref=out_ref.at[where],
            dst_ref=out_ref.at[where],
            send_sem=send_sem.at[sem],
            recv_sem=recv_sem.at[sem],
            device_id=red.peer[order[step]],
            device_id_type=pl.DeviceIdType.MESH,
        )

    paths = [("xylh", start, count) for _, start, count in Reduction.paths(rows, 1)]
    for path in paths:
        copy(path, 0).start()
    for step in range(5):
        for path in paths:
            copy(path, step).wait()
            if step < 4:
                copy(path, step + 1).start()


def gathered(x, ident):
    rows, width = x.shape
    out = pl.pallas_call(
        gather_kernel,
        name="gather",
        in_specs=[full(x.shape)],
        out_specs=full((2, 2, 2, 2, rows, width)),
        out_shape=sds((2, 2, 2, 2, rows, width), bf16),
        scratch_shapes=[pltpu.SemaphoreType.DMA((15,)), pltpu.SemaphoreType.DMA((15,))],
        compiler_params=pltpu.CompilerParams(
            vmem_limit_bytes=24 * 1024 * 1024, collective_id=ident, has_side_effects=True
        ),
        cost_estimate=pl.CostEstimate(flops=0, bytes_accessed=100 << 20, transcendentals=0),
    )(x)
    return out.reshape(PIECES, rows, width)


def attn_forward_kernel(
    tools, h_ref, wa_ref, wb_ref, vec_ref, seg_ref,
    g_ref, at_ref, qe_ref, ke_ref, ve_ref, ot_ref, ol_ref,
):
    length, width = h_ref.shape
    hd = width // HEADS
    rows = width // PIECES
    scale = math.log2(math.e) / math.sqrt(hd)
    tools.wait(0)
    x = h_ref[...].astype(f32)
    xh, _ = normalised(x)
    a = (xh * vec_ref[0:1, :] + vec_ref[1:2, :]).astype(bf16)
    at_ref[...] = a.T
    tools.flush(1, ...)
    tools.wait(1, 2)
    q = (mm(a, weight(wa_ref, 0, rows)) + vec_ref[2:3, :]).astype(bf16)
    qe_ref[:, 0:hd, :] = q.T.reshape(HEADS, hd, length)
    k = mm(a, weight(wa_ref, 1, rows)).astype(bf16)
    ke_ref[:, 0:hd, :] = k.T.reshape(HEADS, hd, length)
    v = (mm(a, weight(wb_ref, 0, rows)) + vec_ref[3:4, :]).astype(bf16)
    ve_ref[:, 0:hd, :] = v.T.reshape(HEADS, hd, length)
    mask_q, mask_k = mask_rows(seg_ref, length, seg_ref.shape[1])
    qe_ref[:, hd:, :] = jnp.broadcast_to(mask_q.astype(bf16)[None], (HEADS, EXTRA, length))
    ke_ref[:, hd:, :] = jnp.broadcast_to(mask_k.astype(bf16)[None], (HEADS, EXTRA, length))
    ve_ref[:, hd:, :] = jnp.ones((HEADS, EXTRA, length), bf16)
    tools.flush(3, ...)
    tools.flush(4, ...)
    row = lax.broadcasted_iota(jnp.int32, (EXTRA, length // FORWARD_PARTS), 0)

    part = length // FORWARD_PARTS

    def head(i):
        for t in range(FORWARD_PARTS):
            cols = slice(t * part, (t + 1) * part)
            st = mm_tn(ke_ref[i], qe_ref[i, :, cols])
            peak = jnp.max(st, axis=0, keepdims=True)
            e = jnp.exp2((st - peak) * scale).astype(bf16)
            mix = mm(ve_ref[i], e)
            total = mix[hd : hd + 1, :]
            o = mix[0:hd, :] * (1.0 / total)
            high = o.astype(bf16)
            ot_ref[i, :, cols] = high
            ol_ref[i, :, cols] = (o - high.astype(f32)).astype(bf16)
            lse = -(peak + jnp.log2(total) * (1.0 / scale))
            hi, mid, low = split3(lse)
            ext = jnp.where(row == 6, low.astype(f32), mask_q[:, cols])
            ext = jnp.where(row == 4, hi.astype(f32), jnp.where(row == 5, mid.astype(f32), ext))
            qe_ref[i, hd:, cols] = ext.astype(bf16)
        for k in (2, 5, 6):
            tools.flush(k, i)

    def some_heads(j, carry):
        for k in range(UNROLL):
            head(UNROLL * j + k)
        return carry

    lax.fori_loop(0, HEADS // UNROLL, some_heads, 0)
    g_ref[...] = x + (mm_tn(joined(ot_ref), weight(wb_ref, 1, rows)) + vec_ref[4:5, :])
    tools.flush(0, ...)


def full(shape):
    return pl.BlockSpec(shape, lambda: (0,) * len(shape))


ANY = pl.BlockSpec(memory_space=pl.ANY)


class Late:
    def __init__(self, turn, base=0, rows=None):
        self.turn, self.base, self.rows = turn, base, rows


class Tools:
    red = pair = tail = None

    def wait(self, *numbers):
        for i in numbers:
            self.fetch[i].wait()

    def flush(self, k, index):
        pltpu.make_async_copy(self.made[k].at[index], self.out[k].at[index], self.out_sem.at[k]).start()

    def finish(self):
        for k in self.made:
            pltpu.make_async_copy(self.made[k], self.out[k], self.out_sem.at[k]).wait()
        if self.pair is not None:
            self.pair.drain()


def call(kernel, name, args, specs, outs, flops, nbytes, scratch, grads=None, ident=None, carry=None, tail=False):
    args, specs = list(args), list(specs)
    n_args = len(args)
    late = sorted((i for i in range(n_args) if isinstance(specs[i], Late)), key=lambda i: specs[i].turn)
    shapes = {}
    for i in late:
        a = args[i]
        rows = specs[i].rows
        shapes[i] = (a.shape[0], rows) + a.shape[2:] if rows else a.shape
    use = [pltpu.VMEM(shapes[i], args[i].dtype) for i in late] + [pltpu.SemaphoreType.DMA((max(1, len(late)),))]
    use += [pltpu.VMEM(o.shape, o.dtype) for o in outs] + [pltpu.SemaphoreType.DMA((max(1, len(outs)),))]
    results = list(outs)
    out_specs = [ANY] * len(outs)
    if grads is not None:
        rows, width, regions = grads
        six_shape = (2, 2, 2, 2, rows, width)
        use.append(pltpu.VMEM(six_shape, bf16))
        if ident is None:
            use.append(pltpu.SemaphoreType.DMA)
            results.append(sds(six_shape, bf16))
            out_specs.append(ANY)
        else:
            use += Halving.scratch(rows, width, regions)
            if tail:
                use += Reduction.scratch(rows, 1, width)
                results.append(sds((rows, width), bf16))
                out_specs.append(full((rows, width)))
            else:
                results.append(sds((2, 2, 2, rows, width), bf16))
                out_specs.append(ANY)
    if carry is not None:
        held, subs = carry
        crows, cwidth = held.shape[3:]
        args.append(held)
        specs.append(None)
        use += [pltpu.VMEM(held.shape, bf16), pltpu.SemaphoreType.DMA] + Reduction.scratch(crows, subs, cwidth)
        results.append(sds((crows, cwidth), bf16))
        out_specs.append(full((crows, cwidth)))
    n_use = len(use)
    base_specs = [ANY if s is None or isinstance(s, Late) else s for s in specs]

    def body(*refs):
        refs = list(refs)
        ins, refs = refs[: len(args)], refs[len(args) :]
        res, refs = refs[: len(results)], refs[len(results) :]
        used, own_scratch = refs[:n_use], refs[n_use:]
        take = lambda n: [used.pop(0) for _ in range(n)]
        t = Tools()
        buffers, (in_sem,) = take(len(late)), take(1)
        made, (t.out_sem,) = take(len(outs)), take(1)
        t.fetch = {}
        for k, i in enumerate(late):
            src = ins[i]
            if specs[i].rows:
                src = src.at[:, specs[i].base : specs[i].base + specs[i].rows]
            t.fetch[i] = pltpu.make_async_copy(src, buffers[k], in_sem.at[k])
            ins[i] = buffers[k]
        t.made, t.out = dict(enumerate(made)), dict(enumerate(res))
        links = Links() if ident is not None else None
        grad = ()
        after = len(outs)
        if grads is not None:
            (grad_ref,) = take(1)
            grad = (grad_ref,)
            if ident is None:
                t.made[after], t.out[after] = grad_ref, res[after]
                (t.grad_sem,) = take(1)
            else:
                t.pair = Halving(links, grad_ref, take(4), None if tail else res[after])
                if tail:
                    t.tail = Reduction(links, 1, grad_ref, links.at["c"], res[after], take(Reduction.scratch_count(1)))
            after += 1
        if carry is not None:
            own, own_sem = take(2)
            t.red = Reduction(links, subs, own, None, res[after], take(Reduction.scratch_count(subs)))
            load = pltpu.make_async_copy(ins[n_args], own, own_sem)
            load.start()
        for i in late:
            t.fetch[i].start()
        if ident is not None:
            links.meet("cylhx" if carry is not None or tail else "c")
        if carry is not None:
            load.wait()
            for path in range(3 * subs):
                t.red.begin(path)
        kernel(t, *ins[:n_args], *made, *grad, *own_scratch)
        if grads is not None and ident is None:
            k = len(outs)
            pltpu.make_async_copy(t.made[k], t.out[k], t.grad_sem).start()
            pltpu.make_async_copy(t.made[k], t.out[k], t.grad_sem).wait()
            del t.made[k]
        t.finish()

    return pl.pallas_call(
        body,
        name=name,
        in_specs=base_specs,
        out_specs=out_specs,
        out_shape=results,
        scratch_shapes=use + list(scratch),
        compiler_params=pltpu.CompilerParams(
            vmem_limit_bytes=VMEM_BYTES, collective_id=ident, has_side_effects=ident is not None
        ),
        cost_estimate=pl.CostEstimate(flops=flops, bytes_accessed=nbytes, transcendentals=0),
    )(*args)


def advance_at(red, index, plan):
    if red is None:
        return
    for at, moves in plan.items():

        @pl.when(index == at)
        def _(moves=moves):
            red.run(moves)


def sds(shape, dtype):
    return jax.ShapeDtypeStruct(shape, dtype)


SMEM = pltpu.SMEM


def attn_forward(h, square, vec, seg):
    (first, base_a), (second, base_b) = square
    n, d = h.shape
    hd = d // HEADS
    rows = d // PIECES
    ext = hd + EXTRA
    outs = (
        sds((n, d), f32),
        sds((d, n), bf16),
        sds((HEADS, ext, n), bf16),
        sds((HEADS, ext, n), bf16),
        sds((HEADS, ext, n), bf16),
        sds((HEADS, hd, n), bf16),
        sds((HEADS, hd, n), bf16),
    )
    specs = [Late(0), Late(1, base_a, 2 * rows), Late(2, base_b, 2 * rows), full(vec.shape), pl.BlockSpec(memory_space=SMEM)]
    flops = 8 * n * d * d + 2 * HEADS * 2 * n * n * 256
    return call(attn_forward_kernel, "attn_forward", (h, first, second, vec, seg), specs, outs, flops, 30 << 20, ())


def ff_forward_kernel(base, g_ref, w_any, vec_ref, h_ref, b_ref, z_ref, s_ref, w_ref, w_sem):
    width = g_ref.shape[1]
    rows = width // PIECES
    blocks = z_ref.shape[1] // width

    @pl.when(pl.program_id(0) == 0)
    def _():
        fetch = window(w_any, w_ref, w_sem, base)
        fetch.start()
        fetch.wait()

    gg = g_ref[...]
    xh, _ = normalised(gg)
    b = (xh * vec_ref[5:6, :] + vec_ref[6:7, :]).astype(bf16)
    b_ref[...] = b
    acc = gg + vec_ref[7:8, :]
    for j in range(blocks):
        w = weight(w_ref, j, rows)
        u = mm(b, w) + vec_ref[8 + j : 9 + j, :]
        z, slope = gelu_parts(u)
        zb = z.astype(bf16)
        z_ref[:, j * width : (j + 1) * width] = zb
        s_ref[:, j * width : (j + 1) * width] = slope.astype(bf16)
        wd = down(w_ref, j, rows, blocks)
        acc = acc + mm(zb, wd)
    h_ref[...] = acc


def ff_forward(g, wide, vec, ff):
    wide, base = wide
    n, d = g.shape
    tile = 256
    outs = (sds((n, d), f32), sds((n, d), bf16), sds((n, ff), bf16), sds((n, ff), bf16))
    row = lambda w: pl.BlockSpec((tile, w), lambda i: (i, 0))
    return pl.pallas_call(
        functools.partial(ff_forward_kernel, base),
        name="ff_forward",
        grid=(n // tile,),
        in_specs=[
            row(d),
            pl.BlockSpec(memory_space=pl.ANY),
            pl.BlockSpec(vec.shape, lambda i: (0, 0)),
        ],
        out_specs=[row(d), row(d), row(ff), row(ff)],
        out_shape=outs,
        scratch_shapes=[pltpu.VMEM((PIECES, 2 * ff // PIECES, d), bf16), pltpu.SemaphoreType.DMA],
        compiler_params=pltpu.CompilerParams(vmem_limit_bytes=VMEM_BYTES),
        cost_estimate=pl.CostEstimate(flops=4 * n * d * ff, bytes_accessed=30 << 20, transcendentals=0),
    )(g, wide, vec)


def put_vectors(grad_ref, base, cols_ref, per):
    pad = grad_ref.shape[4] - base
    lanes = grad_ref.shape[5] // 128
    count = per // lanes
    for m in range(lanes):
        part = cols_ref[pl.ds(m, PIECES * count, stride=lanes), :]
        part = part.reshape(PIECES, count, 128)
        part = jnp.concatenate([part, jnp.zeros((PIECES, pad - count, 128), f32)], axis=1)
        part = part.reshape(2, 2, 2, 2, pad, 128)
        grad_ref[:, :, :, :, base : base + pad, m * 128 : (m + 1) * 128] = part.astype(bf16)


EVERY = slice(None)


def ff_tail(tools, z_ref, du_ref, b_ref, cm_ref, grad_ref, cols_ref, vecs, width, blocks):
    rows = width // PIECES
    quarter = PIECES // blocks
    n = b_ref.shape[0]
    pair = tools.pair
    lower = pl.ds(rows * blocks, rows * blocks)

    def regions(j):
        up = (EVERY, EVERY, EVERY, pl.ds(pl.multiple_of(rows * j, 16), rows))
        return (j, (lax.div(j, 2), lax.rem(j, 2), EVERY, lower)), (blocks + j, up)

    def settle(j):
        if pair is not None:
            for k, where in regions(j):
                pair.settle(k, where)

    def block(j, carry):
        advance_at(tools.red, 2 * j, FF_BLOCKS)
        cols = pl.ds(pl.multiple_of(j * width, 128), width)
        (kd, where_d), (ku, where_u) = regions(j)
        dwd = mm_tn(z_ref[:, cols], cm_ref[...]).reshape(2, 2, rows * blocks, width)
        grad_ref[lax.div(j, 2), lax.rem(j, 2), :, :, lower, :] = dwd.astype(bf16)
        if pair is not None:
            pair.send(kd, where_d)
        advance_at(tools.red, 2 * j + 1, FF_BLOCKS)
        dwu = mm_tn(b_ref[...], du_ref[:, cols])
        grad_ref[:, :, :, :, where_u[3], :] = dwu.reshape(2, 2, 2, 2, rows, width).astype(bf16)
        if pair is not None:
            pair.send(ku, where_u)

            @pl.when(j > 0)
            def _():
                settle(j - 1)

        return carry

    lax.fori_loop(0, blocks, block, 0)
    ones = jnp.ones((n, 128), bf16)
    vt = jnp.concatenate([*vecs, jnp.zeros((128 - len(vecs), width), f32)], axis=0).T
    vt = vt.reshape(PIECES, rows, 128)
    lane = lax.broadcasted_iota(jnp.int32, (quarter, rows, 128), 2)
    for j in range(blocks):
        part = mm_tn(du_ref[:, j * width : (j + 1) * width], ones)
        part = part.reshape(quarter, blocks, rows, 128)
        piece = vt[quarter * j : quarter * (j + 1)]
        for c in range(blocks):
            piece = jnp.where(lane == len(vecs) + c, part[:, c], piece)
        cols_ref[quarter * rows * j : quarter * rows * (j + 1), :] = piece.reshape(quarter * rows, 128)
    put_vectors(grad_ref, 2 * rows * blocks, cols_ref, rows)
    if pair is not None:
        last = (EVERY, EVERY, EVERY, pl.ds(2 * rows * blocks, 2 * EXTRA))
        pair.send(2 * blocks, last)
        settle(blocks - 1)
        pair.settle(2 * blocks, last)


def ff_last_kernel(
    tools, g_ref, w_ref, vec_ref, cot_ref, live_ref, out_ref, dg_ref, grad_ref, z_ref, du_ref, b_ref, cm_ref, cols_ref,
):
    n, width = g_ref.shape
    rows = width // PIECES
    blocks = z_ref.shape[1] // width
    tile = n // 4
    gain = vec_ref[5:6, :]
    tools.wait(0, 3, 1)

    def step(t, sums):
        sum_gain, sum_bias, sum_down = sums
        span = pl.ds(pl.multiple_of(t * tile, 16), tile)
        gg = g_ref[span, :]
        xh, r = normalised(gg)
        b = (xh * gain + vec_ref[6:7, :]).astype(bf16)
        b_ref[span, :] = b
        grad = cot_ref[span, :].astype(f32) * live_ref[0, t].astype(f32)
        cm = grad.astype(bf16)
        cm_ref[span, :] = cm
        acc = gg + vec_ref[7:8, :]
        db = jnp.zeros((tile, width), f32)
        for j in range(blocks):
            cols = slice(j * width, (j + 1) * width)
            w = weight(w_ref, j, rows)
            wd = down(w_ref, j, rows, blocks)
            u = mm(b, w) + vec_ref[8 + j : 9 + j, :]
            dz = mm_nt(cm, wd)
            z, slope = gelu_parts(u)
            zb = z.astype(bf16)
            z_ref[span, cols] = zb
            acc = acc + mm(zb, wd)
            du = (slope * dz).astype(bf16)
            du_ref[span, cols] = du
            db = db + mm_nt(du, w)
        out_ref[span, :] = acc.astype(bf16)
        dg_ref[span, :] = grad + norm_back(db, xh, r, gain)
        tools.flush(0, (span, EVERY))
        tools.flush(1, (span, EVERY))
        sum_gain = sum_gain + jnp.sum(db * xh, axis=0, keepdims=True)
        sum_bias = sum_bias + jnp.sum(db, axis=0, keepdims=True)
        sum_down = sum_down + jnp.sum(cm.astype(f32), axis=0, keepdims=True)
        return sum_gain, sum_bias, sum_down

    zero = jnp.zeros((1, width), f32)
    sums = lax.fori_loop(0, 4, step, (zero, zero, zero))
    ff_tail(tools, z_ref, du_ref, b_ref, cm_ref, grad_ref, cols_ref, sums, width, blocks)


def ff_last(g, wide, vec, cot, live, ff, ident=None):
    wide, base = wide
    n, d = g.shape
    rows = d // PIECES
    blocks = ff // d
    outs = (sds((n, d), bf16), sds((n, d), f32))
    specs = [Late(0), Late(1, base, 2 * rows * blocks), full(vec.shape), Late(2), pl.BlockSpec(memory_space=SMEM)]
    scratch = [
        pltpu.VMEM((n, ff), bf16), pltpu.VMEM((n, ff), bf16), pltpu.VMEM((n, d), bf16),
        pltpu.VMEM((n, d), bf16), pltpu.VMEM((d, 128), f32),
    ]
    grads = (2 * rows * blocks + 2 * EXTRA, d, 2 * blocks + 1)
    return call(
        ff_last_kernel, "ff_last", (g, wide, vec, cot, live), specs, outs, 12 * n * d * ff, 30 << 20, scratch,
        grads, ident,
    )


def ff_backward_kernel(
    tools, g_ref, w_ref, vec_ref, c_ref, b_ref, z_ref, s_ref, dg_ref, grad_ref, cm_ref, cols_ref,
):
    n, width = g_ref.shape
    rows = width // PIECES
    blocks = z_ref.shape[1] // width
    tile = n // 4
    gain = vec_ref[5:6, :]
    tools.wait(3, 1, 6, 0)

    def step(t, sums):
        sum_gain, sum_bias, sum_down = sums
        span = pl.ds(pl.multiple_of(t * tile, 16), tile)
        xh, r = normalised(g_ref[span, :])
        grad = c_ref[span, :]
        cm = grad.astype(bf16)
        cm_ref[span, :] = cm
        db = jnp.zeros((tile, width), f32)
        for j in range(blocks):
            cols = slice(j * width, (j + 1) * width)
            advance_at(tools.red, t * blocks + j, FF_TILES)
            w = weight(w_ref, j, rows)
            wd = down(w_ref, j, rows, blocks)
            du = (s_ref[span, cols].astype(f32) * mm_nt(cm, wd)).astype(bf16)
            s_ref[span, cols] = du
            db = db + mm_nt(du, w)
        dg_ref[span, :] = grad + norm_back(db, xh, r, gain)
        tools.flush(0, (span, EVERY))
        sum_gain = sum_gain + jnp.sum(db * xh, axis=0, keepdims=True)
        sum_bias = sum_bias + jnp.sum(db, axis=0, keepdims=True)
        sum_down = sum_down + jnp.sum(cm.astype(f32), axis=0, keepdims=True)
        return sum_gain, sum_bias, sum_down

    zero = jnp.zeros((1, width), f32)
    sums = lax.fori_loop(0, 4, step, (zero, zero, zero))
    tools.wait(5, 4)
    ff_tail(tools, z_ref, s_ref, b_ref, cm_ref, grad_ref, cols_ref, sums, width, blocks)
    if tools.red is not None:
        tools.red.run(FF_END)


def ff_backward(g, wide, vec, c, b, z, s, ident=None, carry=None):
    wide, base = wide
    n, d = g.shape
    ff = z.shape[1]
    rows = d // PIECES
    blocks = ff // d
    outs = (sds((n, d), f32),)
    specs = [Late(3), Late(1, base, 2 * rows * blocks), full(vec.shape), Late(0), Late(5), Late(4), Late(2)]
    scratch = [pltpu.VMEM((n, d), bf16), pltpu.VMEM((d, 128), f32)]
    grads = (2 * rows * blocks + 2 * EXTRA, d, 2 * blocks + 1)
    return call(
        ff_backward_kernel, "ff_backward", (g, wide, vec, c, b, z, s), specs, outs, 8 * n * d * ff, 40 << 20, scratch,
        grads, ident, carry,
    )


def attn_backward_kernel(
    tools, h_ref, dg_ref, wa_ref, wb_ref, vec_ref, at_ref, qe_ref, ke_ref, ve_ref, ot_ref, ol_ref,
    c_ref, grad_ref, doe_ref, dq_ref, dk_ref, dv_ref, cols_ref,
):
    n, width = h_ref.shape
    hd = width // HEADS
    rows = width // PIECES
    scale = math.log2(math.e) / math.sqrt(hd)
    factor = 1.0 / math.sqrt(hd)
    red, pair, tail = tools.red, tools.pair, tools.tail

    def region(j):
        return (EVERY, EVERY, EVERY, pl.ds(j * rows, rows if j < 4 else 2 * EXTRA))

    def put(j, value):
        grad_ref[:, :, :, :, j * rows : (j + 1) * rows, :] = value.reshape(2, 2, 2, 2, rows, width).astype(bf16)
        if pair is not None:
            pair.send(j, region(j))

    tools.wait(1, 9)
    co = dg_ref[...].astype(bf16)
    put(3, mm(joined(ot_ref), co))
    tools.wait(3)
    dot = mm_nt(weight(wb_ref, 1, rows), co).astype(bf16)
    doe_ref[:, 0:hd, :] = dot.reshape(HEADS, hd, n)
    row = lax.broadcasted_iota(jnp.int32, (EXTRA, n), 0)
    tools.wait(6, 7, 8, 10)
    part = n // BACKWARD_PARTS

    def head(i):
        doh = doe_ref[i, 0:hd, :]
        delta = jnp.sum(doh.astype(f32) * (ot_ref[i].astype(f32) + ol_ref[i].astype(f32)), axis=0, keepdims=True)
        hi, mid, low = split3(-delta)
        ext = jnp.where(row == 0, hi.astype(f32), jnp.where(row == 1, mid.astype(f32), jnp.where(row == 2, low.astype(f32), 0.0)))
        doe_ref[i, hd:, :] = ext.astype(bf16)
        dk = dv = None
        for t in range(BACKWARD_PARTS):
            cols = slice(t * part, (t + 1) * part)
            s = mm_tn(qe_ref[i, :, cols], ke_ref[i])
            p = jnp.exp2(s * scale)
            dp = mm_tn(doe_ref[i, :, cols], ve_ref[i])
            ds = (p * dp).astype(bf16)
            dv_t = mm(doe_ref[i, 0:hd, cols], p.astype(bf16))
            dk_t = mm(qe_ref[i, 0:hd, cols], ds)
            dv = dv_t if t == 0 else dv + dv_t
            dk = dk_t if t == 0 else dk + dk_t
            dq_ref[i, :, cols] = (mm_nt(ke_ref[i, 0:hd, :], ds) * factor).astype(bf16)
        dv_ref[i] = dv.astype(bf16)
        dk_ref[i] = (dk * factor).astype(bf16)

    def some_heads(j, carry):
        advance_at(red, j, ATTN_PLAN)
        for k in range(UNROLL):
            head(UNROLL * j + k)
        return carry

    lax.fori_loop(0, HEADS // UNROLL, some_heads, 0)
    tools.wait(5, 0, 2)
    if red is not None:
        red.run(ATTN_MIDDLE)
    if pair is not None:
        pair.settle(3, region(3))
    at = at_ref[...]
    put(0, mm_nt(at, joined(dq_ref)))
    put(1, mm_nt(at, joined(dk_ref)))
    put(2, mm_nt(at, joined(dv_ref)))
    if pair is not None:
        for j in range(3):
            pair.settle(j, region(j))
    if tail is not None:
        tail.begin(0)
        tail.begin(1)
    tile = n // 4

    def norm_tile(t, sums):
        advance_at(red, t, ATTN_TILES)
        sum_gain, sum_bias, sum_out = sums
        span = pl.ds(pl.multiple_of(t * tile, 128), tile)
        dat = mm(weight(wa_ref, 0, rows), dq_ref[:, :, span].reshape(width, tile))
        dat = dat + mm(weight(wa_ref, 1, rows), dk_ref[:, :, span].reshape(width, tile))
        dat = dat + mm(weight(wb_ref, 0, rows), dv_ref[:, :, span].reshape(width, tile))
        da = dat.T
        xh, r = normalised(h_ref[span, :].astype(f32))
        dg = dg_ref[span, :]
        c_ref[span, :] = dg + norm_back(da, xh, r, vec_ref[0:1, :])
        tools.flush(0, (span, EVERY))
        sum_gain = sum_gain + jnp.sum(da * xh, axis=0, keepdims=True)
        sum_bias = sum_bias + jnp.sum(da, axis=0, keepdims=True)
        sum_out = sum_out + jnp.sum(dg.astype(bf16).astype(f32), axis=0, keepdims=True)
        return sum_gain, sum_bias, sum_out

    zero = jnp.zeros((1, width), f32)
    vecs = lax.fori_loop(0, 4, norm_tile, (zero, zero, zero))
    vt = jnp.concatenate([*vecs, jnp.zeros((128 - len(vecs), width), f32)], axis=0).T
    lane = lax.broadcasted_iota(jnp.int32, (width, 128), 1)
    vt = jnp.where(lane == 3, jnp.sum(joined(dq_ref).astype(f32), axis=1, keepdims=True), vt)
    vt = jnp.where(lane == 4, jnp.sum(joined(dv_ref).astype(f32), axis=1, keepdims=True), vt)
    cols_ref[...] = vt
    put_vectors(grad_ref, 4 * rows, cols_ref, rows)
    if pair is not None:
        pair.send(4, region(4))
        pair.settle(4, region(4))
    if tail is not None:
        tail.begin(2)
    if red is not None:
        red.run(ATTN_END)
    if tail is not None:
        for step in range(1, Reduction.STEPS):
            tail.run([(0, step)])


def attn_backward(h, dg, square, vec, kept, ident=None, carry=None, tail=False):
    (first, base_a), (second, base_b) = square
    n, d = h.shape
    hd = d // HEADS
    rows = d // PIECES
    at, qe, ke, ve, ot, ol = kept
    outs = (sds((n, d), f32),)
    specs = [Late(8), Late(0), Late(9, base_a, 2 * rows), Late(2, base_b, 2 * rows), full(vec.shape)]
    specs += [Late(7), Late(3), Late(4), Late(5), Late(1), Late(6)]
    scratch = [pltpu.VMEM((HEADS, hd + EXTRA, n), bf16)] + [pltpu.VMEM((HEADS, hd, n), bf16)] * 3
    scratch += [pltpu.VMEM((d, 128), f32)]
    flops = 16 * n * d * d + 5 * HEADS * 2 * n * n * 256
    return call(
        attn_backward_kernel, "attn_backward", (h, dg, first, second, vec, at, qe, ke, ve, ot, ol), specs, outs, flops, 40 << 20,
        scratch, (4 * rows + 2 * EXTRA, d, 5), ident, carry, tail,
    )


NAMES = (
    "ln1_gain", "ln1_bias", "q_weight", "q_bias", "k_weight", "v_weight", "v_bias", "o_weight", "o_bias",
    "ln2_gain", "ln2_bias", "up_weight", "up_bias", "down_weight", "down_bias",
)
ROW_VECTORS = ("ln1_gain", "ln1_bias", "q_bias", "v_bias", "o_bias", "ln2_gain", "ln2_bias", "down_bias")


def gather(x, axis="fsdp"):
    return lax.all_gather(x, axis, axis=0, tiled=True)


def column_blocks(up, d):
    return [up[:, j * d : (j + 1) * d] for j in range(up.shape[1] // d)]


def pack_kernel(first_rows, rest_rows, *refs):
    names = [n for n in NAMES if n.endswith("weight")]
    weights = dict(zip(names, refs))
    vectors = refs[len(names) : len(names) + len(ROW_VECTORS) + 1]
    first, rest, wide_ref, rows_ref, sems = refs[len(names) + len(ROW_VECTORS) + 1 :]
    per, d = vectors[0].shape[1], first.shape[1]
    moves = []
    for target, pieces in ((rest, rest_rows), (first, first_rows)):
        at = 0
        for name, l, column in pieces:
            src = weights[name].at[l]
            if column is not None:
                src = src.at[:, column * d : (column + 1) * d]
            count = src.shape[0]
            copy = pltpu.make_async_copy(src, target.at[at : at + count, :], sems.at[len(moves)])
            copy.start()
            moves.append(copy)
            at += count
    wide_ref[...] = jnp.zeros_like(wide_ref)
    for l in range(vectors[0].shape[0]):
        for k, ref in enumerate(vectors):
            wide_ref[l : l + 1, k * per : k * per + ref.shape[1]] = ref[l : l + 1, :].astype(f32)
    rows_ref[...] = wide_ref[...].astype(bf16)
    copy = pltpu.make_async_copy(rows_ref, first.at[at : at + 2 * EXTRA, :], sems.at[len(moves)])
    copy.start()
    for move in moves + [copy]:
        move.wait()


def fetch_even(w, layers, shards):
    d = w["q_weight"].shape[2]
    per = w["q_weight"].shape[1]
    ff = w["up_weight"].shape[2]
    blocks = ff // d
    square = lambda l, names: [(n + "_weight", l, None) for n in names]
    wide = lambda l: [("up_weight", l, j) for j in range(blocks)] + [("down_weight", l, None)]
    first, rest = square(0, "qkvo"), wide(0)
    for l in range(1, layers):
        first = first + square(l, "qk")
        rest = rest + square(l, "vo") + wide(l)
    tall = 4 * per + 2 * per * (layers - 1)
    long = 2 * per * blocks * layers + 2 * per * (layers - 1)
    names = [n for n in NAMES if n.endswith("weight")]
    vectors = [w[x] for x in (*ROW_VECTORS, "up_bias")]
    first, rest = pl.pallas_call(
        functools.partial(pack_kernel, first, rest),
        name="pack",
        in_specs=[full(w[n].shape) for n in names] + [full(x.shape) for x in vectors],
        out_specs=[ANY, ANY],
        out_shape=[sds((tall + 2 * EXTRA, d), bf16), sds((long, d), bf16)],
        scratch_shapes=[
            pltpu.VMEM((2 * EXTRA, d), f32), pltpu.VMEM((2 * EXTRA, d), bf16),
            pltpu.SemaphoreType.DMA((len(first) + len(rest) + 1,)),
        ],
    )(*(w[n] for n in names), *vectors)
    rest = gather(rest).reshape(shards, -1, d)
    first = gathered(first, 20)
    flat = first[:, tall : tall + layers, :]
    count = len(ROW_VECTORS)
    vecs = flat[:, :, : count * per].reshape(shards, layers, count, per).transpose(1, 2, 0, 3)
    vecs = vecs.reshape(layers, count, d)
    ups = flat[:, :, count * per : count * per + ff // shards].transpose(1, 0, 2).reshape(layers, ff // d, d)
    vec = jnp.concatenate([vecs, ups], axis=1).astype(f32)
    wides = [(rest, 0)]
    squares = [((first, 0), (first, 2 * per))]
    base = 2 * per * blocks
    for l in range(1, layers):
        squares.append(((first, 2 * per * (l + 1)), (rest, base)))
        wides.append((rest, base + 2 * per))
        base += 2 * per + 2 * per * blocks
    return squares, wides, [vec[l] for l in range(layers)]


def fetch_any(w, layers):
    d = w["q_weight"].shape[2]
    squares, wides, vecs = [], [], []
    for l in range(layers):
        whole = {x: gather(w[x][l]) for x in NAMES}
        cut = lambda x: x.reshape(PIECES, x.shape[0] // PIECES, d)
        four = jnp.concatenate([cut(whole[x]) for x in ("q_weight", "k_weight", "v_weight", "o_weight")], axis=1)
        squares.append(((four, 0), (four, 2 * (d // PIECES))))
        blocks = [cut(x) for x in column_blocks(whole["up_weight"], d)] + [cut(whole["down_weight"])]
        wides.append((jnp.concatenate(blocks, axis=1), 0))
        rows = [whole[x][None] for x in ROW_VECTORS] + [whole["up_bias"].reshape(-1, d)]
        vecs.append(jnp.concatenate(rows, axis=0).astype(f32))
    return squares, wides, vecs


def over_rep(x):
    size = lax.axis_size("rep")
    if size == 1:
        return x.astype(f32)
    other = lax.ppermute(x, "rep", [(i, (i + 1) % size) for i in range(size)])
    return x.astype(f32) + other.astype(f32)


def restack(grads_square, grads_wide, d, ff):
    per = d // PIECES
    blocks = ff // d
    gs, gw = grads_square, grads_wide
    out = {x: gs[:, j * per : (j + 1) * per].reshape(d, d) for j, x in enumerate(("q_weight", "k_weight", "v_weight", "o_weight"))}
    out["up_weight"] = jnp.concatenate([gw[:, j * per : (j + 1) * per].reshape(d, d) for j in range(blocks)], axis=1)
    out["down_weight"] = gw[:, blocks * per : 2 * blocks * per].reshape(ff, d)
    count = per // (d // 128)
    vs = gs[:, 4 * per : 4 * per + count].reshape(d, 128)
    vw = gw[:, 2 * blocks * per : 2 * blocks * per + count].reshape(PIECES, per, 128)
    for j, x in enumerate(("ln1_gain", "ln1_bias", "o_bias", "q_bias", "v_bias")):
        out[x] = vs[:, j]
    for j, x in enumerate(("ln2_gain", "ln2_bias", "down_bias")):
        out[x] = vw[:, :, j].reshape(d)
    out["up_bias"] = vw[:, :, 3 : 3 + blocks].transpose(0, 2, 1).reshape(ff)
    sums = {}
    for x, g in out.items():
        sums[x] = over_rep(lax.psum_scatter(g, "fsdp", scatter_dimension=0, tiled=True))
    return sums


def finish_kernel(layers, blocks, *refs):
    given, made, (cols_ref, sems) = refs[: 2 * layers + 2], refs[2 * layers + 2 : -2], refs[-2:]
    ins, outs = given[2:], dict(zip(NAMES, made[2:]))
    moves = [pltpu.make_async_copy(given[k], made[k], sems.at[k]) for k in range(2)]
    for move in moves:
        move.start()
    per = outs["q_weight"].shape[1]
    width = outs["q_weight"].shape[2]
    lanes = width // 128
    for l in range(layers):
        square, wide = ins[2 * l], ins[2 * l + 1]
        for j, x in enumerate(("q_weight", "k_weight", "v_weight", "o_weight")):
            outs[x][l] = square[j * per : (j + 1) * per, :].astype(f32)
        for j in range(blocks):
            outs["up_weight"][l, :, j * width : (j + 1) * width] = wide[j * per : (j + 1) * per, :].astype(f32)
        outs["down_weight"][l] = wide[blocks * per : 2 * blocks * per, :].astype(f32)
        for ref, base, names in (
            (square, 4 * per, ("ln1_gain", "ln1_bias", "o_bias", "q_bias", "v_bias")),
            (wide, 2 * blocks * per, ("ln2_gain", "ln2_bias", "down_bias")),
        ):
            for m in range(lanes):
                part = ref[base : base + per // lanes, m * 128 : (m + 1) * 128].astype(f32)
                cols_ref[pl.ds(m, per // lanes, stride=lanes), :] = part
            turned = cols_ref[...].T
            for j, x in enumerate(names):
                outs[x][l : l + 1, :] = turned[j : j + 1, :]
            if ref is wide:
                for c in range(blocks):
                    row = turned[len(names) + c : len(names) + c + 1, :]
                    outs["up_bias"][l : l + 1, c * per : (c + 1) * per] = row
    for move in moves:
        move.wait()


def finish(block_out, grad, pairs, d, ff):
    layers, per = len(pairs), d // PIECES
    shapes = {x: (layers, per) for x in NAMES}
    for x in ("q_weight", "k_weight", "v_weight", "o_weight"):
        shapes[x] = (layers, per, d)
    shapes["up_weight"], shapes["down_weight"], shapes["up_bias"] = (layers, per, ff), (layers, ff // PIECES, d), (layers, ff // PIECES)
    args = [x for pair in pairs for x in pair]
    return pl.pallas_call(
        functools.partial(finish_kernel, layers, ff // d),
        name="finish",
        in_specs=[full(x.shape) for x in (block_out, grad, *args)],
        out_specs=[ANY, ANY] + [full(shapes[x]) for x in NAMES],
        out_shape=[sds(x.shape, x.dtype) for x in (block_out, grad)] + [sds(shapes[x], f32) for x in NAMES],
        scratch_shapes=[pltpu.VMEM((per, 128), f32), pltpu.SemaphoreType.DMA((2,))],
        compiler_params=pltpu.CompilerParams(vmem_limit_bytes=VMEM_BYTES),
    )(block_out, grad, *args)


def on_device(tokens, segment, live, cotangent, *weights):
    w = dict(zip(NAMES, weights))
    layers, per, d = w["q_weight"].shape
    ff = w["up_weight"].shape[2]
    shards = lax.axis_size("fsdp")
    even = shards == PIECES and lax.axis_size("rep") == 2
    squares, wides, vecs = fetch_even(w, layers, shards) if even else fetch_any(w, layers)
    hidden = tokens
    kept = []
    for l in range(layers - 1):
        g, *saved = attn_forward(hidden, squares[l], vecs[l], segment)
        after, *more = ff_forward(g, wides[l], vecs[l], ff)
        kept.append((hidden, g, saved, more))
        hidden = after
    l = layers - 1
    g, *saved = attn_forward(hidden, squares[l], vecs[l], segment)
    if not even:
        whole = lambda x: x.reshape((PIECES,) + x.shape[4:])
        block_out, grad, gw = ff_last(g, wides[l], vecs[l], cotangent, live, ff)
        grad, gs = attn_backward(hidden, grad, squares[l], vecs[l], saved)
        results = [restack(whole(gs), whole(gw), d, ff)]
        for l in reversed(range(layers - 1)):
            hidden, g, saved, more = kept[l]
            grad, gw = ff_backward(g, wides[l], vecs[l], grad, *more)
            grad, gs = attn_backward(hidden, grad, squares[l], vecs[l], saved)
            results.insert(0, restack(whole(gs), whole(gw), d, ff))
    else:
        block_out, grad, gw = ff_last(g, wides[l], vecs[l], cotangent, live, ff, 1)
        grad, gs, rw = attn_backward(hidden, grad, squares[l], vecs[l], saved, 2 + 2 * l, (gw, 2), l == 0)
        pairs = []
        for l in reversed(range(layers - 1)):
            hidden, g, saved, more = kept[l]
            grad, gw, rs = ff_backward(g, wides[l], vecs[l], grad, *more, ident=3 + 2 * l, carry=(gs, 2))
            pairs.insert(0, (rs, rw))
            grad, gs, rw = attn_backward(hidden, grad, squares[l], vecs[l], saved, 2 + 2 * l, (gw, 2), l == 0)
        pairs.insert(0, (gs, rw))
        return tuple(finish(block_out, grad, pairs, d, ff))
    return (block_out, grad) + tuple(jnp.stack([r[x] for r in results]) for x in NAMES)


def solution(mesh):
    tok = P(("fsdp", "rep"), None)
    specs = tuple(P(None, "fsdp", None) if x.endswith("weight") else P(None, "fsdp") for x in NAMES)
    return jax.shard_map(
        on_device,
        mesh=mesh,
        in_specs=(tok, tok, tok, tok) + specs,
        out_specs=(tok, tok) + specs,
        check_vma=False,
    )
```

```python
import functools
import math

import jax
import jax.numpy as jnp
from jax import lax
from jax.experimental import pallas as pl
from jax.experimental.pallas import tpu as pltpu
from jax.sharding import PartitionSpec as P

HEADS = 16
PIECES = 16
EXTRA = 16
EPSILON = 1e-06
BIG = 1e30
bf16 = jnp.bfloat16
f32 = jnp.float32
FORWARD_PARTS = 1
BACKWARD_PARTS = 4
UNROLL = 2
FORWARD_UNROLL = 4
ATTN_PLAN = {2: [(0, 1)], 4: [(1, 1)], 5: [(0, 2)], 6: [(1, 2)], 7: [(0, 3)]}
ATTN_MIDDLE = [(1, 3), (0, 4)]
ATTN_TILES = {0: [(0, 5)], 1: [(1, 4)]}
ATTN_END = [(1, 5)]
FF_TILES = {7: [(0, 1)], 13: [(1, 1), (0, 2)]}
FF_BLOCKS = {1: [(0, 3), (1, 2)], 4: [(0, 4), (1, 3)], 7: [(0, 5), (1, 4)]}
FF_END = [(1, 5)]
VMEM_BYTES = 60 * 1024 * 1024


def mm(a, b):
    return jnp.dot(a, b, preferred_element_type=f32)


def mm_tn(a, b):
    return lax.dot_general(a, b, (((0,), (0,)), ((), ())), preferred_element_type=f32)


def mm_nt(a, b):
    return lax.dot_general(a, b, (((1,), (1,)), ((), ())), preferred_element_type=f32)


def normalised(x):
    mean = jnp.mean(x, axis=-1, keepdims=True)
    centred = x - mean
    var = jnp.mean(centred * centred, axis=-1, keepdims=True)
    r = lax.rsqrt(var + EPSILON)
    return centred * r, r


def norm_back(d, xh, r, gain):
    e = d * gain
    m1 = jnp.mean(e, axis=-1, keepdims=True)
    m2 = jnp.mean(e * xh, axis=-1, keepdims=True)
    return r * (e - m1 - xh * m2)


def split3(x):
    hi = x.astype(bf16)
    rest = x - hi.astype(f32)
    mid = rest.astype(bf16)
    low = (rest - mid.astype(f32)).astype(bf16)
    return hi, mid, low


def joined(ref):
    x = ref[...]
    return x.reshape(x.shape[0] * x.shape[1], x.shape[2])


def weight(ref, index, rows):
    x = ref[:, index * rows : (index + 1) * rows, :]
    return x.reshape(x.shape[0] * rows, x.shape[2])


def window(w_any, w_ref, sem, base):
    return pltpu.make_async_copy(w_any.at[:, base : base + w_ref.shape[1], :], w_ref, sem)


def down(ref, j, rows, blocks):
    quarter = PIECES // blocks
    x = ref[quarter * j : quarter * (j + 1), rows * blocks : 2 * rows * blocks, :]
    return x.reshape(quarter * rows * blocks, x.shape[2])


def gelu_parts(u):
    c0 = math.sqrt(2.0 / math.pi)
    c1 = c0 * 0.044715
    u2 = u * u
    t = jnp.tanh(u * (c0 + c1 * u2))
    half = 0.5 * (1.0 + t)
    z = u * half
    slope = half + u * (half * (1.0 - t)) * (c0 + (3.0 * c1) * u2)
    return z, slope


def mask_rows(seg_ref, length, slots):
    width = length // slots
    qs, ks = [], []
    for s in range(slots):
        row = lax.broadcasted_iota(jnp.int32, (EXTRA, width), 0)
        seg = seg_ref[0, s]
        same = row == seg
        first = row < slots
        qs.append(jnp.where(same | ~first, 0.0, 1.0))
        ks.append(jnp.where(same, -BIG, jnp.where((row >= 4) & (row < 7), 1.0, 0.0)))
    return jnp.concatenate(qs, axis=1), jnp.concatenate(ks, axis=1)


class Links:
    def __init__(self):
        me = lax.axis_index("fsdp")
        x = lax.axis_index("rep")
        c = lax.rem(me, 2)
        y = lax.rem(lax.div(me, 2), 2)
        low = lax.rem(lax.div(me, 4), 2)
        high = lax.div(me, 8)
        self.at = {"c": c, "y": y, "l": low, "h": high, "x": x}
        self.peer = {
            "c": {"fsdp": me + 1 - 2 * c, "rep": x},
            "y": {"fsdp": me + 2 - 4 * y, "rep": x},
            "l": {"fsdp": me + 4 - 8 * low, "rep": x},
            "h": {"fsdp": me + 8 - 16 * high, "rep": x},
            "x": {"fsdp": me, "rep": 1 - x},
        }

    def meet(self, names="cylhx"):
        barrier = pltpu.get_barrier_semaphore()
        for name in names:
            pl.semaphore_signal(barrier, inc=1, device_id=self.peer[name], device_id_type=pl.DeviceIdType.MESH)
        pl.semaphore_wait(barrier, len(names))

    def remote(self, src, dst, sems, who):
        return pltpu.make_async_remote_copy(
            src_ref=src,
            dst_ref=dst,
            send_sem=sems[0],
            recv_sem=sems[1],
            device_id=self.peer[who],
            device_id_type=pl.DeviceIdType.MESH,
        )


class Reduction:
    ORDERS = ("yxlh", "xylh", "lhyx")
    STEPS = 6

    @classmethod
    def paths(cls, rows, subs):
        found, start = [], 0
        for sub in range(subs):
            units = rows // 32 * (sub + 1) // subs - rows // 32 * sub // subs
            third = (units + 2) // 4
            first = (units - third + 1) // 2
            for order, count in zip(cls.ORDERS, (first, units - third - first, third)):
                found.append((order, start, 32 * count))
                start += 32 * count
        return found

    @classmethod
    def scratch(cls, rows, subs, width):
        shapes = []
        for order, _, count in cls.paths(rows, subs):
            free = 3
            for axis in order:
                if axis == "x":
                    count //= 2
                else:
                    free -= 1
                shapes.append(pltpu.VMEM((2,) * free + (count, width), bf16))
        return shapes + [pltpu.SemaphoreType.DMA((15 * subs,)), pltpu.SemaphoreType.DMA((15 * subs,))]

    @staticmethod
    def scratch_count(subs):
        return 12 * subs + 2

    def __init__(self, links, subs, own, core, fin_ref, refs):
        self.links, self.subs, self.own, self.core, self.fin = links, subs, own, core, fin_ref
        self.at = links.at
        self.bufs = [refs[4 * k : 4 + 4 * k] for k in range(3 * subs)]
        self.send_sem, self.recv_sem = refs[-2], refs[-1]
        self.parts = self.paths(own.shape[-2], subs)

    def places(self, path, step):
        order, start, count = self.parts[path]
        fixed = {}
        rows = pl.ds(start, count)
        send = None
        for axis in order[: step + 1]:
            send = (dict(fixed), rows)
            if axis == "x":
                half = count // 2
                send = (dict(fixed), pl.ds(pl.multiple_of(start + (1 - self.at["x"]) * half, 16), half))
                rows = pl.ds(pl.multiple_of(start + self.at["x"] * half, 16), half)
            else:
                send[0][axis] = 1 - self.at[axis]
                fixed[axis] = self.at[axis]
        return send, (fixed, rows)

    def index(self, place, free=()):
        fixed, rows = place
        found, free = [], list(free)
        for axis in "hly":
            found.append(fixed[axis] if axis in fixed else (free.pop(0) if free else slice(None)))
        if self.core is not None:
            found.append(self.core)
        return (*found, rows, slice(None))

    def exchange(self, path, step):
        sems = (self.send_sem.at[5 * path + step], self.recv_sem.at[5 * path + step])
        if step == 4:
            keep = self.places(path, 3)[1]
            return self.links.remote(self.own.at[self.index(keep)], self.fin.at[keep[1], :], sems, "x")
        send, _ = self.places(path, step)
        axis = self.parts[path][0][step]
        return self.links.remote(self.own.at[self.index(send)], self.bufs[path][step], sems, axis)

    def begin(self, path):
        self.exchange(path, 0).start()

    def add(self, place, other):
        free = 3 - len(place[0])

        def one(i, carry):
            bits = [lax.rem(lax.div(i, 2 ** (free - 1 - b)), 2) for b in range(free)]
            where = self.index(place, bits)
            self.own[where] = self.own[where] + other(bits)
            return carry

        if free:
            lax.fori_loop(0, 2**free, one, 0)
        else:
            one(0, 0)

    def advance(self, path, step):
        k = step - 1
        self.exchange(path, k).wait()
        if k == 4:
            return
        place = self.places(path, k)[1]
        buf = self.bufs[path][k]
        self.add(place, lambda bits: buf[(*bits, slice(None), slice(None))])
        self.exchange(path, k + 1).start()
        if k == 3:
            self.fin[place[1], :] = self.own[self.index(place)]

    def run(self, moves):
        for sub, step in moves:
            for path in range(3 * sub, 3 * sub + 3):
                self.advance(path, step)


class Halving:
    def __init__(self, links, grad, refs, half_any):
        self.links, self.grad, self.half = links, grad, half_any
        self.got, self.send_sem, self.recv_sem, self.out_sem = refs
        self.core = links.at["c"]

    @staticmethod
    def scratch(rows, width, regions):
        dma = pltpu.SemaphoreType.DMA
        return [pltpu.VMEM((2, 2, 2, rows, width), bf16), dma((regions,)), dma((regions,)), dma]

    def copy(self, k, where):
        h, l, y, rows = where
        src = self.grad.at[h, l, y, 1 - self.core, rows, :]
        sems = (self.send_sem.at[k], self.recv_sem.at[k])
        return self.links.remote(src, self.got.at[h, l, y, rows, :], sems, "c")

    def send(self, k, where):
        self.copy(k, where).start()

    def settle(self, k, where):
        self.copy(k, where).wait()
        h, l, y, rows = where
        whole = [isinstance(i, slice) for i in (h, l, y)]
        free = sum(whole)

        def one(i, carry):
            bits = [lax.rem(lax.div(i, 2 ** (free - 1 - b)), 2) for b in range(free)]
            at = [bits.pop(0) if w else i for w, i in zip(whole, (h, l, y))]
            mine = (*at, self.core, rows, slice(None))
            self.grad[mine] = self.grad[mine] + self.got[(*at, rows, slice(None))]
            return carry

        lax.fori_loop(0, 2**free, one, 0)
        if self.half is not None:
            pltpu.make_async_copy(
                self.grad.at[h, l, y, self.core, rows, :], self.half.at[h, l, y, rows, :], self.out_sem
            ).start()

    def drain(self):
        if self.half is not None:
            every = slice(None)
            pltpu.make_async_copy(
                self.grad.at[every, every, every, self.core, every, every], self.half, self.out_sem
            ).wait()


def gather_kernel(x_ref, out_ref, send_sem, recv_sem):
    red = Links()
    at = red.at
    rows = x_ref.shape[0]
    mine = (at["h"], at["l"], at["y"], at["c"])
    out_ref[(*mine, slice(None), slice(None))] = x_ref[...]
    red.meet()

    def copy(path, step):
        order, start, count = path
        order = order[::-1] + "c"
        free = order[:step]
        half = count // 2
        if "x" in free:
            span = pl.ds(start, count)
        else:
            span = pl.ds(pl.multiple_of(start + at["x"] * half, 16), half)
        where = tuple(slice(None) if a in free else at[a] for a in "hlyc") + (span, slice(None))
        sem = 5 * paths.index(path) + step
        return pltpu.make_async_remote_copy(
            src_ref=out_ref.at[where],
            dst_ref=out_ref.at[where],
            send_sem=send_sem.at[sem],
            recv_sem=recv_sem.at[sem],
            device_id=red.peer[order[step]],
            device_id_type=pl.DeviceIdType.MESH,
        )

    paths = [("xylh", start, count) for _, start, count in Reduction.paths(rows, 1)]
    for path in paths:
        copy(path, 0).start()
    for step in range(5):
        for path in paths:
            copy(path, step).wait()
            if step < 4:
                copy(path, step + 1).start()


def gathered(x, ident):
    rows, width = x.shape
    out = pl.pallas_call(
        gather_kernel,
        name="gather",
        in_specs=[full(x.shape)],
        out_specs=full((2, 2, 2, 2, rows, width)),
        out_shape=sds((2, 2, 2, 2, rows, width), bf16),
        scratch_shapes=[pltpu.SemaphoreType.DMA((15,)), pltpu.SemaphoreType.DMA((15,))],
        compiler_params=pltpu.CompilerParams(
            vmem_limit_bytes=24 * 1024 * 1024, collective_id=ident, has_side_effects=True
        ),
        cost_estimate=pl.CostEstimate(flops=0, bytes_accessed=100 << 20, transcendentals=0),
    )(x)
    return out.reshape(PIECES, rows, width)


def attn_forward_kernel(
    tools, h_ref, wa_ref, wb_ref, vec_ref, seg_ref,
    g_ref, at_ref, qe_ref, ke_ref, ve_ref, ot_ref, ol_ref,
):
    length, width = h_ref.shape
    hd = width // HEADS
    rows = width // PIECES
    scale = math.log2(math.e) / math.sqrt(hd)
    tools.wait(0)
    x = h_ref[...].astype(f32)
    xh, _ = normalised(x)
    a = (xh * vec_ref[0:1, :] + vec_ref[1:2, :]).astype(bf16)
    at_ref[...] = a.T
    tools.flush(1, ...)
    tools.wait(1, 2)
    q = (mm(a, weight(wa_ref, 0, rows)) + vec_ref[2:3, :]).astype(bf16)
    qe_ref[:, 0:hd, :] = q.T.reshape(HEADS, hd, length)
    k = mm(a, weight(wa_ref, 1, rows)).astype(bf16)
    ke_ref[:, 0:hd, :] = k.T.reshape(HEADS, hd, length)
    v = (mm(a, weight(wb_ref, 0, rows)) + vec_ref[3:4, :]).astype(bf16)
    ve_ref[:, 0:hd, :] = v.T.reshape(HEADS, hd, length)
    mask_q, mask_k = mask_rows(seg_ref, length, seg_ref.shape[1])
    qe_ref[:, hd:, :] = jnp.broadcast_to(mask_q.astype(bf16)[None], (HEADS, EXTRA, length))
    ke_ref[:, hd:, :] = jnp.broadcast_to(mask_k.astype(bf16)[None], (HEADS, EXTRA, length))
    ve_ref[:, hd:, :] = jnp.ones((HEADS, EXTRA, length), bf16)
    tools.flush(3, ...)
    tools.flush(4, ...)
    row = lax.broadcasted_iota(jnp.int32, (EXTRA, length // FORWARD_PARTS), 0)

    part = length // FORWARD_PARTS

    def head(i):
        for t in range(FORWARD_PARTS):
            cols = slice(t * part, (t + 1) * part)
            st = mm_tn(ke_ref[i], qe_ref[i, :, cols])
            peak = jnp.max(st, axis=0, keepdims=True)
            e = jnp.exp2((st - peak) * scale).astype(bf16)
            mix = mm(ve_ref[i], e)
            total = mix[hd : hd + 1, :]
            o = mix[0:hd, :] * (1.0 / total)
            high = o.astype(bf16)
            ot_ref[i, :, cols] = high
            ol_ref[i, :, cols] = (o - high.astype(f32)).astype(bf16)
            lse = -(peak + jnp.log2(total) * (1.0 / scale))
            hi, mid, low = split3(lse)
            ext = jnp.where(row == 6, low.astype(f32), mask_q[:, cols])
            ext = jnp.where(row == 4, hi.astype(f32), jnp.where(row == 5, mid.astype(f32), ext))
            qe_ref[i, hd:, cols] = ext.astype(bf16)
        for k in (2, 5, 6):
            tools.flush(k, i)

    def some_heads(j, carry):
        for k in range(FORWARD_UNROLL):
            head(FORWARD_UNROLL * j + k)
        return carry

    lax.fori_loop(0, HEADS // FORWARD_UNROLL, some_heads, 0)
    g_ref[...] = x + (mm_tn(joined(ot_ref), weight(wb_ref, 1, rows)) + vec_ref[4:5, :])
    tools.flush(0, ...)


def full(shape):
    return pl.BlockSpec(shape, lambda: (0,) * len(shape))


ANY = pl.BlockSpec(memory_space=pl.ANY)


class Late:
    def __init__(self, turn, base=0, rows=None):
        self.turn, self.base, self.rows = turn, base, rows


class Tools:
    red = pair = tail = None

    def wait(self, *numbers):
        for i in numbers:
            self.fetch[i].wait()

    def flush(self, k, index):
        pltpu.make_async_copy(self.made[k].at[index], self.out[k].at[index], self.out_sem.at[k]).start()

    def finish(self):
        for k in self.made:
            pltpu.make_async_copy(self.made[k], self.out[k], self.out_sem.at[k]).wait()
        if self.pair is not None:
            self.pair.drain()


def call(kernel, name, args, specs, outs, flops, nbytes, scratch, grads=None, ident=None, carry=None, tail=False):
    args, specs = list(args), list(specs)
    n_args = len(args)
    late = sorted((i for i in range(n_args) if isinstance(specs[i], Late)), key=lambda i: specs[i].turn)
    shapes = {}
    for i in late:
        a = args[i]
        rows = specs[i].rows
        shapes[i] = (a.shape[0], rows) + a.shape[2:] if rows else a.shape
    use = [pltpu.VMEM(shapes[i], args[i].dtype) for i in late] + [pltpu.SemaphoreType.DMA((max(1, len(late)),))]
    use += [pltpu.VMEM(o.shape, o.dtype) for o in outs] + [pltpu.SemaphoreType.DMA((max(1, len(outs)),))]
    results = list(outs)
    out_specs = [ANY] * len(outs)
    if grads is not None:
        rows, width, regions = grads
        six_shape = (2, 2, 2, 2, rows, width)
        use.append(pltpu.VMEM(six_shape, bf16))
        if ident is None:
            use.append(pltpu.SemaphoreType.DMA)
            results.append(sds(six_shape, bf16))
            out_specs.append(ANY)
        else:
            use += Halving.scratch(rows, width, regions)
            if tail:
                use += Reduction.scratch(rows, 1, width)
                results.append(sds((rows, width), bf16))
                out_specs.append(full((rows, width)))
            else:
                results.append(sds((2, 2, 2, rows, width), bf16))
                out_specs.append(ANY)
    if carry is not None:
        held, subs = carry
        crows, cwidth = held.shape[3:]
        args.append(held)
        specs.append(None)
        use += [pltpu.VMEM(held.shape, bf16), pltpu.SemaphoreType.DMA] + Reduction.scratch(crows, subs, cwidth)
        results.append(sds((crows, cwidth), bf16))
        out_specs.append(full((crows, cwidth)))
    n_use = len(use)
    base_specs = [ANY if s is None or isinstance(s, Late) else s for s in specs]

    def body(*refs):
        refs = list(refs)
        ins, refs = refs[: len(args)], refs[len(args) :]
        res, refs = refs[: len(results)], refs[len(results) :]
        used, own_scratch = refs[:n_use], refs[n_use:]
        take = lambda n: [used.pop(0) for _ in range(n)]
        t = Tools()
        buffers, (in_sem,) = take(len(late)), take(1)
        made, (t.out_sem,) = take(len(outs)), take(1)
        t.fetch = {}
        for k, i in enumerate(late):
            src = ins[i]
            if specs[i].rows:
                src = src.at[:, specs[i].base : specs[i].base + specs[i].rows]
            t.fetch[i] = pltpu.make_async_copy(src, buffers[k], in_sem.at[k])
            ins[i] = buffers[k]
        t.made, t.out = dict(enumerate(made)), dict(enumerate(res))
        links = Links() if ident is not None else None
        grad = ()
        after = len(outs)
        if grads is not None:
            (grad_ref,) = take(1)
            grad = (grad_ref,)
            if ident is None:
                t.made[after], t.out[after] = grad_ref, res[after]
                (t.grad_sem,) = take(1)
            else:
                t.pair = Halving(links, grad_ref, take(4), None if tail else res[after])
                if tail:
                    t.tail = Reduction(links, 1, grad_ref, links.at["c"], res[after], take(Reduction.scratch_count(1)))
            after += 1
        if carry is not None:
            own, own_sem = take(2)
            t.red = Reduction(links, subs, own, None, res[after], take(Reduction.scratch_count(subs)))
            load = pltpu.make_async_copy(ins[n_args], own, own_sem)
            load.start()
        for i in late:
            t.fetch[i].start()
        if ident is not None:
            links.meet("cylhx" if carry is not None or tail else "c")
        if carry is not None:
            load.wait()
            for path in range(3 * subs):
                t.red.begin(path)
        kernel(t, *ins[:n_args], *made, *grad, *own_scratch)
        if grads is not None and ident is None:
            k = len(outs)
            pltpu.make_async_copy(t.made[k], t.out[k], t.grad_sem).start()
            pltpu.make_async_copy(t.made[k], t.out[k], t.grad_sem).wait()
            del t.made[k]
        t.finish()

    return pl.pallas_call(
        body,
        name=name,
        in_specs=base_specs,
        out_specs=out_specs,
        out_shape=results,
        scratch_shapes=use + list(scratch),
        compiler_params=pltpu.CompilerParams(
            vmem_limit_bytes=VMEM_BYTES, collective_id=ident, has_side_effects=ident is not None
        ),
        cost_estimate=pl.CostEstimate(flops=flops, bytes_accessed=nbytes, transcendentals=0),
    )(*args)


def advance_at(red, index, plan):
    if red is None:
        return
    for at, moves in plan.items():

        @pl.when(index == at)
        def _(moves=moves):
            red.run(moves)


def sds(shape, dtype):
    return jax.ShapeDtypeStruct(shape, dtype)


SMEM = pltpu.SMEM


def attn_forward(h, square, vec, seg):
    (first, base_a), (second, base_b) = square
    n, d = h.shape
    hd = d // HEADS
    rows = d // PIECES
    ext = hd + EXTRA
    outs = (
        sds((n, d), f32),
        sds((d, n), bf16),
        sds((HEADS, ext, n), bf16),
        sds((HEADS, ext, n), bf16),
        sds((HEADS, ext, n), bf16),
        sds((HEADS, hd, n), bf16),
        sds((HEADS, hd, n), bf16),
    )
    specs = [Late(0), Late(1, base_a, 2 * rows), Late(2, base_b, 2 * rows), full(vec.shape), pl.BlockSpec(memory_space=SMEM)]
    flops = 8 * n * d * d + 2 * HEADS * 2 * n * n * 256
    return call(attn_forward_kernel, "attn_forward", (h, first, second, vec, seg), specs, outs, flops, 30 << 20, ())


def ff_forward_kernel(base, g_ref, w_any, vec_ref, h_ref, b_ref, z_ref, s_ref, w_ref, w_sem):
    width = g_ref.shape[1]
    rows = width // PIECES
    blocks = z_ref.shape[1] // width

    @pl.when(pl.program_id(0) == 0)
    def _():
        fetch = window(w_any, w_ref, w_sem, base)
        fetch.start()
        fetch.wait()

    gg = g_ref[...]
    xh, _ = normalised(gg)
    b = (xh * vec_ref[5:6, :] + vec_ref[6:7, :]).astype(bf16)
    b_ref[...] = b
    acc = gg + vec_ref[7:8, :]
    for j in range(blocks):
        w = weight(w_ref, j, rows)
        u = mm(b, w) + vec_ref[8 + j : 9 + j, :]
        z, slope = gelu_parts(u)
        zb = z.astype(bf16)
        z_ref[:, j * width : (j + 1) * width] = zb
        s_ref[:, j * width : (j + 1) * width] = slope.astype(bf16)
        wd = down(w_ref, j, rows, blocks)
        acc = acc + mm(zb, wd)
    h_ref[...] = acc


def ff_forward(g, wide, vec, ff):
    wide, base = wide
    n, d = g.shape
    tile = 256
    outs = (sds((n, d), f32), sds((n, d), bf16), sds((n, ff), bf16), sds((n, ff), bf16))
    row = lambda w: pl.BlockSpec((tile, w), lambda i: (i, 0))
    return pl.pallas_call(
        functools.partial(ff_forward_kernel, base),
        name="ff_forward",
        grid=(n // tile,),
        in_specs=[
            row(d),
            pl.BlockSpec(memory_space=pl.ANY),
            pl.BlockSpec(vec.shape, lambda i: (0, 0)),
        ],
        out_specs=[row(d), row(d), row(ff), row(ff)],
        out_shape=outs,
        scratch_shapes=[pltpu.VMEM((PIECES, 2 * ff // PIECES, d), bf16), pltpu.SemaphoreType.DMA],
        compiler_params=pltpu.CompilerParams(vmem_limit_bytes=VMEM_BYTES),
        cost_estimate=pl.CostEstimate(flops=4 * n * d * ff, bytes_accessed=30 << 20, transcendentals=0),
    )(g, wide, vec)


def put_vectors(grad_ref, base, cols_ref, per):
    pad = grad_ref.shape[4] - base
    lanes = grad_ref.shape[5] // 128
    count = per // lanes
    for m in range(lanes):
        part = cols_ref[pl.ds(m, PIECES * count, stride=lanes), :]
        part = part.reshape(PIECES, count, 128)
        part = jnp.concatenate([part, jnp.zeros((PIECES, pad - count, 128), f32)], axis=1)
        part = part.reshape(2, 2, 2, 2, pad, 128)
        grad_ref[:, :, :, :, base : base + pad, m * 128 : (m + 1) * 128] = part.astype(bf16)


EVERY = slice(None)
ATTN_VECTORS = 5


def ff_tail(tools, z_ref, du_ref, b_ref, cm_ref, grad_ref, cols_ref, number, vecs, width, blocks):
    rows = width // PIECES
    quarter = PIECES // blocks
    n = b_ref.shape[0]
    pair = tools.pair
    lower = pl.ds(rows * blocks, rows * blocks)

    def regions(j):
        up = (EVERY, EVERY, EVERY, pl.ds(pl.multiple_of(rows * j, 16), rows))
        return (j, (lax.div(j, 2), lax.rem(j, 2), EVERY, lower)), (blocks + j, up)

    def settle(j):
        if pair is not None:
            for k, where in regions(j):
                pair.settle(k, where)

    def block(j, carry):
        advance_at(tools.red, 2 * j, FF_BLOCKS)
        cols = pl.ds(pl.multiple_of(j * width, 128), width)
        (kd, where_d), (ku, where_u) = regions(j)
        dwd = mm_tn(z_ref[:, cols], cm_ref[...]).reshape(2, 2, rows * blocks, width)
        grad_ref[lax.div(j, 2), lax.rem(j, 2), :, :, lower, :] = dwd.astype(bf16)
        if pair is not None:
            pair.send(kd, where_d)
        advance_at(tools.red, 2 * j + 1, FF_BLOCKS)
        dwu = mm_tn(b_ref[...], du_ref[:, cols])
        grad_ref[:, :, :, :, where_u[3], :] = dwu.reshape(2, 2, 2, 2, rows, width).astype(bf16)
        if pair is not None:
            pair.send(ku, where_u)

            @pl.when(j > 0)
            def _():
                settle(j - 1)

        return carry

    lax.fori_loop(0, blocks, block, 0)
    ones = jnp.ones((n, 128), bf16)
    first = ATTN_VECTORS
    blank = jnp.zeros((first, width), f32)
    vt = jnp.concatenate([blank, *vecs, jnp.zeros((128 - first - len(vecs), width), f32)], axis=0).T
    vt = vt.reshape(PIECES, rows, 128)
    lane = lax.broadcasted_iota(jnp.int32, (quarter, rows, 128), 2)
    for j in range(blocks):
        part = mm_tn(du_ref[:, j * width : (j + 1) * width], ones)
        part = part.reshape(quarter, blocks, rows, 128)
        piece = vt[quarter * j : quarter * (j + 1)]
        for c in range(blocks):
            piece = jnp.where(lane == first + len(vecs) + c, part[:, c], piece)
        cols_ref[quarter * rows * j : quarter * rows * (j + 1), :] = piece.reshape(quarter * rows, 128)
    tools.flush(number, ...)
    if pair is not None:
        settle(blocks - 1)


def ff_last_kernel(
    tools, g_ref, w_ref, vec_ref, cot_ref, live_ref, out_ref, dg_ref, cols_ref, grad_ref, z_ref, du_ref, b_ref, cm_ref,
):
    n, width = g_ref.shape
    rows = width // PIECES
    blocks = z_ref.shape[1] // width
    tile = n // 4
    gain = vec_ref[5:6, :]
    tools.wait(0, 3, 1)

    def step(t, sums):
        sum_gain, sum_bias, sum_down = sums
        span = pl.ds(pl.multiple_of(t * tile, 16), tile)
        gg = g_ref[span, :]
        xh, r = normalised(gg)
        b = (xh * gain + vec_ref[6:7, :]).astype(bf16)
        b_ref[span, :] = b
        grad = cot_ref[span, :].astype(f32) * live_ref[0, t].astype(f32)
        cm = grad.astype(bf16)
        cm_ref[span, :] = cm
        acc = gg + vec_ref[7:8, :]
        db = jnp.zeros((tile, width), f32)
        for j in range(blocks):
            cols = slice(j * width, (j + 1) * width)
            w = weight(w_ref, j, rows)
            wd = down(w_ref, j, rows, blocks)
            u = mm(b, w) + vec_ref[8 + j : 9 + j, :]
            dz = mm_nt(cm, wd)
            z, slope = gelu_parts(u)
            zb = z.astype(bf16)
            z_ref[span, cols] = zb
            acc = acc + mm(zb, wd)
            du = (slope * dz).astype(bf16)
            du_ref[span, cols] = du
            db = db + mm_nt(du, w)
        out_ref[span, :] = acc.astype(bf16)
        dg_ref[span, :] = grad + norm_back(db, xh, r, gain)
        tools.flush(0, (span, EVERY))
        tools.flush(1, (span, EVERY))
        sum_gain = sum_gain + jnp.sum(db * xh, axis=0, keepdims=True)
        sum_bias = sum_bias + jnp.sum(db, axis=0, keepdims=True)
        sum_down = sum_down + jnp.sum(cm.astype(f32), axis=0, keepdims=True)
        return sum_gain, sum_bias, sum_down

    zero = jnp.zeros((1, width), f32)
    sums = lax.fori_loop(0, 4, step, (zero, zero, zero))
    ff_tail(tools, z_ref, du_ref, b_ref, cm_ref, grad_ref, cols_ref, 2, sums, width, blocks)


def ff_last(g, wide, vec, cot, live, ff, ident=None):
    wide, base = wide
    n, d = g.shape
    rows = d // PIECES
    blocks = ff // d
    outs = (sds((n, d), bf16), sds((n, d), f32), sds((d, 128), f32))
    specs = [Late(0), Late(1, base, 2 * rows * blocks), full(vec.shape), Late(2), pl.BlockSpec(memory_space=SMEM)]
    scratch = [
        pltpu.VMEM((n, ff), bf16), pltpu.VMEM((n, ff), bf16), pltpu.VMEM((n, d), bf16),
        pltpu.VMEM((n, d), bf16),
    ]
    grads = (2 * rows * blocks, d, 2 * blocks)
    return call(
        ff_last_kernel, "ff_last", (g, wide, vec, cot, live), specs, outs, 12 * n * d * ff, 30 << 20, scratch,
        grads, ident,
    )


def ff_backward_kernel(
    tools, g_ref, w_ref, vec_ref, c_ref, b_ref, z_ref, s_ref, dg_ref, cols_ref, grad_ref, cm_ref,
):
    n, width = g_ref.shape
    rows = width // PIECES
    blocks = z_ref.shape[1] // width
    tile = n // 4
    gain = vec_ref[5:6, :]
    tools.wait(3, 1, 6, 0)

    def step(t, sums):
        sum_gain, sum_bias, sum_down = sums
        span = pl.ds(pl.multiple_of(t * tile, 16), tile)
        xh, r = normalised(g_ref[span, :])
        grad = c_ref[span, :]
        cm = grad.astype(bf16)
        cm_ref[span, :] = cm
        db = jnp.zeros((tile, width), f32)
        for j in range(blocks):
            cols = slice(j * width, (j + 1) * width)
            advance_at(tools.red, t * blocks + j, FF_TILES)
            w = weight(w_ref, j, rows)
            wd = down(w_ref, j, rows, blocks)
            du = (s_ref[span, cols].astype(f32) * mm_nt(cm, wd)).astype(bf16)
            s_ref[span, cols] = du
            db = db + mm_nt(du, w)
        dg_ref[span, :] = grad + norm_back(db, xh, r, gain)
        tools.flush(0, (span, EVERY))
        sum_gain = sum_gain + jnp.sum(db * xh, axis=0, keepdims=True)
        sum_bias = sum_bias + jnp.sum(db, axis=0, keepdims=True)
        sum_down = sum_down + jnp.sum(cm.astype(f32), axis=0, keepdims=True)
        return sum_gain, sum_bias, sum_down

    zero = jnp.zeros((1, width), f32)
    sums = lax.fori_loop(0, 4, step, (zero, zero, zero))
    tools.wait(5, 4)
    ff_tail(tools, z_ref, s_ref, b_ref, cm_ref, grad_ref, cols_ref, 1, sums, width, blocks)
    if tools.red is not None:
        tools.red.run(FF_END)


def ff_backward(g, wide, vec, c, b, z, s, ident=None, carry=None):
    wide, base = wide
    n, d = g.shape
    ff = z.shape[1]
    rows = d // PIECES
    blocks = ff // d
    outs = (sds((n, d), f32), sds((d, 128), f32))
    specs = [Late(3), Late(1, base, 2 * rows * blocks), full(vec.shape), Late(0), Late(5), Late(4), Late(2)]
    scratch = [pltpu.VMEM((n, d), bf16)]
    grads = (2 * rows * blocks, d, 2 * blocks)
    return call(
        ff_backward_kernel, "ff_backward", (g, wide, vec, c, b, z, s), specs, outs, 8 * n * d * ff, 40 << 20, scratch,
        grads, ident, carry,
    )


def attn_backward_kernel(
    tools, h_ref, dg_ref, wa_ref, wb_ref, vec_ref, at_ref, qe_ref, ke_ref, ve_ref, ot_ref, ol_ref, extra_ref,
    c_ref, grad_ref, doe_ref, dq_ref, dk_ref, dv_ref, cols_ref,
):
    n, width = h_ref.shape
    hd = width // HEADS
    rows = width // PIECES
    scale = math.log2(math.e) / math.sqrt(hd)
    factor = 1.0 / math.sqrt(hd)
    red, pair, tail = tools.red, tools.pair, tools.tail

    def region(j):
        return (EVERY, EVERY, EVERY, pl.ds(j * rows, rows if j < 4 else 2 * EXTRA))

    def put(j, value):
        grad_ref[:, :, :, :, j * rows : (j + 1) * rows, :] = value.reshape(2, 2, 2, 2, rows, width).astype(bf16)
        if pair is not None:
            pair.send(j, region(j))

    tools.wait(1, 9)
    co = dg_ref[...].astype(bf16)
    put(3, mm(joined(ot_ref), co))
    tools.wait(3)
    dot = mm_nt(weight(wb_ref, 1, rows), co).astype(bf16)
    doe_ref[:, 0:hd, :] = dot.reshape(HEADS, hd, n)
    row = lax.broadcasted_iota(jnp.int32, (EXTRA, n), 0)
    tools.wait(6, 7, 8, 10)
    part = n // BACKWARD_PARTS

    def head(i):
        doh = doe_ref[i, 0:hd, :]
        delta = jnp.sum(doh.astype(f32) * (ot_ref[i].astype(f32) + ol_ref[i].astype(f32)), axis=0, keepdims=True)
        hi, mid, low = split3(-delta)
        ext = jnp.where(row == 0, hi.astype(f32), jnp.where(row == 1, mid.astype(f32), jnp.where(row == 2, low.astype(f32), 0.0)))
        doe_ref[i, hd:, :] = ext.astype(bf16)
        dk = dv = None
        for t in range(BACKWARD_PARTS):
            cols = slice(t * part, (t + 1) * part)
            s = mm_tn(qe_ref[i, :, cols], ke_ref[i])
            p = jnp.exp2(s * scale)
            dp = mm_tn(doe_ref[i, :, cols], ve_ref[i])
            ds = (p * dp).astype(bf16)
            dv_t = mm(doe_ref[i, 0:hd, cols], p.astype(bf16))
            dk_t = mm(qe_ref[i, 0:hd, cols], ds)
            dv = dv_t if t == 0 else dv + dv_t
            dk = dk_t if t == 0 else dk + dk_t
            dq_ref[i, :, cols] = (mm_nt(ke_ref[i, 0:hd, :], ds) * factor).astype(bf16)
        dv_ref[i] = dv.astype(bf16)
        dk_ref[i] = (dk * factor).astype(bf16)

    def some_heads(j, carry):
        advance_at(red, j, ATTN_PLAN)
        for k in range(UNROLL):
            head(UNROLL * j + k)
        return carry

    lax.fori_loop(0, HEADS // UNROLL, some_heads, 0)
    tools.wait(5, 0, 2, 11)
    if red is not None:
        red.run(ATTN_MIDDLE)
    if pair is not None:
        pair.settle(3, region(3))
    at = at_ref[...]
    put(0, mm_nt(at, joined(dq_ref)))
    put(1, mm_nt(at, joined(dk_ref)))
    put(2, mm_nt(at, joined(dv_ref)))
    if pair is not None:
        for j in range(3):
            pair.settle(j, region(j))
    if tail is not None:
        tail.begin(0)
        tail.begin(1)
    tile = n // 4

    def norm_tile(t, sums):
        advance_at(red, t, ATTN_TILES)
        sum_gain, sum_bias, sum_out = sums
        span = pl.ds(pl.multiple_of(t * tile, 128), tile)
        dat = mm(weight(wa_ref, 0, rows), dq_ref[:, :, span].reshape(width, tile))
        dat = dat + mm(weight(wa_ref, 1, rows), dk_ref[:, :, span].reshape(width, tile))
        dat = dat + mm(weight(wb_ref, 0, rows), dv_ref[:, :, span].reshape(width, tile))
        da = dat.T
        xh, r = normalised(h_ref[span, :].astype(f32))
        dg = dg_ref[span, :]
        c_ref[span, :] = dg + norm_back(da, xh, r, vec_ref[0:1, :])
        tools.flush(0, (span, EVERY))
        sum_gain = sum_gain + jnp.sum(da * xh, axis=0, keepdims=True)
        sum_bias = sum_bias + jnp.sum(da, axis=0, keepdims=True)
        sum_out = sum_out + jnp.sum(dg.astype(bf16).astype(f32), axis=0, keepdims=True)
        return sum_gain, sum_bias, sum_out

    zero = jnp.zeros((1, width), f32)
    vecs = lax.fori_loop(0, 4, norm_tile, (zero, zero, zero))
    vt = jnp.concatenate([*vecs, jnp.zeros((128 - len(vecs), width), f32)], axis=0).T
    lane = lax.broadcasted_iota(jnp.int32, (width, 128), 1)
    vt = jnp.where(lane == 3, jnp.sum(joined(dq_ref).astype(f32), axis=1, keepdims=True), vt)
    vt = jnp.where(lane == 4, jnp.sum(joined(dv_ref).astype(f32), axis=1, keepdims=True), vt)
    cols_ref[...] = vt + extra_ref[...]
    put_vectors(grad_ref, 4 * rows, cols_ref, rows)
    if pair is not None:
        pair.send(4, region(4))
        pair.settle(4, region(4))
    if tail is not None:
        tail.begin(2)
    if red is not None:
        red.run(ATTN_END)
    if tail is not None:
        for step in range(1, Reduction.STEPS):
            tail.run([(0, step)])


def attn_backward(h, dg, square, vec, kept, extra, ident=None, carry=None, tail=False):
    (first, base_a), (second, base_b) = square
    n, d = h.shape
    hd = d // HEADS
    rows = d // PIECES
    at, qe, ke, ve, ot, ol = kept
    outs = (sds((n, d), f32),)
    specs = [Late(8), Late(0), Late(9, base_a, 2 * rows), Late(2, base_b, 2 * rows), full(vec.shape)]
    specs += [Late(7), Late(3), Late(4), Late(5), Late(1), Late(6), Late(10)]
    scratch = [pltpu.VMEM((HEADS, hd + EXTRA, n), bf16)] + [pltpu.VMEM((HEADS, hd, n), bf16)] * 3
    scratch += [pltpu.VMEM((d, 128), f32)]
    flops = 16 * n * d * d + 5 * HEADS * 2 * n * n * 256
    return call(
        attn_backward_kernel, "attn_backward", (h, dg, first, second, vec, at, qe, ke, ve, ot, ol, extra), specs, outs, flops, 40 << 20,
        scratch, (4 * rows + 2 * EXTRA, d, 5), ident, carry, tail,
    )


NAMES = (
    "ln1_gain", "ln1_bias", "q_weight", "q_bias", "k_weight", "v_weight", "v_bias", "o_weight", "o_bias",
    "ln2_gain", "ln2_bias", "up_weight", "up_bias", "down_weight", "down_bias",
)
COLUMN_VECTORS = ("ln1_gain", "ln1_bias", "o_bias", "q_bias", "v_bias", "ln2_gain", "ln2_bias", "down_bias")
ROW_VECTORS = ("ln1_gain", "ln1_bias", "q_bias", "v_bias", "o_bias", "ln2_gain", "ln2_bias", "down_bias")


def gather(x, axis="fsdp"):
    return lax.all_gather(x, axis, axis=0, tiled=True)


def column_blocks(up, d):
    return [up[:, j * d : (j + 1) * d] for j in range(up.shape[1] // d)]


def pack_kernel(first_rows, rest_rows, *refs):
    names = [n for n in NAMES if n.endswith("weight")]
    weights = dict(zip(names, refs))
    vectors = refs[len(names) : len(names) + len(ROW_VECTORS) + 1]
    first, rest, wide_ref, rows_ref, sems = refs[len(names) + len(ROW_VECTORS) + 1 :]
    per, d = vectors[0].shape[1], first.shape[1]
    moves = []
    for target, pieces in ((rest, rest_rows), (first, first_rows)):
        at = 0
        for name, l, column in pieces:
            src = weights[name].at[l]
            if column is not None:
                src = src.at[:, column * d : (column + 1) * d]
            count = src.shape[0]
            copy = pltpu.make_async_copy(src, target.at[at : at + count, :], sems.at[len(moves)])
            copy.start()
            moves.append(copy)
            at += count
    wide_ref[...] = jnp.zeros_like(wide_ref)
    for l in range(vectors[0].shape[0]):
        for k, ref in enumerate(vectors):
            wide_ref[l : l + 1, k * per : k * per + ref.shape[1]] = ref[l : l + 1, :].astype(f32)
    rows_ref[...] = wide_ref[...].astype(bf16)
    copy = pltpu.make_async_copy(rows_ref, first.at[at : at + 2 * EXTRA, :], sems.at[len(moves)])
    copy.start()
    for move in moves + [copy]:
        move.wait()


def fetch_even(w, layers, shards):
    d = w["q_weight"].shape[2]
    per = w["q_weight"].shape[1]
    ff = w["up_weight"].shape[2]
    blocks = ff // d
    square = lambda l, names: [(n + "_weight", l, None) for n in names]
    wide = lambda l: [("up_weight", l, j) for j in range(blocks)] + [("down_weight", l, None)]
    first, rest = square(0, "qkvo"), wide(0)
    for l in range(1, layers):
        first = first + square(l, "qk")
        rest = rest + square(l, "vo") + wide(l)
    tall = 4 * per + 2 * per * (layers - 1)
    long = 2 * per * blocks * layers + 2 * per * (layers - 1)
    names = [n for n in NAMES if n.endswith("weight")]
    vectors = [w[x] for x in (*ROW_VECTORS, "up_bias")]
    first, rest = pl.pallas_call(
        functools.partial(pack_kernel, first, rest),
        name="pack",
        in_specs=[full(w[n].shape) for n in names] + [full(x.shape) for x in vectors],
        out_specs=[ANY, ANY],
        out_shape=[sds((tall + 2 * EXTRA, d), bf16), sds((long, d), bf16)],
        scratch_shapes=[
            pltpu.VMEM((2 * EXTRA, d), f32), pltpu.VMEM((2 * EXTRA, d), bf16),
            pltpu.SemaphoreType.DMA((len(first) + len(rest) + 1,)),
        ],
    )(*(w[n] for n in names), *vectors)
    rest = gather(rest).reshape(shards, -1, d)
    first = gathered(first, 20)
    flat = first[:, tall : tall + layers, :]
    count = len(ROW_VECTORS)
    vecs = flat[:, :, : count * per].reshape(shards, layers, count, per).transpose(1, 2, 0, 3)
    vecs = vecs.reshape(layers, count, d)
    ups = flat[:, :, count * per : count * per + ff // shards].transpose(1, 0, 2).reshape(layers, ff // d, d)
    vec = jnp.concatenate([vecs, ups], axis=1).astype(f32)
    wides = [(rest, 0)]
    squares = [((first, 0), (first, 2 * per))]
    base = 2 * per * blocks
    for l in range(1, layers):
        squares.append(((first, 2 * per * (l + 1)), (rest, base)))
        wides.append((rest, base + 2 * per))
        base += 2 * per + 2 * per * blocks
    return squares, wides, [vec[l] for l in range(layers)]


def fetch_any(w, layers):
    d = w["q_weight"].shape[2]
    squares, wides, vecs = [], [], []
    for l in range(layers):
        whole = {x: gather(w[x][l]) for x in NAMES}
        cut = lambda x: x.reshape(PIECES, x.shape[0] // PIECES, d)
        four = jnp.concatenate([cut(whole[x]) for x in ("q_weight", "k_weight", "v_weight", "o_weight")], axis=1)
        squares.append(((four, 0), (four, 2 * (d // PIECES))))
        blocks = [cut(x) for x in column_blocks(whole["up_weight"], d)] + [cut(whole["down_weight"])]
        wides.append((jnp.concatenate(blocks, axis=1), 0))
        rows = [whole[x][None] for x in ROW_VECTORS] + [whole["up_bias"].reshape(-1, d)]
        vecs.append(jnp.concatenate(rows, axis=0).astype(f32))
    return squares, wides, vecs


def over_rep(x):
    size = lax.axis_size("rep")
    if size == 1:
        return x.astype(f32)
    other = lax.ppermute(x, "rep", [(i, (i + 1) % size) for i in range(size)])
    return x.astype(f32) + other.astype(f32)


def restack(grads_square, grads_wide, d, ff):
    per = d // PIECES
    blocks = ff // d
    gs, gw = grads_square, grads_wide
    out = {x: gs[:, j * per : (j + 1) * per].reshape(d, d) for j, x in enumerate(("q_weight", "k_weight", "v_weight", "o_weight"))}
    out["up_weight"] = jnp.concatenate([gw[:, j * per : (j + 1) * per].reshape(d, d) for j in range(blocks)], axis=1)
    out["down_weight"] = gw[:, blocks * per : 2 * blocks * per].reshape(ff, d)
    count = per // (d // 128)
    vs = gs[:, 4 * per : 4 * per + count].reshape(PIECES, per, 128)
    for j, x in enumerate(COLUMN_VECTORS):
        out[x] = vs[:, :, j].reshape(d)
    first = len(COLUMN_VECTORS)
    out["up_bias"] = vs[:, :, first : first + blocks].transpose(0, 2, 1).reshape(ff)
    sums = {}
    for x, g in out.items():
        sums[x] = over_rep(lax.psum_scatter(g, "fsdp", scatter_dimension=0, tiled=True))
    return sums


def finish_kernel(layers, blocks, *refs):
    given, made, (cols_ref, sems) = refs[: 2 * layers + 2], refs[2 * layers + 2 : -2], refs[-2:]
    ins, outs = given[2:], dict(zip(NAMES, made[2:]))
    moves = [pltpu.make_async_copy(given[k], made[k], sems.at[k]) for k in range(2)]
    for move in moves:
        move.start()
    per = outs["q_weight"].shape[1]
    width = outs["q_weight"].shape[2]
    lanes = width // 128
    for l in range(layers):
        square, wide = ins[2 * l], ins[2 * l + 1]
        for j, x in enumerate(("q_weight", "k_weight", "v_weight", "o_weight")):
            outs[x][l] = square[j * per : (j + 1) * per, :].astype(f32)
        for j in range(blocks):
            outs["up_weight"][l, :, j * width : (j + 1) * width] = wide[j * per : (j + 1) * per, :].astype(f32)
        outs["down_weight"][l] = wide[blocks * per : 2 * blocks * per, :].astype(f32)
        for m in range(lanes):
            part = square[4 * per : 4 * per + per // lanes, m * 128 : (m + 1) * 128].astype(f32)
            cols_ref[pl.ds(m, per // lanes, stride=lanes), :] = part
        turned = cols_ref[...].T
        for j, x in enumerate(COLUMN_VECTORS):
            outs[x][l : l + 1, :] = turned[j : j + 1, :]
        for c in range(blocks):
            j = len(COLUMN_VECTORS) + c
            outs["up_bias"][l : l + 1, c * per : (c + 1) * per] = turned[j : j + 1, :]
    for move in moves:
        move.wait()


def finish(block_out, grad, pairs, d, ff):
    layers, per = len(pairs), d // PIECES
    shapes = {x: (layers, per) for x in NAMES}
    for x in ("q_weight", "k_weight", "v_weight", "o_weight"):
        shapes[x] = (layers, per, d)
    shapes["up_weight"], shapes["down_weight"], shapes["up_bias"] = (layers, per, ff), (layers, ff // PIECES, d), (layers, ff // PIECES)
    args = [x for pair in pairs for x in pair]
    return pl.pallas_call(
        functools.partial(finish_kernel, layers, ff // d),
        name="finish",
        in_specs=[full(x.shape) for x in (block_out, grad, *args)],
        out_specs=[ANY, ANY] + [full(shapes[x]) for x in NAMES],
        out_shape=[sds(x.shape, x.dtype) for x in (block_out, grad)] + [sds(shapes[x], f32) for x in NAMES],
        scratch_shapes=[pltpu.VMEM((per, 128), f32), pltpu.SemaphoreType.DMA((2,))],
        compiler_params=pltpu.CompilerParams(vmem_limit_bytes=VMEM_BYTES),
    )(block_out, grad, *args)


def on_device(tokens, segment, live, cotangent, *weights):
    w = dict(zip(NAMES, weights))
    layers, per, d = w["q_weight"].shape
    ff = w["up_weight"].shape[2]
    shards = lax.axis_size("fsdp")
    even = shards == PIECES and lax.axis_size("rep") == 2
    squares, wides, vecs = fetch_even(w, layers, shards) if even else fetch_any(w, layers)
    hidden = tokens
    kept = []
    for l in range(layers - 1):
        g, *saved = attn_forward(hidden, squares[l], vecs[l], segment)
        after, *more = ff_forward(g, wides[l], vecs[l], ff)
        kept.append((hidden, g, saved, more))
        hidden = after
    l = layers - 1
    g, *saved = attn_forward(hidden, squares[l], vecs[l], segment)
    if not even:
        whole = lambda x: x.reshape((PIECES,) + x.shape[4:])
        block_out, grad, extra, gw = ff_last(g, wides[l], vecs[l], cotangent, live, ff)
        grad, gs = attn_backward(hidden, grad, squares[l], vecs[l], saved, extra)
        results = [restack(whole(gs), whole(gw), d, ff)]
        for l in reversed(range(layers - 1)):
            hidden, g, saved, more = kept[l]
            grad, extra, gw = ff_backward(g, wides[l], vecs[l], grad, *more)
            grad, gs = attn_backward(hidden, grad, squares[l], vecs[l], saved, extra)
            results.insert(0, restack(whole(gs), whole(gw), d, ff))
    else:
        block_out, grad, extra, gw = ff_last(g, wides[l], vecs[l], cotangent, live, ff, 1)
        grad, gs, rw = attn_backward(hidden, grad, squares[l], vecs[l], saved, extra, 2 + 2 * l, (gw, 2), l == 0)
        pairs = []
        for l in reversed(range(layers - 1)):
            hidden, g, saved, more = kept[l]
            grad, extra, gw, rs = ff_backward(g, wides[l], vecs[l], grad, *more, ident=3 + 2 * l, carry=(gs, 2))
            pairs.insert(0, (rs, rw))
            grad, gs, rw = attn_backward(hidden, grad, squares[l], vecs[l], saved, extra, 2 + 2 * l, (gw, 2), l == 0)
        pairs.insert(0, (gs, rw))
        return tuple(finish(block_out, grad, pairs, d, ff))
    return (block_out, grad) + tuple(jnp.stack([r[x] for r in results]) for x in NAMES)


def solution(mesh):
    tok = P(("fsdp", "rep"), None)
    specs = tuple(P(None, "fsdp", None) if x.endswith("weight") else P(None, "fsdp") for x in NAMES)
    return jax.shard_map(
        on_device,
        mesh=mesh,
        in_specs=(tok, tok, tok, tok) + specs,
        out_specs=(tok, tok) + specs,
        check_vma=False,
    )
```

```python
import functools
import math

import jax
import jax.numpy as jnp
from jax import lax
from jax.experimental import pallas as pl
from jax.experimental.pallas import tpu as pltpu
from jax.sharding import PartitionSpec as P

HEADS = 16
PIECES = 16
EXTRA = 16
EPSILON = 1e-06
BIG = 1e30
bf16 = jnp.bfloat16
f32 = jnp.float32
FORWARD_PARTS = 1
BACKWARD_PARTS = 4
UNROLL = 2
FORWARD_UNROLL = 4
ATTN_PLAN = {2: [(0, 1)], 4: [(1, 1)], 5: [(0, 2)], 6: [(1, 2)], 7: [(0, 3)]}
ATTN_MIDDLE = [(1, 3), (0, 4)]
ATTN_TILES = {0: [(0, 5)], 1: [(1, 4)]}
ATTN_END = [(1, 5)]
FF_TILES = {6: [(0, 1)], 14: [(1, 1), (0, 2)]}
FF_BLOCKS = {1: [(0, 3), (1, 2)], 4: [(0, 4), (1, 3)], 7: [(0, 5), (1, 4)]}
FF_END = [(1, 5)]
VMEM_BYTES = 60 * 1024 * 1024


def mm(a, b):
    return jnp.dot(a, b, preferred_element_type=f32)


def mm_tn(a, b):
    return lax.dot_general(a, b, (((0,), (0,)), ((), ())), preferred_element_type=f32)


def mm_nt(a, b):
    return lax.dot_general(a, b, (((1,), (1,)), ((), ())), preferred_element_type=f32)


def normalised(x):
    mean = jnp.mean(x, axis=-1, keepdims=True)
    centred = x - mean
    var = jnp.mean(centred * centred, axis=-1, keepdims=True)
    r = lax.rsqrt(var + EPSILON)
    return centred * r, r


def norm_back(d, xh, r, gain):
    e = d * gain
    m1 = jnp.mean(e, axis=-1, keepdims=True)
    m2 = jnp.mean(e * xh, axis=-1, keepdims=True)
    return r * (e - m1 - xh * m2)


def split3(x):
    hi = x.astype(bf16)
    rest = x - hi.astype(f32)
    mid = rest.astype(bf16)
    low = (rest - mid.astype(f32)).astype(bf16)
    return hi, mid, low


def joined(ref):
    x = ref[...]
    return x.reshape(x.shape[0] * x.shape[1], x.shape[2])


def weight(ref, index, rows):
    x = ref[:, index * rows : (index + 1) * rows, :]
    return x.reshape(x.shape[0] * rows, x.shape[2])


def window(w_any, w_ref, sem, base):
    return pltpu.make_async_copy(w_any.at[:, base : base + w_ref.shape[1], :], w_ref, sem)


def down(ref, j, rows, blocks):
    quarter = PIECES // blocks
    x = ref[quarter * j : quarter * (j + 1), rows * blocks : 2 * rows * blocks, :]
    return x.reshape(quarter * rows * blocks, x.shape[2])


def gelu_parts(u):
    c0 = math.sqrt(2.0 / math.pi)
    c1 = c0 * 0.044715
    u2 = u * u
    t = jnp.tanh(u * (c0 + c1 * u2))
    half = 0.5 * (1.0 + t)
    z = u * half
    slope = half + u * (half * (1.0 - t)) * (c0 + (3.0 * c1) * u2)
    return z, slope


def mask_rows(seg_ref, length, slots):
    width = length // slots
    qs, ks = [], []
    for s in range(slots):
        row = lax.broadcasted_iota(jnp.int32, (EXTRA, width), 0)
        seg = seg_ref[0, s]
        same = row == seg
        first = row < slots
        qs.append(jnp.where(same | ~first, 0.0, 1.0))
        ks.append(jnp.where(same, -BIG, jnp.where((row >= 4) & (row < 7), 1.0, 0.0)))
    return jnp.concatenate(qs, axis=1), jnp.concatenate(ks, axis=1)


class Links:
    def __init__(self):
        me = lax.axis_index("fsdp")
        x = lax.axis_index("rep")
        c = lax.rem(me, 2)
        y = lax.rem(lax.div(me, 2), 2)
        low = lax.rem(lax.div(me, 4), 2)
        high = lax.div(me, 8)
        self.at = {"c": c, "y": y, "l": low, "h": high, "x": x}
        self.peer = {
            "c": {"fsdp": me + 1 - 2 * c, "rep": x},
            "y": {"fsdp": me + 2 - 4 * y, "rep": x},
            "l": {"fsdp": me + 4 - 8 * low, "rep": x},
            "h": {"fsdp": me + 8 - 16 * high, "rep": x},
            "x": {"fsdp": me, "rep": 1 - x},
        }

    def meet(self, names="cylhx"):
        barrier = pltpu.get_barrier_semaphore()
        for name in names:
            pl.semaphore_signal(barrier, inc=1, device_id=self.peer[name], device_id_type=pl.DeviceIdType.MESH)
        pl.semaphore_wait(barrier, len(names))

    def remote(self, src, dst, sems, who):
        return pltpu.make_async_remote_copy(
            src_ref=src,
            dst_ref=dst,
            send_sem=sems[0],
            recv_sem=sems[1],
            device_id=self.peer[who],
            device_id_type=pl.DeviceIdType.MESH,
        )


class Reduction:
    ORDERS = ("yxlh", "xylh", "lhyx")
    STEPS = 6

    @classmethod
    def paths(cls, rows, subs):
        found, start = [], 0
        for sub in range(subs):
            units = rows // 32 * (sub + 1) // subs - rows // 32 * sub // subs
            third = (units + 2) // 4
            first = (units - third + 1) // 2
            for order, count in zip(cls.ORDERS, (first, units - third - first, third)):
                found.append((order, start, 32 * count))
                start += 32 * count
        return found

    @classmethod
    def scratch(cls, rows, subs, width):
        shapes = []
        for order, _, count in cls.paths(rows, subs):
            free = 3
            for axis in order:
                if axis == "x":
                    count //= 2
                else:
                    free -= 1
                shapes.append(pltpu.VMEM((2,) * free + (count, width), bf16))
        return shapes + [pltpu.SemaphoreType.DMA((15 * subs,)), pltpu.SemaphoreType.DMA((15 * subs,))]

    @staticmethod
    def scratch_count(subs):
        return 12 * subs + 2

    def __init__(self, links, subs, own, core, fin_ref, refs):
        self.links, self.subs, self.own, self.core, self.fin = links, subs, own, core, fin_ref
        self.at = links.at
        self.bufs = [refs[4 * k : 4 + 4 * k] for k in range(3 * subs)]
        self.send_sem, self.recv_sem = refs[-2], refs[-1]
        self.parts = self.paths(own.shape[-2], subs)

    def places(self, path, step):
        order, start, count = self.parts[path]
        fixed = {}
        rows = pl.ds(start, count)
        send = None
        for axis in order[: step + 1]:
            send = (dict(fixed), rows)
            if axis == "x":
                half = count // 2
                send = (dict(fixed), pl.ds(pl.multiple_of(start + (1 - self.at["x"]) * half, 16), half))
                rows = pl.ds(pl.multiple_of(start + self.at["x"] * half, 16), half)
            else:
                send[0][axis] = 1 - self.at[axis]
                fixed[axis] = self.at[axis]
        return send, (fixed, rows)

    def index(self, place, free=()):
        fixed, rows = place
        found, free = [], list(free)
        for axis in "hly":
            found.append(fixed[axis] if axis in fixed else (free.pop(0) if free else slice(None)))
        if self.core is not None:
            found.append(self.core)
        return (*found, rows, slice(None))

    def exchange(self, path, step):
        sems = (self.send_sem.at[5 * path + step], self.recv_sem.at[5 * path + step])
        if step == 4:
            keep = self.places(path, 3)[1]
            return self.links.remote(self.own.at[self.index(keep)], self.fin.at[keep[1], :], sems, "x")
        send, _ = self.places(path, step)
        axis = self.parts[path][0][step]
        return self.links.remote(self.own.at[self.index(send)], self.bufs[path][step], sems, axis)

    def begin(self, path):
        self.exchange(path, 0).start()

    def add(self, place, other):
        free = 3 - len(place[0])

        def one(i, carry):
            bits = [lax.rem(lax.div(i, 2 ** (free - 1 - b)), 2) for b in range(free)]
            where = self.index(place, bits)
            self.own[where] = self.own[where] + other(bits)
            return carry

        if free:
            lax.fori_loop(0, 2**free, one, 0)
        else:
            one(0, 0)

    def advance(self, path, step):
        k = step - 1
        self.exchange(path, k).wait()
        if k == 4:
            return
        place = self.places(path, k)[1]
        buf = self.bufs[path][k]
        self.add(place, lambda bits: buf[(*bits, slice(None), slice(None))])
        self.exchange(path, k + 1).start()
        if k == 3:
            self.fin[place[1], :] = self.own[self.index(place)]

    def run(self, moves):
        for sub, step in moves:
            for path in range(3 * sub, 3 * sub + 3):
                self.advance(path, step)


class Halving:
    def __init__(self, links, grad, refs, half_any):
        self.links, self.grad, self.half = links, grad, half_any
        self.got, self.send_sem, self.recv_sem, self.out_sem = refs
        self.core = links.at["c"]

    @staticmethod
    def scratch(rows, width, regions):
        dma = pltpu.SemaphoreType.DMA
        return [pltpu.VMEM((2, 2, 2, rows, width), bf16), dma((regions,)), dma((regions,)), dma]

    def copy(self, k, where):
        h, l, y, rows = where
        src = self.grad.at[h, l, y, 1 - self.core, rows, :]
        sems = (self.send_sem.at[k], self.recv_sem.at[k])
        return self.links.remote(src, self.got.at[h, l, y, rows, :], sems, "c")

    def send(self, k, where):
        self.copy(k, where).start()

    def settle(self, k, where):
        self.copy(k, where).wait()
        h, l, y, rows = where
        whole = [isinstance(i, slice) for i in (h, l, y)]
        free = sum(whole)

        def one(i, carry):
            bits = [lax.rem(lax.div(i, 2 ** (free - 1 - b)), 2) for b in range(free)]
            at = [bits.pop(0) if w else i for w, i in zip(whole, (h, l, y))]
            mine = (*at, self.core, rows, slice(None))
            self.grad[mine] = self.grad[mine] + self.got[(*at, rows, slice(None))]
            return carry

        lax.fori_loop(0, 2**free, one, 0)
        if self.half is not None:
            pltpu.make_async_copy(
                self.grad.at[h, l, y, self.core, rows, :], self.half.at[h, l, y, rows, :], self.out_sem
            ).start()

    def drain(self):
        if self.half is not None:
            every = slice(None)
            pltpu.make_async_copy(
                self.grad.at[every, every, every, self.core, every, every], self.half, self.out_sem
            ).wait()


def gather_kernel(x_ref, out_ref, send_sem, recv_sem):
    red = Links()
    at = red.at
    rows = x_ref.shape[0]
    mine = (at["h"], at["l"], at["y"], at["c"])
    out_ref[(*mine, slice(None), slice(None))] = x_ref[...]
    red.meet()

    def copy(path, step):
        order, start, count = path
        order = order[::-1] + "c"
        free = order[:step]
        half = count // 2
        if "x" in free:
            span = pl.ds(start, count)
        else:
            span = pl.ds(pl.multiple_of(start + at["x"] * half, 16), half)
        where = tuple(slice(None) if a in free else at[a] for a in "hlyc") + (span, slice(None))
        sem = 5 * paths.index(path) + step
        return pltpu.make_async_remote_copy(
            src_ref=out_ref.at[where],
            dst_ref=out_ref.at[where],
            send_sem=send_sem.at[sem],
            recv_sem=recv_sem.at[sem],
            device_id=red.peer[order[step]],
            device_id_type=pl.DeviceIdType.MESH,
        )

    paths = [("xylh", start, count) for _, start, count in Reduction.paths(rows, 1)]
    for path in paths:
        copy(path, 0).start()
    for step in range(5):
        for path in paths:
            copy(path, step).wait()
            if step < 4:
                copy(path, step + 1).start()


def gathered(x, ident):
    rows, width = x.shape
    out = pl.pallas_call(
        gather_kernel,
        name="gather",
        in_specs=[full(x.shape)],
        out_specs=full((2, 2, 2, 2, rows, width)),
        out_shape=sds((2, 2, 2, 2, rows, width), bf16),
        scratch_shapes=[pltpu.SemaphoreType.DMA((15,)), pltpu.SemaphoreType.DMA((15,))],
        compiler_params=pltpu.CompilerParams(
            vmem_limit_bytes=24 * 1024 * 1024, collective_id=ident, has_side_effects=True
        ),
        cost_estimate=pl.CostEstimate(flops=0, bytes_accessed=100 << 20, transcendentals=0),
    )(x)
    return out.reshape(PIECES, rows, width)


def attn_forward_kernel(
    tools, h_ref, wa_ref, wb_ref, vec_ref, seg_ref,
    g_ref, at_ref, qe_ref, ke_ref, ve_ref, ot_ref, ol_ref,
):
    length, width = h_ref.shape
    hd = width // HEADS
    rows = width // PIECES
    scale = math.log2(math.e) / math.sqrt(hd)
    tools.wait(0)
    x = h_ref[...].astype(f32)
    xh, _ = normalised(x)
    a = (xh * vec_ref[0:1, :] + vec_ref[1:2, :]).astype(bf16)
    at_ref[...] = a.T
    tools.flush(1, ...)
    tools.wait(1, 2)
    q = (mm(a, weight(wa_ref, 0, rows)) + vec_ref[2:3, :]).astype(bf16)
    qe_ref[:, 0:hd, :] = q.T.reshape(HEADS, hd, length)
    k = mm(a, weight(wa_ref, 1, rows)).astype(bf16)
    ke_ref[:, 0:hd, :] = k.T.reshape(HEADS, hd, length)
    v = (mm(a, weight(wb_ref, 0, rows)) + vec_ref[3:4, :]).astype(bf16)
    ve_ref[:, 0:hd, :] = v.T.reshape(HEADS, hd, length)
    mask_q, mask_k = mask_rows(seg_ref, length, seg_ref.shape[1])
    qe_ref[:, hd:, :] = jnp.broadcast_to(mask_q.astype(bf16)[None], (HEADS, EXTRA, length))
    ke_ref[:, hd:, :] = jnp.broadcast_to(mask_k.astype(bf16)[None], (HEADS, EXTRA, length))
    ve_ref[:, hd:, :] = jnp.ones((HEADS, EXTRA, length), bf16)
    tools.flush(3, ...)
    tools.flush(4, ...)
    row = lax.broadcasted_iota(jnp.int32, (EXTRA, length // FORWARD_PARTS), 0)

    part = length // FORWARD_PARTS

    def head(i):
        for t in range(FORWARD_PARTS):
            cols = slice(t * part, (t + 1) * part)
            st = mm_tn(ke_ref[i], qe_ref[i, :, cols])
            peak = jnp.max(st, axis=0, keepdims=True)
            e = jnp.exp2((st - peak) * scale).astype(bf16)
            mix = mm(ve_ref[i], e)
            total = mix[hd : hd + 1, :]
            o = mix[0:hd, :] * (1.0 / total)
            high = o.astype(bf16)
            ot_ref[i, :, cols] = high
            ol_ref[i, :, cols] = (o - high.astype(f32)).astype(bf16)
            lse = -(peak + jnp.log2(total) * (1.0 / scale))
            hi, mid, low = split3(lse)
            ext = jnp.where(row == 6, low.astype(f32), mask_q[:, cols])
            ext = jnp.where(row == 4, hi.astype(f32), jnp.where(row == 5, mid.astype(f32), ext))
            qe_ref[i, hd:, cols] = ext.astype(bf16)
        for k in (2, 5, 6):
            tools.flush(k, i)

    def some_heads(j, carry):
        for k in range(FORWARD_UNROLL):
            head(FORWARD_UNROLL * j + k)
        return carry

    lax.fori_loop(0, HEADS // FORWARD_UNROLL, some_heads, 0)
    g_ref[...] = x + (mm_tn(joined(ot_ref), weight(wb_ref, 1, rows)) + vec_ref[4:5, :])
    tools.flush(0, ...)


def full(shape):
    return pl.BlockSpec(shape, lambda: (0,) * len(shape))


ANY = pl.BlockSpec(memory_space=pl.ANY)


class Late:
    def __init__(self, turn, base=0, rows=None):
        self.turn, self.base, self.rows = turn, base, rows


class Tools:
    red = pair = tail = None

    def wait(self, *numbers):
        for i in numbers:
            self.fetch[i].wait()

    def flush(self, k, index):
        pltpu.make_async_copy(self.made[k].at[index], self.out[k].at[index], self.out_sem.at[k]).start()

    def finish(self):
        for k in self.made:
            pltpu.make_async_copy(self.made[k], self.out[k], self.out_sem.at[k]).wait()
        if self.pair is not None:
            self.pair.drain()


def call(kernel, name, args, specs, outs, flops, nbytes, scratch, grads=None, ident=None, carry=None, tail=False):
    args, specs = list(args), list(specs)
    n_args = len(args)
    late = sorted((i for i in range(n_args) if isinstance(specs[i], Late)), key=lambda i: specs[i].turn)
    shapes = {}
    for i in late:
        a = args[i]
        rows = specs[i].rows
        shapes[i] = (a.shape[0], rows) + a.shape[2:] if rows else a.shape
    use = [pltpu.VMEM(shapes[i], args[i].dtype) for i in late] + [pltpu.SemaphoreType.DMA((max(1, len(late)),))]
    use += [pltpu.VMEM(o.shape, o.dtype) for o in outs] + [pltpu.SemaphoreType.DMA((max(1, len(outs)),))]
    results = list(outs)
    out_specs = [ANY] * len(outs)
    if grads is not None:
        rows, width, regions = grads
        six_shape = (2, 2, 2, 2, rows, width)
        use.append(pltpu.VMEM(six_shape, bf16))
        if ident is None:
            use.append(pltpu.SemaphoreType.DMA)
            results.append(sds(six_shape, bf16))
            out_specs.append(ANY)
        else:
            use += Halving.scratch(rows, width, regions)
            if tail:
                use += Reduction.scratch(rows, 1, width)
                results.append(sds((rows, width), bf16))
                out_specs.append(full((rows, width)))
            else:
                results.append(sds((2, 2, 2, rows, width), bf16))
                out_specs.append(ANY)
    if carry is not None:
        held, subs = carry
        crows, cwidth = held.shape[3:]
        args.append(held)
        specs.append(None)
        use += [pltpu.VMEM(held.shape, bf16), pltpu.SemaphoreType.DMA] + Reduction.scratch(crows, subs, cwidth)
        results.append(sds((crows, cwidth), bf16))
        out_specs.append(full((crows, cwidth)))
    n_use = len(use)
    base_specs = [ANY if s is None or isinstance(s, Late) else s for s in specs]

    def body(*refs):
        refs = list(refs)
        ins, refs = refs[: len(args)], refs[len(args) :]
        res, refs = refs[: len(results)], refs[len(results) :]
        used, own_scratch = refs[:n_use], refs[n_use:]
        take = lambda n: [used.pop(0) for _ in range(n)]
        t = Tools()
        buffers, (in_sem,) = take(len(late)), take(1)
        made, (t.out_sem,) = take(len(outs)), take(1)
        t.fetch = {}
        for k, i in enumerate(late):
            src = ins[i]
            if specs[i].rows:
                src = src.at[:, specs[i].base : specs[i].base + specs[i].rows]
            t.fetch[i] = pltpu.make_async_copy(src, buffers[k], in_sem.at[k])
            ins[i] = buffers[k]
        t.made, t.out = dict(enumerate(made)), dict(enumerate(res))
        links = Links() if ident is not None else None
        grad = ()
        after = len(outs)
        if grads is not None:
            (grad_ref,) = take(1)
            grad = (grad_ref,)
            if ident is None:
                t.made[after], t.out[after] = grad_ref, res[after]
                (t.grad_sem,) = take(1)
            else:
                t.pair = Halving(links, grad_ref, take(4), None if tail else res[after])
                if tail:
                    t.tail = Reduction(links, 1, grad_ref, links.at["c"], res[after], take(Reduction.scratch_count(1)))
            after += 1
        if carry is not None:
            own, own_sem = take(2)
            t.red = Reduction(links, subs, own, None, res[after], take(Reduction.scratch_count(subs)))
            load = pltpu.make_async_copy(ins[n_args], own, own_sem)
            load.start()
        for i in late:
            t.fetch[i].start()
        if ident is not None:
            links.meet("cylhx" if carry is not None or tail else "c")
        if carry is not None:
            load.wait()
            for path in range(3 * subs):
                t.red.begin(path)
        kernel(t, *ins[:n_args], *made, *grad, *own_scratch)
        if grads is not None and ident is None:
            k = len(outs)
            pltpu.make_async_copy(t.made[k], t.out[k], t.grad_sem).start()
            pltpu.make_async_copy(t.made[k], t.out[k], t.grad_sem).wait()
            del t.made[k]
        t.finish()

    return pl.pallas_call(
        body,
        name=name,
        in_specs=base_specs,
        out_specs=out_specs,
        out_shape=results,
        scratch_shapes=use + list(scratch),
        compiler_params=pltpu.CompilerParams(
            vmem_limit_bytes=VMEM_BYTES, collective_id=ident, has_side_effects=ident is not None
        ),
        cost_estimate=pl.CostEstimate(flops=flops, bytes_accessed=nbytes, transcendentals=0),
    )(*args)


def advance_at(red, index, plan):
    if red is None:
        return
    for at, moves in plan.items():

        @pl.when(index == at)
        def _(moves=moves):
            red.run(moves)


def sds(shape, dtype):
    return jax.ShapeDtypeStruct(shape, dtype)


SMEM = pltpu.SMEM


def attn_forward(h, square, vec, seg):
    (first, base_a), (second, base_b) = square
    n, d = h.shape
    hd = d // HEADS
    rows = d // PIECES
    ext = hd + EXTRA
    outs = (
        sds((n, d), f32),
        sds((d, n), bf16),
        sds((HEADS, ext, n), bf16),
        sds((HEADS, ext, n), bf16),
        sds((HEADS, ext, n), bf16),
        sds((HEADS, hd, n), bf16),
        sds((HEADS, hd, n), bf16),
    )
    specs = [Late(0), Late(1, base_a, 2 * rows), Late(2, base_b, 2 * rows), full(vec.shape), pl.BlockSpec(memory_space=SMEM)]
    flops = 8 * n * d * d + 2 * HEADS * 2 * n * n * 256
    return call(attn_forward_kernel, "attn_forward", (h, first, second, vec, seg), specs, outs, flops, 30 << 20, ())


def ff_forward_kernel(base, g_ref, w_any, vec_ref, h_ref, b_ref, z_ref, s_ref, w_ref, w_sem):
    width = g_ref.shape[1]
    rows = width // PIECES
    blocks = z_ref.shape[1] // width

    @pl.when(pl.program_id(0) == 0)
    def _():
        fetch = window(w_any, w_ref, w_sem, base)
        fetch.start()
        fetch.wait()

    gg = g_ref[...]
    xh, _ = normalised(gg)
    b = (xh * vec_ref[5:6, :] + vec_ref[6:7, :]).astype(bf16)
    b_ref[...] = b
    acc = gg + vec_ref[7:8, :]
    for j in range(blocks):
        w = weight(w_ref, j, rows)
        u = mm(b, w) + vec_ref[8 + j : 9 + j, :]
        z, slope = gelu_parts(u)
        zb = z.astype(bf16)
        z_ref[:, j * width : (j + 1) * width] = zb
        s_ref[:, j * width : (j + 1) * width] = slope.astype(bf16)
        wd = down(w_ref, j, rows, blocks)
        acc = acc + mm(zb, wd)
    h_ref[...] = acc


def ff_forward(g, wide, vec, ff):
    wide, base = wide
    n, d = g.shape
    tile = 256
    outs = (sds((n, d), f32), sds((n, d), bf16), sds((n, ff), bf16), sds((n, ff), bf16))
    row = lambda w: pl.BlockSpec((tile, w), lambda i: (i, 0))
    return pl.pallas_call(
        functools.partial(ff_forward_kernel, base),
        name="ff_forward",
        grid=(n // tile,),
        in_specs=[
            row(d),
            pl.BlockSpec(memory_space=pl.ANY),
            pl.BlockSpec(vec.shape, lambda i: (0, 0)),
        ],
        out_specs=[row(d), row(d), row(ff), row(ff)],
        out_shape=outs,
        scratch_shapes=[pltpu.VMEM((PIECES, 2 * ff // PIECES, d), bf16), pltpu.SemaphoreType.DMA],
        compiler_params=pltpu.CompilerParams(vmem_limit_bytes=VMEM_BYTES),
        cost_estimate=pl.CostEstimate(flops=4 * n * d * ff, bytes_accessed=30 << 20, transcendentals=0),
    )(g, wide, vec)


def put_vectors(grad_ref, base, cols_ref, per):
    pad = grad_ref.shape[4] - base
    lanes = grad_ref.shape[5] // 128
    count = per // lanes
    for m in range(lanes):
        part = cols_ref[pl.ds(m, PIECES * count, stride=lanes), :]
        part = part.reshape(PIECES, count, 128)
        part = jnp.concatenate([part, jnp.zeros((PIECES, pad - count, 128), f32)], axis=1)
        part = part.reshape(2, 2, 2, 2, pad, 128)
        grad_ref[:, :, :, :, base : base + pad, m * 128 : (m + 1) * 128] = part.astype(bf16)


EVERY = slice(None)
ATTN_VECTORS = 5


def ff_tail(tools, z_ref, du_ref, b_ref, cm_ref, grad_ref, cols_ref, number, vecs, width, blocks):
    rows = width // PIECES
    quarter = PIECES // blocks
    n = b_ref.shape[0]
    pair = tools.pair
    lower = pl.ds(rows * blocks, rows * blocks)

    def regions(j):
        up = (EVERY, EVERY, EVERY, pl.ds(pl.multiple_of(rows * j, 16), rows))
        return (j, (lax.div(j, 2), lax.rem(j, 2), EVERY, lower)), (blocks + j, up)

    def settle(j):
        if pair is not None:
            for k, where in regions(j):
                pair.settle(k, where)

    def block(j, carry):
        advance_at(tools.red, j, {at // 2: m for at, m in FF_BLOCKS.items() if at % 2 == 0})
        cols = pl.ds(pl.multiple_of(j * width, 128), width)
        (kd, where_d), (ku, where_u) = regions(j)
        dwd = mm_tn(z_ref[:, cols], cm_ref[...]).reshape(2, 2, rows * blocks, width)
        grad_ref[lax.div(j, 2), lax.rem(j, 2), :, :, lower, :] = dwd.astype(bf16)
        if pair is not None:
            pair.send(kd, where_d)
        advance_at(tools.red, j, {at // 2: m for at, m in FF_BLOCKS.items() if at % 2 == 1})
        dwu = mm_tn(b_ref[...], du_ref[:, cols])
        grad_ref[:, :, :, :, where_u[3], :] = dwu.reshape(2, 2, 2, 2, rows, width).astype(bf16)
        if pair is not None:
            pair.send(ku, where_u)

            @pl.when(j > 0)
            def _():
                settle(j - 1)

        return carry

    lax.fori_loop(0, blocks, block, 0)
    ones = jnp.ones((n, 128), bf16)
    first = ATTN_VECTORS
    blank = jnp.zeros((first, width), f32)
    vt = jnp.concatenate([blank, *vecs, jnp.zeros((128 - first - len(vecs), width), f32)], axis=0).T
    vt = vt.reshape(PIECES, rows, 128)
    lane = lax.broadcasted_iota(jnp.int32, (quarter, rows, 128), 2)
    for j in range(blocks):
        part = mm_tn(du_ref[:, j * width : (j + 1) * width], ones)
        part = part.reshape(quarter, blocks, rows, 128)
        piece = vt[quarter * j : quarter * (j + 1)]
        for c in range(blocks):
            piece = jnp.where(lane == first + len(vecs) + c, part[:, c], piece)
        cols_ref[quarter * rows * j : quarter * rows * (j + 1), :] = piece.reshape(quarter * rows, 128)
    tools.flush(number, ...)
    if pair is not None:
        settle(blocks - 1)


def ff_last_kernel(
    tools, g_ref, w_ref, vec_ref, cot_ref, live_ref, out_ref, dg_ref, cols_ref, grad_ref, z_ref, du_ref, b_ref, cm_ref,
):
    n, width = g_ref.shape
    rows = width // PIECES
    blocks = z_ref.shape[1] // width
    tile = n // 4
    gain = vec_ref[5:6, :]
    tools.wait(0, 3, 1)

    def step(t, sums):
        sum_gain, sum_bias, sum_down = sums
        span = pl.ds(pl.multiple_of(t * tile, 16), tile)
        gg = g_ref[span, :]
        xh, r = normalised(gg)
        b = (xh * gain + vec_ref[6:7, :]).astype(bf16)
        b_ref[span, :] = b
        grad = cot_ref[span, :].astype(f32) * live_ref[0, t].astype(f32)
        cm = grad.astype(bf16)
        cm_ref[span, :] = cm
        acc = gg + vec_ref[7:8, :]
        db = jnp.zeros((tile, width), f32)
        for j in range(blocks):
            cols = slice(j * width, (j + 1) * width)
            w = weight(w_ref, j, rows)
            wd = down(w_ref, j, rows, blocks)
            u = mm(b, w) + vec_ref[8 + j : 9 + j, :]
            dz = mm_nt(cm, wd)
            z, slope = gelu_parts(u)
            zb = z.astype(bf16)
            z_ref[span, cols] = zb
            acc = acc + mm(zb, wd)
            du = (slope * dz).astype(bf16)
            du_ref[span, cols] = du
            db = db + mm_nt(du, w)
        out_ref[span, :] = acc.astype(bf16)
        dg_ref[span, :] = grad + norm_back(db, xh, r, gain)
        tools.flush(0, (span, EVERY))
        tools.flush(1, (span, EVERY))
        sum_gain = sum_gain + jnp.sum(db * xh, axis=0, keepdims=True)
        sum_bias = sum_bias + jnp.sum(db, axis=0, keepdims=True)
        sum_down = sum_down + jnp.sum(cm.astype(f32), axis=0, keepdims=True)
        return sum_gain, sum_bias, sum_down

    zero = jnp.zeros((1, width), f32)
    sums = lax.fori_loop(0, 4, step, (zero, zero, zero))
    ff_tail(tools, z_ref, du_ref, b_ref, cm_ref, grad_ref, cols_ref, 2, sums, width, blocks)


def ff_last(g, wide, vec, cot, live, ff, ident=None):
    wide, base = wide
    n, d = g.shape
    rows = d // PIECES
    blocks = ff // d
    outs = (sds((n, d), bf16), sds((n, d), f32), sds((d, 128), f32))
    specs = [Late(0), Late(1, base, 2 * rows * blocks), full(vec.shape), Late(2), pl.BlockSpec(memory_space=SMEM)]
    scratch = [
        pltpu.VMEM((n, ff), bf16), pltpu.VMEM((n, ff), bf16), pltpu.VMEM((n, d), bf16),
        pltpu.VMEM((n, d), bf16),
    ]
    grads = (2 * rows * blocks, d, 2 * blocks)
    return call(
        ff_last_kernel, "ff_last", (g, wide, vec, cot, live), specs, outs, 12 * n * d * ff, 30 << 20, scratch,
        grads, ident,
    )


def ff_backward_kernel(
    tools, g_ref, w_ref, vec_ref, c_ref, b_ref, z_ref, s_ref, dg_ref, cols_ref, grad_ref, cm_ref,
):
    n, width = g_ref.shape
    rows = width // PIECES
    blocks = z_ref.shape[1] // width
    tile = n // 4
    gain = vec_ref[5:6, :]
    tools.wait(3, 1, 6, 0)

    def step(t, sums):
        sum_gain, sum_bias, sum_down = sums
        span = pl.ds(pl.multiple_of(t * tile, 16), tile)
        xh, r = normalised(g_ref[span, :])
        grad = c_ref[span, :]
        cm = grad.astype(bf16)
        cm_ref[span, :] = cm
        db = jnp.zeros((tile, width), f32)
        for j in range(blocks):
            cols = slice(j * width, (j + 1) * width)
            advance_at(tools.red, t, {at // blocks: m for at, m in FF_TILES.items() if at % blocks == j})
            w = weight(w_ref, j, rows)
            wd = down(w_ref, j, rows, blocks)
            du = (s_ref[span, cols].astype(f32) * mm_nt(cm, wd)).astype(bf16)
            s_ref[span, cols] = du
            db = db + mm_nt(du, w)
        dg_ref[span, :] = grad + norm_back(db, xh, r, gain)
        tools.flush(0, (span, EVERY))
        sum_gain = sum_gain + jnp.sum(db * xh, axis=0, keepdims=True)
        sum_bias = sum_bias + jnp.sum(db, axis=0, keepdims=True)
        sum_down = sum_down + jnp.sum(cm.astype(f32), axis=0, keepdims=True)
        return sum_gain, sum_bias, sum_down

    zero = jnp.zeros((1, width), f32)
    sums = lax.fori_loop(0, 4, step, (zero, zero, zero))
    tools.wait(5, 4)
    ff_tail(tools, z_ref, s_ref, b_ref, cm_ref, grad_ref, cols_ref, 1, sums, width, blocks)
    if tools.red is not None:
        tools.red.run(FF_END)


def ff_backward(g, wide, vec, c, b, z, s, ident=None, carry=None):
    wide, base = wide
    n, d = g.shape
    ff = z.shape[1]
    rows = d // PIECES
    blocks = ff // d
    outs = (sds((n, d), f32), sds((d, 128), f32))
    specs = [Late(3), Late(1, base, 2 * rows * blocks), full(vec.shape), Late(0), Late(5), Late(4), Late(2)]
    scratch = [pltpu.VMEM((n, d), bf16)]
    grads = (2 * rows * blocks, d, 2 * blocks)
    return call(
        ff_backward_kernel, "ff_backward", (g, wide, vec, c, b, z, s), specs, outs, 8 * n * d * ff, 40 << 20, scratch,
        grads, ident, carry,
    )


def attn_backward_kernel(
    tools, h_ref, dg_ref, wa_ref, wb_ref, vec_ref, at_ref, qe_ref, ke_ref, ve_ref, ot_ref, ol_ref, extra_ref,
    c_ref, grad_ref, doe_ref, dq_ref, dk_ref, dv_ref, cols_ref,
):
    n, width = h_ref.shape
    hd = width // HEADS
    rows = width // PIECES
    scale = math.log2(math.e) / math.sqrt(hd)
    factor = 1.0 / math.sqrt(hd)
    red, pair, tail = tools.red, tools.pair, tools.tail

    def region(j):
        return (EVERY, EVERY, EVERY, pl.ds(j * rows, rows if j < 4 else 2 * EXTRA))

    def put(j, value):
        grad_ref[:, :, :, :, j * rows : (j + 1) * rows, :] = value.reshape(2, 2, 2, 2, rows, width).astype(bf16)
        if pair is not None:
            pair.send(j, region(j))

    tools.wait(1, 9)
    co = dg_ref[...].astype(bf16)
    put(3, mm(joined(ot_ref), co))
    tools.wait(3)
    dot = mm_nt(weight(wb_ref, 1, rows), co).astype(bf16)
    doe_ref[:, 0:hd, :] = dot.reshape(HEADS, hd, n)
    row = lax.broadcasted_iota(jnp.int32, (EXTRA, n), 0)
    tools.wait(6, 7, 8, 10)
    part = n // BACKWARD_PARTS

    def head(i):
        doh = doe_ref[i, 0:hd, :]
        delta = jnp.sum(doh.astype(f32) * (ot_ref[i].astype(f32) + ol_ref[i].astype(f32)), axis=0, keepdims=True)
        hi, mid, low = split3(-delta)
        ext = jnp.where(row == 0, hi.astype(f32), jnp.where(row == 1, mid.astype(f32), jnp.where(row == 2, low.astype(f32), 0.0)))
        doe_ref[i, hd:, :] = ext.astype(bf16)
        dk = dv = None
        for t in range(BACKWARD_PARTS):
            cols = slice(t * part, (t + 1) * part)
            s = mm_tn(qe_ref[i, :, cols], ke_ref[i])
            p = jnp.exp2(s * scale)
            dp = mm_tn(doe_ref[i, :, cols], ve_ref[i])
            ds = (p * dp).astype(bf16)
            dv_t = mm(doe_ref[i, 0:hd, cols], p.astype(bf16))
            dk_t = mm(qe_ref[i, 0:hd, cols], ds)
            dv = dv_t if t == 0 else dv + dv_t
            dk = dk_t if t == 0 else dk + dk_t
            dq_ref[i, :, cols] = (mm_nt(ke_ref[i, 0:hd, :], ds) * factor).astype(bf16)
        dv_ref[i] = dv.astype(bf16)
        dk_ref[i] = (dk * factor).astype(bf16)

    def some_heads(j, carry):
        advance_at(red, j, ATTN_PLAN)
        for k in range(UNROLL):
            head(UNROLL * j + k)
        return carry

    lax.fori_loop(0, HEADS // UNROLL, some_heads, 0)
    tools.wait(5, 0, 2, 11)
    if red is not None:
        red.run(ATTN_MIDDLE)
    if pair is not None:
        pair.settle(3, region(3))
    at = at_ref[...]
    put(0, mm_nt(at, joined(dq_ref)))
    put(1, mm_nt(at, joined(dk_ref)))
    put(2, mm_nt(at, joined(dv_ref)))
    if pair is not None:
        for j in range(3):
            pair.settle(j, region(j))
    if tail is not None:
        tail.begin(0)
        tail.begin(1)
    tile = n // 4

    def norm_tile(t, sums):
        advance_at(red, t, ATTN_TILES)
        sum_gain, sum_bias, sum_out = sums
        span = pl.ds(pl.multiple_of(t * tile, 128), tile)
        dat = mm(weight(wa_ref, 0, rows), dq_ref[:, :, span].reshape(width, tile))
        dat = dat + mm(weight(wa_ref, 1, rows), dk_ref[:, :, span].reshape(width, tile))
        dat = dat + mm(weight(wb_ref, 0, rows), dv_ref[:, :, span].reshape(width, tile))
        da = dat.T
        xh, r = normalised(h_ref[span, :].astype(f32))
        dg = dg_ref[span, :]
        c_ref[span, :] = dg + norm_back(da, xh, r, vec_ref[0:1, :])
        tools.flush(0, (span, EVERY))
        sum_gain = sum_gain + jnp.sum(da * xh, axis=0, keepdims=True)
        sum_bias = sum_bias + jnp.sum(da, axis=0, keepdims=True)
        sum_out = sum_out + jnp.sum(dg.astype(bf16).astype(f32), axis=0, keepdims=True)
        return sum_gain, sum_bias, sum_out

    zero = jnp.zeros((1, width), f32)
    vecs = lax.fori_loop(0, 4, norm_tile, (zero, zero, zero))
    vt = jnp.concatenate([*vecs, jnp.zeros((128 - len(vecs), width), f32)], axis=0).T
    lane = lax.broadcasted_iota(jnp.int32, (width, 128), 1)
    vt = jnp.where(lane == 3, jnp.sum(joined(dq_ref).astype(f32), axis=1, keepdims=True), vt)
    vt = jnp.where(lane == 4, jnp.sum(joined(dv_ref).astype(f32), axis=1, keepdims=True), vt)
    cols_ref[...] = vt + extra_ref[...]
    put_vectors(grad_ref, 4 * rows, cols_ref, rows)
    if pair is not None:
        pair.send(4, region(4))
        pair.settle(4, region(4))
    if tail is not None:
        tail.begin(2)
    if red is not None:
        red.run(ATTN_END)
    if tail is not None:
        for step in range(1, Reduction.STEPS):
            tail.run([(0, step)])


def attn_backward(h, dg, square, vec, kept, extra, ident=None, carry=None, tail=False):
    (first, base_a), (second, base_b) = square
    n, d = h.shape
    hd = d // HEADS
    rows = d // PIECES
    at, qe, ke, ve, ot, ol = kept
    outs = (sds((n, d), f32),)
    specs = [Late(8), Late(0), Late(9, base_a, 2 * rows), Late(2, base_b, 2 * rows), full(vec.shape)]
    specs += [Late(7), Late(3), Late(4), Late(5), Late(1), Late(6), Late(10)]
    scratch = [pltpu.VMEM((HEADS, hd + EXTRA, n), bf16)] + [pltpu.VMEM((HEADS, hd, n), bf16)] * 3
    scratch += [pltpu.VMEM((d, 128), f32)]
    flops = 16 * n * d * d + 5 * HEADS * 2 * n * n * 256
    return call(
        attn_backward_kernel, "attn_backward", (h, dg, first, second, vec, at, qe, ke, ve, ot, ol, extra), specs, outs, flops, 40 << 20,
        scratch, (4 * rows + 2 * EXTRA, d, 5), ident, carry, tail,
    )


NAMES = (
    "ln1_gain", "ln1_bias", "q_weight", "q_bias", "k_weight", "v_weight", "v_bias", "o_weight", "o_bias",
    "ln2_gain", "ln2_bias", "up_weight", "up_bias", "down_weight", "down_bias",
)
COLUMN_VECTORS = ("ln1_gain", "ln1_bias", "o_bias", "q_bias", "v_bias", "ln2_gain", "ln2_bias", "down_bias")
ROW_VECTORS = ("ln1_gain", "ln1_bias", "q_bias", "v_bias", "o_bias", "ln2_gain", "ln2_bias", "down_bias")


def gather(x, axis="fsdp"):
    return lax.all_gather(x, axis, axis=0, tiled=True)


def column_blocks(up, d):
    return [up[:, j * d : (j + 1) * d] for j in range(up.shape[1] // d)]


def pack_kernel(first_rows, rest_rows, *refs):
    names = [n for n in NAMES if n.endswith("weight")]
    weights = dict(zip(names, refs))
    vectors = refs[len(names) : len(names) + len(ROW_VECTORS) + 1]
    first, rest, wide_ref, rows_ref, sems = refs[len(names) + len(ROW_VECTORS) + 1 :]
    per, d = vectors[0].shape[1], first.shape[1]
    moves = []
    for target, pieces in ((rest, rest_rows), (first, first_rows)):
        at = 0
        for name, l, column in pieces:
            src = weights[name].at[l]
            if column is not None:
                src = src.at[:, column * d : (column + 1) * d]
            count = src.shape[0]
            copy = pltpu.make_async_copy(src, target.at[at : at + count, :], sems.at[len(moves)])
            copy.start()
            moves.append(copy)
            at += count
    wide_ref[...] = jnp.zeros_like(wide_ref)
    for l in range(vectors[0].shape[0]):
        for k, ref in enumerate(vectors):
            wide_ref[l : l + 1, k * per : k * per + ref.shape[1]] = ref[l : l + 1, :].astype(f32)
    rows_ref[...] = wide_ref[...].astype(bf16)
    copy = pltpu.make_async_copy(rows_ref, first.at[at : at + 2 * EXTRA, :], sems.at[len(moves)])
    copy.start()
    for move in moves + [copy]:
        move.wait()


def fetch_even(w, layers, shards):
    d = w["q_weight"].shape[2]
    per = w["q_weight"].shape[1]
    ff = w["up_weight"].shape[2]
    blocks = ff // d
    square = lambda l, names: [(n + "_weight", l, None) for n in names]
    wide = lambda l: [("up_weight", l, j) for j in range(blocks)] + [("down_weight", l, None)]
    first, rest = square(0, "qkvo"), wide(0)
    for l in range(1, layers):
        first = first + square(l, "qk")
        rest = rest + square(l, "vo") + wide(l)
    tall = 4 * per + 2 * per * (layers - 1)
    long = 2 * per * blocks * layers + 2 * per * (layers - 1)
    names = [n for n in NAMES if n.endswith("weight")]
    vectors = [w[x] for x in (*ROW_VECTORS, "up_bias")]
    first, rest = pl.pallas_call(
        functools.partial(pack_kernel, first, rest),
        name="pack",
        in_specs=[full(w[n].shape) for n in names] + [full(x.shape) for x in vectors],
        out_specs=[ANY, ANY],
        out_shape=[sds((tall + 2 * EXTRA, d), bf16), sds((long, d), bf16)],
        scratch_shapes=[
            pltpu.VMEM((2 * EXTRA, d), f32), pltpu.VMEM((2 * EXTRA, d), bf16),
            pltpu.SemaphoreType.DMA((len(first) + len(rest) + 1,)),
        ],
    )(*(w[n] for n in names), *vectors)
    rest = gather(rest).reshape(shards, -1, d)
    first = gathered(first, 20)
    flat = first[:, tall : tall + layers, :]
    count = len(ROW_VECTORS)
    vecs = flat[:, :, : count * per].reshape(shards, layers, count, per).transpose(1, 2, 0, 3)
    vecs = vecs.reshape(layers, count, d)
    ups = flat[:, :, count * per : count * per + ff // shards].transpose(1, 0, 2).reshape(layers, ff // d, d)
    vec = jnp.concatenate([vecs, ups], axis=1).astype(f32)
    wides = [(rest, 0)]
    squares = [((first, 0), (first, 2 * per))]
    base = 2 * per * blocks
    for l in range(1, layers):
        squares.append(((first, 2 * per * (l + 1)), (rest, base)))
        wides.append((rest, base + 2 * per))
        base += 2 * per + 2 * per * blocks
    return squares, wides, [vec[l] for l in range(layers)]


def fetch_any(w, layers):
    d = w["q_weight"].shape[2]
    squares, wides, vecs = [], [], []
    for l in range(layers):
        whole = {x: gather(w[x][l]) for x in NAMES}
        cut = lambda x: x.reshape(PIECES, x.shape[0] // PIECES, d)
        four = jnp.concatenate([cut(whole[x]) for x in ("q_weight", "k_weight", "v_weight", "o_weight")], axis=1)
        squares.append(((four, 0), (four, 2 * (d // PIECES))))
        blocks = [cut(x) for x in column_blocks(whole["up_weight"], d)] + [cut(whole["down_weight"])]
        wides.append((jnp.concatenate(blocks, axis=1), 0))
        rows = [whole[x][None] for x in ROW_VECTORS] + [whole["up_bias"].reshape(-1, d)]
        vecs.append(jnp.concatenate(rows, axis=0).astype(f32))
    return squares, wides, vecs


def over_rep(x):
    size = lax.axis_size("rep")
    if size == 1:
        return x.astype(f32)
    other = lax.ppermute(x, "rep", [(i, (i + 1) % size) for i in range(size)])
    return x.astype(f32) + other.astype(f32)


def restack(grads_square, grads_wide, d, ff):
    per = d // PIECES
    blocks = ff // d
    gs, gw = grads_square, grads_wide
    out = {x: gs[:, j * per : (j + 1) * per].reshape(d, d) for j, x in enumerate(("q_weight", "k_weight", "v_weight", "o_weight"))}
    out["up_weight"] = jnp.concatenate([gw[:, j * per : (j + 1) * per].reshape(d, d) for j in range(blocks)], axis=1)
    out["down_weight"] = gw[:, blocks * per : 2 * blocks * per].reshape(ff, d)
    count = per // (d // 128)
    vs = gs[:, 4 * per : 4 * per + count].reshape(PIECES, per, 128)
    for j, x in enumerate(COLUMN_VECTORS):
        out[x] = vs[:, :, j].reshape(d)
    first = len(COLUMN_VECTORS)
    out["up_bias"] = vs[:, :, first : first + blocks].transpose(0, 2, 1).reshape(ff)
    sums = {}
    for x, g in out.items():
        sums[x] = over_rep(lax.psum_scatter(g, "fsdp", scatter_dimension=0, tiled=True))
    return sums


def finish_kernel(layers, blocks, *refs):
    given, made, (cols_ref, sems) = refs[: 2 * layers + 2], refs[2 * layers + 2 : -2], refs[-2:]
    ins, outs = given[2:], dict(zip(NAMES, made[2:]))
    moves = [pltpu.make_async_copy(given[k], made[k], sems.at[k]) for k in range(2)]
    for move in moves:
        move.start()
    per = outs["q_weight"].shape[1]
    width = outs["q_weight"].shape[2]
    lanes = width // 128
    for l in range(layers):
        square, wide = ins[2 * l], ins[2 * l + 1]
        for j, x in enumerate(("q_weight", "k_weight", "v_weight", "o_weight")):
            outs[x][l] = square[j * per : (j + 1) * per, :].astype(f32)
        for j in range(blocks):
            outs["up_weight"][l, :, j * width : (j + 1) * width] = wide[j * per : (j + 1) * per, :].astype(f32)
        outs["down_weight"][l] = wide[blocks * per : 2 * blocks * per, :].astype(f32)
        for m in range(lanes):
            part = square[4 * per : 4 * per + per // lanes, m * 128 : (m + 1) * 128].astype(f32)
            cols_ref[pl.ds(m, per // lanes, stride=lanes), :] = part
        turned = cols_ref[...].T
        for j, x in enumerate(COLUMN_VECTORS):
            outs[x][l : l + 1, :] = turned[j : j + 1, :]
        for c in range(blocks):
            j = len(COLUMN_VECTORS) + c
            outs["up_bias"][l : l + 1, c * per : (c + 1) * per] = turned[j : j + 1, :]
    for move in moves:
        move.wait()


def finish(block_out, grad, pairs, d, ff):
    layers, per = len(pairs), d // PIECES
    shapes = {x: (layers, per) for x in NAMES}
    for x in ("q_weight", "k_weight", "v_weight", "o_weight"):
        shapes[x] = (layers, per, d)
    shapes["up_weight"], shapes["down_weight"], shapes["up_bias"] = (layers, per, ff), (layers, ff // PIECES, d), (layers, ff // PIECES)
    args = [x for pair in pairs for x in pair]
    return pl.pallas_call(
        functools.partial(finish_kernel, layers, ff // d),
        name="finish",
        in_specs=[full(x.shape) for x in (block_out, grad, *args)],
        out_specs=[ANY, ANY] + [full(shapes[x]) for x in NAMES],
        out_shape=[sds(x.shape, x.dtype) for x in (block_out, grad)] + [sds(shapes[x], f32) for x in NAMES],
        scratch_shapes=[pltpu.VMEM((per, 128), f32), pltpu.SemaphoreType.DMA((2,))],
        compiler_params=pltpu.CompilerParams(vmem_limit_bytes=VMEM_BYTES),
    )(block_out, grad, *args)


def on_device(tokens, segment, live, cotangent, *weights):
    w = dict(zip(NAMES, weights))
    layers, per, d = w["q_weight"].shape
    ff = w["up_weight"].shape[2]
    shards = lax.axis_size("fsdp")
    even = shards == PIECES and lax.axis_size("rep") == 2
    squares, wides, vecs = fetch_even(w, layers, shards) if even else fetch_any(w, layers)
    hidden = tokens
    kept = []
    for l in range(layers - 1):
        g, *saved = attn_forward(hidden, squares[l], vecs[l], segment)
        after, *more = ff_forward(g, wides[l], vecs[l], ff)
        kept.append((hidden, g, saved, more))
        hidden = after
    l = layers - 1
    g, *saved = attn_forward(hidden, squares[l], vecs[l], segment)
    if not even:
        whole = lambda x: x.reshape((PIECES,) + x.shape[4:])
        block_out, grad, extra, gw = ff_last(g, wides[l], vecs[l], cotangent, live, ff)
        grad, gs = attn_backward(hidden, grad, squares[l], vecs[l], saved, extra)
        results = [restack(whole(gs), whole(gw), d, ff)]
        for l in reversed(range(layers - 1)):
            hidden, g, saved, more = kept[l]
            grad, extra, gw = ff_backward(g, wides[l], vecs[l], grad, *more)
            grad, gs = attn_backward(hidden, grad, squares[l], vecs[l], saved, extra)
            results.insert(0, restack(whole(gs), whole(gw), d, ff))
    else:
        block_out, grad, extra, gw = ff_last(g, wides[l], vecs[l], cotangent, live, ff, 1)
        grad, gs, rw = attn_backward(hidden, grad, squares[l], vecs[l], saved, extra, 2 + 2 * l, (gw, 2), l == 0)
        pairs = []
        for l in reversed(range(layers - 1)):
            hidden, g, saved, more = kept[l]
            grad, extra, gw, rs = ff_backward(g, wides[l], vecs[l], grad, *more, ident=3 + 2 * l, carry=(gs, 2))
            pairs.insert(0, (rs, rw))
            grad, gs, rw = attn_backward(hidden, grad, squares[l], vecs[l], saved, extra, 2 + 2 * l, (gw, 2), l == 0)
        pairs.insert(0, (gs, rw))
        return tuple(finish(block_out, grad, pairs, d, ff))
    return (block_out, grad) + tuple(jnp.stack([r[x] for r in results]) for x in NAMES)


def solution(mesh):
    tok = P(("fsdp", "rep"), None)
    specs = tuple(P(None, "fsdp", None) if x.endswith("weight") else P(None, "fsdp") for x in NAMES)
    return jax.shard_map(
        on_device,
        mesh=mesh,
        in_specs=(tok, tok, tok, tok) + specs,
        out_specs=(tok, tok) + specs,
        check_vma=False,
    )
```
